256 devices in a mesh: group: 2 (over y_lo), dp: 16 (over y_hi, z), tensor: 8 (over x, core).
Axes of the slice: x: 4, y: 4 (y_hi: 2, y_lo: 2; y = y_hi * 2 + y_lo), z: 8, core: 2. Of those that a mesh axis runs over, the one named last changes fastest.
Arguments:
- tokens: bfloat16 [8192, 2048], P('dp'), may hold values from -6 to 6
- upstream: bfloat16 [8192, 2048], P('dp'), may hold values from -6 to 6
- corpus: bfloat16 [4096, 2048], P('dp'), may hold values from -200 to 200
- lengths: int32 [128], P('dp'), may hold values from 1 to 32, as said below
- owners: int32 [128], P('dp'), may hold values from 0 to 31, as said below
- w_in: bfloat16 [2048, 8192], P(('group', 'dp'), 'tensor'), may hold values from -6 to 6
- w_out: bfloat16 [2048, 8192], P(('group', 'dp'), 'tensor'), may hold values from -6 to 6
Outputs:
- new_in: bfloat16 [2048, 8192], P(('group', 'dp'), 'tensor')
- new_out: bfloat16 [2048, 8192], P(('group', 'dp'), 'tensor')
- index: bfloat16 [512, 2048], P(('group', 'dp'), 'tensor')
The draws below stay inside these ranges and needn't reach their ends.
Inputs may be any that keep to these rules, and one draw needn't show every extreme that they name: `owners`: of the 8 passages of one dp index at most 1 have one owner, and some owner receives exactly 1 passages from every dp index. `lengths`: some passage has length 32.
All inputs are finite; a program needn't handle non-finite values.
Results may differ from the reference program's by a relative error of at most 0.012.
Values may be sent and summed in bfloat16 or wider, within the bound.
A program may use at most 128 MiB of HBM per device.

```python
import math
import jax
import jax.numpy as jnp
from jax import lax

D = 2048
FF = 8192
TOK_DEV = 512
CTOK_DEV = 256
PLEN = 32
TOKENS = 8192
CTOKENS = 4096
PSEQ = 8
PASSAGES = 128
OWNERS = 32
SLOT = 1
CAP = 16
N_DP = 16


def draw_corpus(key, part):
    key_a, key_b = jax.random.split(jax.random.fold_in(key, 11), 2)
    columns = jnp.arange(D, dtype=jnp.float32)
    col_scale = 3.0 ** (columns / D) * jnp.exp(jax.random.uniform(key_a, (D,), jnp.float32, 0.0, math.log(3.0)))
    values = jnp.clip(jax.random.normal(key_b, (CTOKENS, D), jnp.float32), -4.0, 4.0)
    result = values * col_scale[None, :]
    return result.astype(jnp.bfloat16)


def draw_lengths(key, part):
    key_a, key_b = jax.random.split(jax.random.fold_in(key, 23))
    values = jax.random.randint(key_a, (PASSAGES,), 1, PLEN + 1)
    where_full = jax.random.randint(key_b, (), 0, PASSAGES)
    return jnp.where(jnp.arange(PASSAGES) == where_full, PLEN, values).astype(jnp.int32)


def draw_owners(key, part):
    key_a, key_b, key_c = jax.random.split(jax.random.fold_in(key, 37), 3)
    slots_all = OWNERS * SLOT
    slot_ids = jnp.arange(slots_all, dtype=jnp.int32)
    filled = jax.random.randint(key_a, (), 0, OWNERS).astype(jnp.int32)
    raw = jax.random.randint(key_b, (N_DP, slots_all), 0, 1 << 16).astype(jnp.int32)
    scores = raw * slots_all + slot_ids[None, :]
    forced = slot_ids // SLOT == filled
    scores = jnp.where(forced[None, :], slot_ids[None, :] - slots_all, scores)
    _, picked = lax.top_k(-scores, PSEQ)
    owner_rows = (picked // SLOT).astype(jnp.int32)
    shuffle_raw = jax.random.randint(key_c, (N_DP, PSEQ), 0, 1 << 16).astype(jnp.int32)
    shuffle_keys = shuffle_raw * PSEQ + jnp.arange(PSEQ, dtype=jnp.int32)[None, :]
    order = jnp.argsort(shuffle_keys, axis=1, stable=True)
    owner_rows = jnp.take_along_axis(owner_rows, order, axis=1)
    return owner_rows.reshape(-1).astype(jnp.int32)


def level_of(key, shape, cuts, smallest, top_value):
    level = 1.0
    for dim, blocks in cuts:
        draws = jax.random.uniform(jax.random.fold_in(jax.random.fold_in(key, 6), dim), (blocks,), jnp.float32, smallest / len(cuts), top_value / len(cuts))
        level = level * jnp.repeat(jnp.exp(draws), shape[dim] // blocks).reshape((-1,) + (1,) * (len(shape) - 1 - dim))
    return level


def gaussian(rng, dims, spread, limit, cuts=(), kind=jnp.bfloat16):
    level = level_of(rng, dims, cuts, -0.22, 0.18) if cuts else 1.0
    array = jax.random.normal(rng, dims, jnp.float32) * spread * level
    return jnp.minimum(jnp.maximum(array, -limit), limit).astype(kind)


def setup_inputs(seed: int = 0) -> dict:
    keys = jax.random.split(jax.random.key(seed), 8)
    tokens = gaussian(keys[0], (TOKENS, D), 1.0, 6.0, ((0, 16),))
    upstream = gaussian(keys[1], (TOKENS, D), 1.0, 6.0, ((0, 16),))
    corpus = draw_corpus(jax.random.fold_in(keys[7], 71), 0)
    lengths = draw_lengths(jax.random.fold_in(keys[7], 71), 0)
    owners = draw_owners(jax.random.fold_in(keys[7], 71), 0)
    w_in = gaussian(keys[5], (D, FF), 1.0, 6.0, ((0, 32), (1, 8)))
    w_out = gaussian(keys[6], (D, FF), 1.0, 6.0, ((0, 32), (1, 8)))
    return {"tokens": tokens, "upstream": upstream, "corpus": corpus, "lengths": lengths, "owners": owners, "w_in": w_in, "w_out": w_out}


LEARN_RATE = 0.5
EPSILON = 1e-06

def reference(tokens, upstream, corpus, lengths, owners, w_in, w_out):
    scale_in = D ** (-0.5)
    scale_out = FF ** (-0.5)
    tok_blocks = tokens.reshape(N_DP, TOK_DEV, D)
    up_blocks = upstream.reshape(N_DP, TOK_DEV, D)

    def learn_block(totals, pair):
        x_rows, y_rows = pair
        preact = jnp.dot(x_rows, w_in, preferred_element_type=jnp.float32) * scale_in
        activation, backward = jax.vjp(jax.nn.gelu, preact)
        hidden = activation.astype(jnp.bfloat16)
        d_hidden = jnp.dot(y_rows, w_out, preferred_element_type=jnp.float32) * scale_out
        d_preact = backward(d_hidden)[0].astype(jnp.bfloat16)
        term_in = (jnp.dot(x_rows.T, d_preact, preferred_element_type=jnp.float32) * scale_in).astype(jnp.bfloat16)
        term_out = (jnp.dot(y_rows.T, hidden, preferred_element_type=jnp.float32) * scale_out).astype(jnp.bfloat16)
        term_in, term_out = lax.optimization_barrier((term_in, term_out))
        return ((totals[0] + term_in.astype(jnp.float32), totals[1] + term_out.astype(jnp.float32)), None)
    start = (jnp.zeros((D, FF), jnp.float32), jnp.zeros((D, FF), jnp.float32))
    (grad_in, grad_out), _ = lax.scan(learn_block, start, (tok_blocks, up_blocks))
    new_in = (w_in.astype(jnp.float32) - LEARN_RATE * grad_in).astype(jnp.bfloat16)
    new_out = (w_out.astype(jnp.float32) - LEARN_RATE * grad_out).astype(jnp.bfloat16)
    corpus_blocks = corpus.reshape(N_DP, CTOK_DEV, D)
    length_blocks = lengths.reshape(N_DP, PSEQ)

    def embed(pair):
        c_rows, lens = pair
        preact = jnp.dot(c_rows, w_in, preferred_element_type=jnp.float32) * scale_in
        hidden = jax.nn.gelu(preact).astype(jnp.bfloat16)
        branch = jnp.dot(hidden, w_out.T, preferred_element_type=jnp.float32) * scale_out
        whole = c_rows.astype(jnp.float32) + branch
        live = (jnp.arange(PLEN)[None, :] < lens[:, None]).astype(jnp.float32)
        summed = jnp.einsum('pl,pld->pd', live, whole.reshape(PSEQ, PLEN, D), precision=lax.Precision.HIGHEST)
        pooled = summed * (1.0 / lens.astype(jnp.float32))[:, None]
        meansq = lax.optimization_barrier(jnp.mean(pooled * pooled, axis=1))
        return (pooled * lax.rsqrt(meansq + EPSILON)[:, None]).astype(jnp.bfloat16)
    embedding = lax.map(embed, (corpus_blocks, length_blocks)).reshape(PASSAGES, D)
    owner_blocks = owners.reshape(N_DP, PSEQ)
    position = jnp.arange(PSEQ)
    same = owner_blocks[:, :, None] == owner_blocks[:, None, :]
    earlier = position[None, :] < position[:, None]
    rank = lax.optimization_barrier(jnp.sum(jnp.logical_and(same, earlier[None, :, :]), axis=2))
    device = jnp.arange(N_DP)[:, None]
    target = (owner_blocks * CAP + device * SLOT + rank).astype(jnp.int32).reshape(-1)
    index = jnp.zeros((OWNERS * CAP, D), jnp.bfloat16).at[target].set(embedding)
    return (new_in, new_out, index)
```

```python
import functools
import math

import jax
import jax.numpy as jnp
from jax import lax
from jax.experimental import pallas as pl
from jax.experimental.pallas import tpu as pltpu
from jax.sharding import Mesh
from jax.sharding import PartitionSpec as P

DP = ("dp_0", "dp_1")
GROUP_DP = ("group", "dp_0", "dp_1")
AXES = ("group", "dp_0", "dp_1", "tensor")
MESH = pl.DeviceIdType.MESH

LEARN_RATE = 0.5
EPSILON = 1e-06
F32 = jnp.float32
BF16 = jnp.bfloat16
NZ = 8


def kernel(
    plen,
    scale_in,
    scale_out,
    tokens_ref,
    upstream_ref,
    corpus_ref,
    len_ref,
    win_ref,
    wout_ref,
    new_in_ref,
    new_out_ref,
    pool_ref,
    tok,
    up,
    cor,
    w_in,
    w_out,
    acc_p,
    acc_d,
    acc_c,
    hid,
    dpre,
    g_in,
    g_out,
    r_in,
    r_out,
    c_out,
    t_in,
    c_in,
    fin,
    land,
    lsem,
    ssem,
    rsem,
):
    g = lax.axis_index("group")
    yh = lax.axis_index("dp_0")
    z = lax.axis_index("dp_1")
    t = lax.axis_index("tensor")
    cls = lax.rem(g + yh, 2)
    half = w_in.shape[-1]
    shard = w_in.shape[-2]
    swap = (1 - g, yh, z, t)
    mate = (1 - g, 1 - yh, z, t)
    diag = (g, 1 - yh, z, t)
    zup = (g, yh, lax.rem(z + 1, NZ), t)
    zdn = (g, yh, lax.rem(z + NZ - 1, NZ), t)
    ring = (zup, zdn)
    step_of = (1, -1)

    def at(k):
        return lax.rem(z + k + 2 * NZ, NZ)

    pair = z // 2
    e = 1 - 2 * lax.rem(z, 2)
    half_nz = NZ // 2
    pairs = (
        None,
        pair,
        lax.rem(pair - e + half_nz, half_nz),
        lax.rem(pair + e + half_nz, half_nz),
        lax.rem(pair + 2, half_nz),
    )

    count = [0]
    sent = []

    def push(src, dst, device):
        k = count[0]
        count[0] += 1
        copy = pltpu.make_async_remote_copy(
            src_ref=src,
            dst_ref=dst,
            send_sem=ssem.at[k],
            recv_sem=rsem.at[k],
            device_id=device,
            device_id_type=MESH,
        )
        copy.start()
        sent.append(copy)
        return copy

    own_cols = pl.ds(pl.multiple_of(cls * half, half), half)
    other_cols = pl.ds(pl.multiple_of((1 - cls) * half, half), half)
    loads = []
    for k, (src, dst) in enumerate(
        (
            (win_ref.at[:, own_cols], w_in.at[g, yh, z]),
            (wout_ref.at[:, own_cols], w_out.at[g, yh, z]),
            (tokens_ref, tok),
            (corpus_ref, cor),
            (upstream_ref, up),
        )
    ):
        copy = pltpu.make_async_copy(src, dst, lsem.at[k])
        copy.start()
        loads.append(copy)

    barrier = pltpu.get_barrier_semaphore()
    for device in (swap, mate, diag, zup, zdn):
        pl.semaphore_signal(barrier, inc=1, device_id=device, device_id_type=MESH)
    pl.semaphore_wait(barrier, 5)

    a0 = push(win_ref.at[:, own_cols], w_in.at[g, yh, z], mate)
    a1 = push(win_ref.at[:, other_cols], w_in.at[g, yh, z], swap)
    a2 = push(win_ref.at[:, other_cols], w_in.at[g, yh, z], diag)
    a3 = push(wout_ref.at[:, other_cols], w_out.at[g, yh, z], swap)
    loads[0].wait()
    loads[1].wait()
    for copy in (a0, a1, a2):
        copy.wait_recv()

    def send_in(s, d):
        o = at(-step_of[d] * (s - 1))
        block = w_in.at[:, :, o] if s < 4 else w_in.at[d, :, o]
        return push(block, block, ring[d])

    def send_out(s, d):
        o = at(-step_of[d] * (s - 1))
        block = w_out.at[:, yh, o] if s < 4 else w_out.at[d, yh, o]
        return push(block, block, ring[d])

    def mate_out(s, d):
        o = at(-step_of[d] * s)
        block = w_out.at[:, yh, o] if s < 4 else w_out.at[d, yh, o]
        return push(block, block, mate)

    def rows_of(ref, rows, p):
        parts = []
        for q in range(4):
            at_q = pl.multiple_of(q * NZ * shard + p * 2 * shard, 2 * shard)
            parts.append(ref[rows, pl.ds(at_q, 2 * shard)])
        return jnp.concatenate(parts, axis=1)

    def weight(w, p):
        parts = []
        for q in range(4):
            block = w[q // 2, q % 2, pl.ds(2 * p, 2)]
            parts.append(block.reshape(2 * shard, half))
        return jnp.concatenate(parts, axis=0)

    def multiply(x, w, acc, p, first):
        tile = 256

        def body(m, carry):
            rows = pl.ds(pl.multiple_of(m * tile, tile), tile)
            part = jnp.dot(rows_of(x, rows, p), weight(w, p), preferred_element_type=F32)
            acc[rows, :] = part if first else acc[rows, :] + part
            return carry

        lax.fori_loop(0, x.shape[0] // tile, body, 0)

    got_in = [[None] * 2 for _ in range(5)]
    got_out = [[None] * 2 for _ in range(5)]
    got_mate = [[None] * 2 for _ in range(5)]
    for d in range(2):
        got_in[1][d] = send_in(1, d)
    a3.wait_recv()
    for d in range(2):
        got_out[1][d] = send_out(1, d)
    got_mate[0][0] = mate_out(0, 0)
    loads[2].wait()
    loads[3].wait()
    for s in range(1, 5):
        for d in range(2):
            got_in[s][d].wait_recv()
            if s < 4:
                got_in[s + 1][d] = send_in(s + 1, d)
        for d in range(2):
            got_out[s][d].wait_recv()
            if s < 4:
                got_out[s + 1][d] = send_out(s + 1, d)
            got_mate[s][d] = mate_out(s, d)
        multiply(tok, w_in, acc_p, pairs[s], s == 1)
        multiply(cor, w_in, acc_c, pairs[s], s == 1)
        if s == 1:
            got_mate[0][0].wait_recv()
            loads[4].wait()
        for d in range(2):
            if s > 1:
                got_mate[s - 1][d].wait_recv()
        if s > 1:
            multiply(up, w_out, acc_d, pairs[s - 1], s == 2)
    for d in range(2):
        got_mate[4][d].wait_recv()
    multiply(up, w_out, acc_d, pairs[4], False)

    root = math.sqrt(2.0 / math.pi)

    def gelu_parts(p):
        th = jnp.tanh(root * (p + 0.044715 * (p * p * p)))
        return 0.5 * (1.0 + th), th

    slab = 32

    def activate(m, carry):
        rows = pl.ds(pl.multiple_of(m * slab, slab), slab)
        p = acc_p[rows, :] * scale_in
        dh = acc_d[rows, :] * scale_out
        cdf, th = gelu_parts(p)
        hid[rows, :] = (p * cdf).astype(BF16)
        slope = cdf + (0.5 * root) * p * (1.0 - th * th) * (1.0 + (3 * 0.044715) * (p * p))
        dpre[rows, :] = (dh * slope).astype(BF16)
        return carry

    lax.fori_loop(0, tok.shape[0] // slab, activate, 0)

    def gradient(x, y, out, scale, p):
        def body(gg, carry):
            parts = []
            for yy in range(2):
                at_q = pl.multiple_of((gg * 2 + yy) * NZ * shard + p * 2 * shard, 2 * shard)
                parts.append(x[:, pl.ds(at_q, 2 * shard)])
            both = lax.dot_general(
                jnp.concatenate(parts, axis=1),
                y[...],
                (((0,), (0,)), ((), ())),
                preferred_element_type=F32,
            )
            both = (both * scale).astype(BF16).reshape(2, 2, shard, half)
            for yy in range(2):
                out[gg, yy, pl.ds(2 * p, 2)] = both[yy]
            return carry

        lax.fori_loop(0, 2, body, 0)

    def add(a, b):
        return (a.astype(F32) + b.astype(F32)).astype(BF16)

    back_in = [[None] * 2 for _ in range(5)]
    back_out = [[None] * 2 for _ in range(5)]
    back_mate = [None] * 5

    def return_in(s, d):
        o = at(step_of[d] * (5 - s))
        if s == 1:
            back_in[1][d] = push(g_in.at[d, :, o], r_in.at[d, 0, d], ring[d])
            return
        back_in[s - 1][d].wait_recv()
        if s == 2:
            for yy in range(2):
                g_in[d, yy, o] = add(g_in[d, yy, o], r_in[d, 0, d, yy])
        else:
            for gg in range(2):
                for yy in range(2):
                    g_in[gg, yy, o] = add(g_in[gg, yy, o], r_in[d, s - 2, gg, yy])
        back_in[s][d] = push(g_in.at[:, :, o], r_in.at[d, s - 1], ring[d])

    def return_out(s, d):
        o = at(step_of[d] * (5 - s))
        if s == 1:
            back_out[1][d] = push(g_out.at[d, yh, o], r_out.at[d, 0, d], ring[d])
            return
        back_out[s - 1][d].wait_recv()
        if s == 2:
            g_out[d, yh, o] = add(g_out[d, yh, o], r_out[d, 0, d])
        else:
            for gg in range(2):
                g_out[gg, yh, o] = add(g_out[gg, yh, o], r_out[d, s - 2, gg])
        back_out[s][d] = push(g_out.at[:, yh, o], r_out.at[d, s - 1], ring[d])

    def to_mate(j):
        back_mate[j] = push(
            g_out.at[:, 1 - yh, pl.ds(2 * pairs[j], 2)], c_out.at[j - 1], mate
        )

    def from_mate(j):
        back_mate[j].wait_recv()
        for gg in range(2):
            for zz in range(2):
                o = 2 * pairs[j] + zz
                g_out[gg, yh, o] = add(g_out[gg, yh, o], c_out[j - 1, gg, zz])

    for s in range(1, 5):
        j = 5 - s
        gradient(tok, dpre, g_in, scale_in, pairs[j])
        for d in range(2):
            return_in(s, d)
        gradient(up, hid, g_out, scale_out, pairs[j])
        to_mate(j)
        if s > 1:
            from_mate(j + 1)
            for d in range(2):
                return_out(s - 1, d)

    passages = pool_ref.shape[0]
    rows_c = cor.shape[0]
    cdf, _ = gelu_parts(acc_c[...] * scale_in)
    ch = (acc_c[...] * scale_in * cdf).astype(BF16)
    row = lax.broadcasted_iota(jnp.int32, (passages, rows_c), 0)
    col = lax.broadcasted_iota(jnp.int32, (passages, rows_c), 1)
    lens = jnp.zeros((passages, rows_c), jnp.int32)
    for i in range(passages):
        lens = jnp.where(row == i, len_ref[i], lens)
    inside = jnp.logical_and(col >= row * plen, col < row * plen + lens)
    live = jnp.where(inside, 1.0, 0.0).astype(BF16)
    ph = jnp.dot(live, ch, preferred_element_type=F32)
    hi = ph.astype(BF16)
    lo = (ph - hi.astype(F32)).astype(BF16)
    hl = jnp.concatenate([hi.astype(F32), lo.astype(F32)], axis=0).astype(BF16)

    def branch(q, carry):
        w = w_out[q // 2, lax.rem(q, 2)].reshape(NZ * shard, half)
        both = lax.dot_general(hl, w, (((1,), (1,)), ((), ())), preferred_element_type=F32)
        cols = pl.ds(pl.multiple_of(q * NZ * shard, NZ * shard), NZ * shard)
        pool_ref[:, cols] = (both[:passages] + both[passages:]) * scale_out
        return carry

    lax.fori_loop(0, 4, branch, 0)

    from_mate(1)
    for d in range(2):
        return_out(4, d)
        back_in[4][d].wait_recv()
    for gg in range(2):
        for yy in range(2):
            total = (
                g_in[gg, yy, z].astype(F32)
                + r_in[0, 3, gg, yy].astype(F32)
                + r_in[1, 3, gg, yy].astype(F32)
            )
            t_in[gg, yy] = total.astype(BF16)
    last = push(t_in.at[:, 1 - yh], c_in, mate)
    for d in range(2):
        back_out[4][d].wait_recv()
    for gg in range(2):
        total = (
            g_out[gg, yh, z].astype(F32)
            + r_out[0, 3, gg].astype(F32)
            + r_out[1, 3, gg].astype(F32)
        )
        fin[1, gg] = (w_out[gg, yh, z].astype(F32) - LEARN_RATE * total).astype(BF16)
    home_out = push(fin.at[1, 1 - g], land.at[1], swap)
    last.wait_recv()
    for gg in range(2):
        total = t_in[gg, yh].astype(F32) + c_in[gg].astype(F32)
        fin[0, gg] = (w_in[gg, yh, z].astype(F32) - LEARN_RATE * total).astype(BF16)
    home_in = push(fin.at[0, 1 - g], land.at[0], swap)
    new_out_ref[:, own_cols] = fin[1, g]
    new_in_ref[:, own_cols] = fin[0, g]
    home_out.wait_recv()
    new_out_ref[:, other_cols] = land[1]
    home_in.wait_recv()
    new_in_ref[:, other_cols] = land[0]
    for copy in sent:
        copy.wait_send()


def fused(tokens, upstream, corpus, lengths, w_in, w_out, scale_in, scale_out):
    shard, local_ff = w_in.shape
    half = local_ff // 2
    n_tok, width = tokens.shape
    n_corpus = corpus.shape[0]
    npass = lengths.shape[0]
    full = (2, 2, NZ, shard, half)
    n_sem = 64
    any_spec = pl.BlockSpec(memory_space=pl.ANY)
    vmem_spec = pl.BlockSpec(memory_space=pltpu.VMEM)
    return pl.pallas_call(
        functools.partial(kernel, n_corpus // npass, scale_in, scale_out),
        out_shape=(
            jax.ShapeDtypeStruct((shard, local_ff), BF16),
            jax.ShapeDtypeStruct((shard, local_ff), BF16),
            jax.ShapeDtypeStruct((npass, width), F32),
        ),
        in_specs=[
            any_spec,
            any_spec,
            any_spec,
            pl.BlockSpec(memory_space=pltpu.SMEM),
            any_spec,
            any_spec,
        ],
        out_specs=(vmem_spec, vmem_spec, vmem_spec),
        scratch_shapes=[
            pltpu.VMEM((n_tok, width), BF16),
            pltpu.VMEM((n_tok, width), BF16),
            pltpu.VMEM((n_corpus, width), BF16),
            pltpu.VMEM(full, BF16),
            pltpu.VMEM(full, BF16),
            pltpu.VMEM((n_tok, half), F32),
            pltpu.VMEM((n_tok, half), F32),
            pltpu.VMEM((n_corpus, half), F32),
            pltpu.VMEM((n_tok, half), BF16),
            pltpu.VMEM((n_tok, half), BF16),
            pltpu.VMEM(full, BF16),
            pltpu.VMEM(full, BF16),
            pltpu.VMEM((2, 4, 2, 2, shard, half), BF16),
            pltpu.VMEM((2, 4, 2, shard, half), BF16),
            pltpu.VMEM((4, 2, 2, shard, half), BF16),
            pltpu.VMEM((2, 2, shard, half), BF16),
            pltpu.VMEM((2, shard, half), BF16),
            pltpu.VMEM((2, 2, shard, half), BF16),
            pltpu.VMEM((2, shard, half), BF16),
            pltpu.SemaphoreType.DMA((5,)),
            pltpu.SemaphoreType.DMA((n_sem,)),
            pltpu.SemaphoreType.DMA((n_sem,)),
        ],
        compiler_params=pltpu.CompilerParams(
            collective_id=0, has_side_effects=True, vmem_limit_bytes=60 * 1024 * 1024
        ),
    )(tokens, upstream, corpus, lengths, w_in, w_out)


def local(tokens, upstream, corpus, lengths, owners, w_in, w_out):
    groups = lax.axis_size("group")
    replicas = lax.axis_size(DP)
    shard_rows = w_in.shape[0]
    local_ff = w_in.shape[1]
    width = shard_rows * groups * replicas
    scale_in = 1.0 / math.sqrt(width)
    scale_out = 1.0 / math.sqrt(local_ff * lax.axis_size("tensor"))
    cols = width // lax.axis_size("tensor")
    n_corpus = corpus.shape[0]
    npass = lengths.shape[0]
    plen = n_corpus // npass
    owner_count = groups * replicas
    new_in, new_out, partial_pool = fused(
        tokens, upstream, corpus, lengths, w_in, w_out, scale_in, scale_out
    )
    live = jnp.arange(plen, dtype=jnp.int32)[None, :] < lengths[:, None]
    own_cols = lax.dynamic_slice_in_dim(corpus, lax.axis_index("tensor") * cols, cols, 1).reshape(
        npass, plen, cols
    )
    base = jnp.einsum("pl,pld->pd", live.astype(BF16), own_cols, preferred_element_type=F32)
    pieces = partial_pool.reshape(npass, -1, cols).transpose(1, 0, 2)
    pieces = lax.all_to_all(pieces, "tensor", 0, 0, tiled=True)
    pooled_branch = lax.psum(jnp.sum(pieces, axis=0), "group")
    pooled = (base + pooled_branch) * (1.0 / lengths.astype(F32))[:, None]
    squared = lax.psum(jnp.sum(pooled * pooled, axis=1), "tensor")
    embedding = (pooled * lax.rsqrt(squared / width + EPSILON)[:, None]).astype(BF16)
    owner_ids = jnp.arange(owner_count, dtype=jnp.int32)
    pick = owners[None, :] == owner_ids[:, None]
    outbox = jnp.einsum(
        "op,pd->od", pick.astype(BF16), embedding, preferred_element_type=F32
    ).astype(BF16)
    inbox = lax.all_to_all(outbox[:, None], GROUP_DP, split_axis=0, concat_axis=0, tiled=True)
    index_rows = inbox[:replicas].reshape(replicas, cols)
    return (new_in, new_out, index_rows)


def solution(mesh):
    torus = Mesh(
        mesh.devices.reshape(mesh.shape["group"], 2, NZ, mesh.shape["tensor"]),
        ("group", "dp_0", "dp_1", "tensor"),
    )
    return jax.shard_map(
        local,
        mesh=torus,
        in_specs=(
            P(DP, None),
            P(DP, None),
            P(DP, None),
            P(DP),
            P(DP),
            P(GROUP_DP, "tensor"),
            P(GROUP_DP, "tensor"),
        ),
        out_specs=(P(GROUP_DP, "tensor"), P(GROUP_DP, "tensor"), P(GROUP_DP, "tensor")),
        check_vma=False,
    )
```

```python
import functools
import math

import jax
import jax.numpy as jnp
from jax import lax
from jax.experimental import pallas as pl
from jax.experimental.pallas import tpu as pltpu
from jax.sharding import Mesh
from jax.sharding import PartitionSpec as P

DP = ("dp_0", "dp_1")
GROUP_DP = ("group", "dp_0", "dp_1")
AXES = ("group", "dp_0", "dp_1", "tensor")
MESH = pl.DeviceIdType.MESH

LEARN_RATE = 0.5
EPSILON = 1e-06
F32 = jnp.float32
BF16 = jnp.bfloat16
NZ = 8
NT = 8


def kernel(
    plen,
    scale_in,
    scale_out,
    tokens_ref,
    upstream_ref,
    corpus_ref,
    len_ref,
    owner_ref,
    win_ref,
    wout_ref,
    new_in_ref,
    new_out_ref,
    index_ref,
    tok,
    up,
    cor,
    w_in,
    w_out,
    acc_p,
    acc_d,
    acc_c,
    hid,
    dpre,
    g_in,
    g_out,
    r_in,
    r_out,
    c_out,
    t_in,
    c_in,
    fin,
    land,
    pool,
    pool_in,
    square,
    square_in,
    letter,
    letter_in,
    lsem,
    ssem,
    rsem,
):
    g = lax.axis_index("group")
    yh = lax.axis_index("dp_0")
    z = lax.axis_index("dp_1")
    t = lax.axis_index("tensor")
    cls = lax.rem(g + yh, 2)
    half = w_in.shape[-1]
    shard = w_in.shape[-2]
    swap = (1 - g, yh, z, t)
    mate = (1 - g, 1 - yh, z, t)
    diag = (g, 1 - yh, z, t)
    zup = (g, yh, lax.rem(z + 1, NZ), t)
    zdn = (g, yh, lax.rem(z + NZ - 1, NZ), t)
    ring = (zup, zdn)

    def cell(dg, dt):
        return (lax.rem(g + dg, 2), yh, z, lax.rem(t + dt, NT))

    step_of = (1, -1)

    def at(k):
        return lax.rem(z + k + 2 * NZ, NZ)

    pair = z // 2
    e = 1 - 2 * lax.rem(z, 2)
    half_nz = NZ // 2
    pairs = (
        None,
        pair,
        lax.rem(pair - e + half_nz, half_nz),
        lax.rem(pair + e + half_nz, half_nz),
        lax.rem(pair + 2, half_nz),
    )

    count = [0]
    sent = []

    def push(src, dst, device):
        k = count[0]
        count[0] += 1
        copy = pltpu.make_async_remote_copy(
            src_ref=src,
            dst_ref=dst,
            send_sem=ssem.at[k],
            recv_sem=rsem.at[k],
            device_id=device,
            device_id_type=MESH,
        )
        copy.start()
        sent.append(copy)
        return copy

    own_cols = pl.ds(pl.multiple_of(cls * half, half), half)
    other_cols = pl.ds(pl.multiple_of((1 - cls) * half, half), half)
    loads = []
    for k, (src, dst) in enumerate(
        (
            (win_ref.at[:, own_cols], w_in.at[g, yh, z]),
            (wout_ref.at[:, own_cols], w_out.at[g, yh, z]),
            (tokens_ref, tok),
            (corpus_ref, cor),
            (upstream_ref, up),
        )
    ):
        copy = pltpu.make_async_copy(src, dst, lsem.at[k])
        copy.start()
        loads.append(copy)

    barrier = pltpu.get_barrier_semaphore()
    met = [swap, mate, diag, zup, zdn]
    met += [cell(dg, dt) for dg in range(2) for dt in range(1, NT)]
    for device in met:
        pl.semaphore_signal(barrier, inc=1, device_id=device, device_id_type=MESH)
    pl.semaphore_wait(barrier, len(met))

    a0 = push(win_ref.at[:, own_cols], w_in.at[g, yh, z], mate)
    a1 = push(win_ref.at[:, other_cols], w_in.at[g, yh, z], swap)
    a2 = push(win_ref.at[:, other_cols], w_in.at[g, yh, z], diag)
    a3 = push(wout_ref.at[:, other_cols], w_out.at[g, yh, z], swap)
    loads[0].wait()
    loads[1].wait()
    for copy in (a0, a1, a2):
        copy.wait_recv()

    def send_in(s, d):
        o = at(-step_of[d] * (s - 1))
        block = w_in.at[:, :, o] if s < 4 else w_in.at[d, :, o]
        return push(block, block, ring[d])

    def send_out(s, d):
        o = at(-step_of[d] * (s - 1))
        block = w_out.at[:, yh, o] if s < 4 else w_out.at[d, yh, o]
        return push(block, block, ring[d])

    def mate_out(s, d):
        o = at(-step_of[d] * s)
        block = w_out.at[:, yh, o] if s < 4 else w_out.at[d, yh, o]
        return push(block, block, mate)

    def rows_of(ref, rows, p):
        parts = []
        for q in range(4):
            at_q = pl.multiple_of(q * NZ * shard + p * 2 * shard, 2 * shard)
            parts.append(ref[rows, pl.ds(at_q, 2 * shard)])
        return jnp.concatenate(parts, axis=1)

    def weight(w, p):
        parts = []
        for q in range(4):
            block = w[q // 2, q % 2, pl.ds(2 * p, 2)]
            parts.append(block.reshape(2 * shard, half))
        return jnp.concatenate(parts, axis=0)

    def multiply(x, w, acc, p, first):
        tile = 256

        def body(m, carry):
            rows = pl.ds(pl.multiple_of(m * tile, tile), tile)
            part = jnp.dot(rows_of(x, rows, p), weight(w, p), preferred_element_type=F32)
            acc[rows, :] = part if first else acc[rows, :] + part
            return carry

        lax.fori_loop(0, x.shape[0] // tile, body, 0)

    got_in = [[None] * 2 for _ in range(5)]
    got_out = [[None] * 2 for _ in range(5)]
    got_mate = [[None] * 2 for _ in range(5)]
    for d in range(2):
        got_in[1][d] = send_in(1, d)
    a3.wait_recv()
    for d in range(2):
        got_out[1][d] = send_out(1, d)
    got_mate[0][0] = mate_out(0, 0)
    loads[2].wait()
    loads[3].wait()
    for s in range(1, 5):
        for d in range(2):
            got_in[s][d].wait_recv()
            if s < 4:
                got_in[s + 1][d] = send_in(s + 1, d)
        for d in range(2):
            got_out[s][d].wait_recv()
            if s < 4:
                got_out[s + 1][d] = send_out(s + 1, d)
            got_mate[s][d] = mate_out(s, d)
        multiply(tok, w_in, acc_p, pairs[s], s == 1)
        multiply(cor, w_in, acc_c, pairs[s], s == 1)
        if s == 1:
            got_mate[0][0].wait_recv()
            loads[4].wait()
        for d in range(2):
            if s > 1:
                got_mate[s - 1][d].wait_recv()
        if s > 1:
            multiply(up, w_out, acc_d, pairs[s - 1], s == 2)
    for d in range(2):
        got_mate[4][d].wait_recv()
    multiply(up, w_out, acc_d, pairs[4], False)

    root = math.sqrt(2.0 / math.pi)

    def gelu_parts(p):
        th = jnp.tanh(root * (p + 0.044715 * (p * p * p)))
        return 0.5 * (1.0 + th), th

    slab = 32

    def activate(m, carry):
        rows = pl.ds(pl.multiple_of(m * slab, slab), slab)
        p = acc_p[rows, :] * scale_in
        dh = acc_d[rows, :] * scale_out
        cdf, th = gelu_parts(p)
        hid[rows, :] = (p * cdf).astype(BF16)
        slope = cdf + (0.5 * root) * p * (1.0 - th * th) * (1.0 + (3 * 0.044715) * (p * p))
        dpre[rows, :] = (dh * slope).astype(BF16)
        return carry

    lax.fori_loop(0, tok.shape[0] // slab, activate, 0)

    def gradient(x, y, out, scale, p):
        def body(gg, carry):
            parts = []
            for yy in range(2):
                at_q = pl.multiple_of((gg * 2 + yy) * NZ * shard + p * 2 * shard, 2 * shard)
                parts.append(x[:, pl.ds(at_q, 2 * shard)])
            both = lax.dot_general(
                jnp.concatenate(parts, axis=1),
                y[...],
                (((0,), (0,)), ((), ())),
                preferred_element_type=F32,
            )
            both = (both * scale).astype(BF16).reshape(2, 2, shard, half)
            for yy in range(2):
                out[gg, yy, pl.ds(2 * p, 2)] = both[yy]
            return carry

        lax.fori_loop(0, 2, body, 0)

    def add(a, b):
        return (a.astype(F32) + b.astype(F32)).astype(BF16)

    back_in = [[None] * 2 for _ in range(5)]
    back_out = [[None] * 2 for _ in range(5)]
    back_mate = [None] * 5

    def return_in(s, d):
        o = at(step_of[d] * (5 - s))
        if s == 1:
            back_in[1][d] = push(g_in.at[d, :, o], r_in.at[d, 0, d], ring[d])
            return
        back_in[s - 1][d].wait_recv()
        if s == 2:
            for yy in range(2):
                g_in[d, yy, o] = add(g_in[d, yy, o], r_in[d, 0, d, yy])
        else:
            for gg in range(2):
                for yy in range(2):
                    g_in[gg, yy, o] = add(g_in[gg, yy, o], r_in[d, s - 2, gg, yy])
        back_in[s][d] = push(g_in.at[:, :, o], r_in.at[d, s - 1], ring[d])

    def return_out(s, d):
        o = at(step_of[d] * (5 - s))
        if s == 1:
            back_out[1][d] = push(g_out.at[d, yh, o], r_out.at[d, 0, d], ring[d])
            return
        back_out[s - 1][d].wait_recv()
        if s == 2:
            g_out[d, yh, o] = add(g_out[d, yh, o], r_out[d, 0, d])
        else:
            for gg in range(2):
                g_out[gg, yh, o] = add(g_out[gg, yh, o], r_out[d, s - 2, gg])
        back_out[s][d] = push(g_out.at[:, yh, o], r_out.at[d, s - 1], ring[d])

    def to_mate(j):
        back_mate[j] = push(
            g_out.at[:, 1 - yh, pl.ds(2 * pairs[j], 2)], c_out.at[j - 1], mate
        )

    def from_mate(j):
        back_mate[j].wait_recv()
        for gg in range(2):
            for zz in range(2):
                o = 2 * pairs[j] + zz
                g_out[gg, yh, o] = add(g_out[gg, yh, o], c_out[j - 1, gg, zz])

    passages = len_ref.shape[0]
    rows_c = cor.shape[0]
    feat = pool.shape[-1]
    mine = pl.ds(pl.multiple_of(t * feat, feat), feat)

    def per_passage(ref, shape):
        row = lax.broadcasted_iota(jnp.int32, shape, 0)
        out = jnp.zeros(shape, jnp.int32)
        for i in range(passages):
            out = jnp.where(row == i, ref[i], out)
        return out

    def pool_rows():
        pre = acc_c[...] * scale_in
        cdf, _ = gelu_parts(pre)
        ch = (pre * cdf).astype(BF16)
        shape = (passages, rows_c)
        row = lax.broadcasted_iota(jnp.int32, shape, 0)
        col = lax.broadcasted_iota(jnp.int32, shape, 1)
        lens = per_passage(len_ref, shape)
        inside = jnp.logical_and(col >= row * plen, col < row * plen + lens)
        live = jnp.where(inside, 1.0, 0.0).astype(BF16)
        ph = jnp.dot(live, ch, preferred_element_type=F32)
        hi = ph.astype(BF16)
        lo = (ph - hi.astype(F32)).astype(BF16)
        hl = jnp.concatenate([hi.astype(F32), lo.astype(F32)], axis=0).astype(BF16)

        def branch(q, carry):
            w = w_out[q // 2, lax.rem(q, 2)].reshape(NZ * shard, half)
            both = lax.dot_general(hl, w, (((1,), (1,)), ((), ())), preferred_element_type=F32)
            both = (both[:passages] + both[passages:]) * scale_out
            for k in range(NZ * shard // feat):
                pool[q * (NZ * shard // feat) + k] = both[:, k * feat : (k + 1) * feat]
            return carry

        lax.fori_loop(0, 4, branch, 0)
        base = jnp.dot(live, cor[:, mine], preferred_element_type=F32)
        copies = []
        for dg in range(2):
            for dt in range(NT):
                if dg or dt:
                    src = pool.at[lax.rem(t + dt, NT)]
                    copies.append(push(src, pool_in.at[dg * NT + dt], cell(dg, dt)))
        return base, copies

    def square_rows(base, copies):
        total = base + pool[t]
        for copy in copies:
            copy.wait_recv()
        for k in range(1, 2 * NT):
            total = total + pool_in[k]
        lens = per_passage(len_ref, total.shape)
        pooled = total * (1.0 / lens.astype(F32))
        own_square = jnp.sum(pooled * pooled, axis=1, keepdims=True)
        square[...] = jnp.broadcast_to(own_square, square.shape)
        copies = [push(square, square_in.at[dt], cell(0, dt)) for dt in range(1, NT)]
        return pooled, own_square, copies

    def post_rows(pooled, own_square, copies):
        for copy in copies:
            copy.wait_recv()
        total = own_square
        for dt in range(1, NT):
            total = total + square_in[dt][:, :1]
        rows = pooled * lax.rsqrt(total / (NT * feat) + EPSILON)
        owners = per_passage(owner_ref, rows.shape)
        copies = []
        for a in range(2):
            for b in range(NZ):
                to_yh, to_z = lax.rem(yh + a, 2), at(b)
                owner = (g * 2 + to_yh) * NZ + to_z
                row = jnp.sum(jnp.where(owners == owner, rows, 0.0), axis=0, keepdims=True)
                if a or b:
                    letter[a * NZ + b] = row
                    copies.append(
                        push(
                            letter.at[a * NZ + b],
                            letter_in.at[yh * NZ + z],
                            (g, to_yh, to_z, t),
                        )
                    )
                else:
                    letter_in[yh * NZ + z] = row
        return copies

    def read_rows(copies):
        for copy in copies:
            copy.wait_recv()
        row = lax.broadcasted_iota(jnp.int32, index_ref.shape, 0)
        out = jnp.zeros(index_ref.shape, F32)
        for d in range(2 * NZ):
            out = jnp.where(row == d, jnp.broadcast_to(letter_in[d], out.shape), out)
        index_ref[...] = out.astype(BF16)

    stage = None
    for s in range(1, 5):
        j = 5 - s
        gradient(tok, dpre, g_in, scale_in, pairs[j])
        for d in range(2):
            return_in(s, d)
        gradient(up, hid, g_out, scale_out, pairs[j])
        to_mate(j)
        if s > 1:
            from_mate(j + 1)
            for d in range(2):
                return_out(s - 1, d)
        if s == 1:
            stage = pool_rows()
        elif s == 2:
            stage = square_rows(*stage)
        elif s == 3:
            stage = post_rows(*stage)

    from_mate(1)
    for d in range(2):
        return_out(4, d)
        back_in[4][d].wait_recv()
    for gg in range(2):
        for yy in range(2):
            total = (
                g_in[gg, yy, z].astype(F32)
                + r_in[0, 3, gg, yy].astype(F32)
                + r_in[1, 3, gg, yy].astype(F32)
            )
            t_in[gg, yy] = total.astype(BF16)
    last = push(t_in.at[:, 1 - yh], c_in, mate)
    for d in range(2):
        back_out[4][d].wait_recv()
    for gg in range(2):
        total = (
            g_out[gg, yh, z].astype(F32)
            + r_out[0, 3, gg].astype(F32)
            + r_out[1, 3, gg].astype(F32)
        )
        fin[1, gg] = (w_out[gg, yh, z].astype(F32) - LEARN_RATE * total).astype(BF16)
    home_out = push(fin.at[1, 1 - g], land.at[1], swap)
    last.wait_recv()
    for gg in range(2):
        total = t_in[gg, yh].astype(F32) + c_in[gg].astype(F32)
        fin[0, gg] = (w_in[gg, yh, z].astype(F32) - LEARN_RATE * total).astype(BF16)
    home_in = push(fin.at[0, 1 - g], land.at[0], swap)
    new_out_ref[:, own_cols] = fin[1, g]
    new_in_ref[:, own_cols] = fin[0, g]
    home_out.wait_recv()
    new_out_ref[:, other_cols] = land[1]
    home_in.wait_recv()
    new_in_ref[:, other_cols] = land[0]
    read_rows(stage)
    for copy in sent:
        copy.wait_send()


def fused(tokens, upstream, corpus, lengths, owners, w_in, w_out, scale_in, scale_out):
    shard, local_ff = w_in.shape
    half = local_ff // 2
    n_tok, width = tokens.shape
    n_corpus = corpus.shape[0]
    npass = lengths.shape[0]
    full = (2, 2, NZ, shard, half)
    n_sem = 96
    feat = width // NT
    any_spec = pl.BlockSpec(memory_space=pl.ANY)
    vmem_spec = pl.BlockSpec(memory_space=pltpu.VMEM)
    return pl.pallas_call(
        functools.partial(kernel, n_corpus // npass, scale_in, scale_out),
        out_shape=(
            jax.ShapeDtypeStruct((shard, local_ff), BF16),
            jax.ShapeDtypeStruct((shard, local_ff), BF16),
            jax.ShapeDtypeStruct((2 * NZ, feat), BF16),
        ),
        in_specs=[
            any_spec,
            any_spec,
            any_spec,
            pl.BlockSpec(memory_space=pltpu.SMEM),
            pl.BlockSpec(memory_space=pltpu.SMEM),
            any_spec,
            any_spec,
        ],
        out_specs=(vmem_spec, vmem_spec, vmem_spec),
        scratch_shapes=[
            pltpu.VMEM((n_tok, width), BF16),
            pltpu.VMEM((n_tok, width), BF16),
            pltpu.VMEM((n_corpus, width), BF16),
            pltpu.VMEM(full, BF16),
            pltpu.VMEM(full, BF16),
            pltpu.VMEM((n_tok, half), F32),
            pltpu.VMEM((n_tok, half), F32),
            pltpu.VMEM((n_corpus, half), F32),
            pltpu.VMEM((n_tok, half), BF16),
            pltpu.VMEM((n_tok, half), BF16),
            pltpu.VMEM(full, BF16),
            pltpu.VMEM(full, BF16),
            pltpu.VMEM((2, 4, 2, 2, shard, half), BF16),
            pltpu.VMEM((2, 4, 2, shard, half), BF16),
            pltpu.VMEM((4, 2, 2, shard, half), BF16),
            pltpu.VMEM((2, 2, shard, half), BF16),
            pltpu.VMEM((2, shard, half), BF16),
            pltpu.VMEM((2, 2, shard, half), BF16),
            pltpu.VMEM((2, shard, half), BF16),
            pltpu.VMEM((NT, npass, feat), F32),
            pltpu.VMEM((2 * NT, npass, feat), F32),
            pltpu.VMEM((npass, 128), F32),
            pltpu.VMEM((NT, npass, 128), F32),
            pltpu.VMEM((2 * NZ, 1, feat), F32),
            pltpu.VMEM((2 * NZ, 1, feat), F32),
            pltpu.SemaphoreType.DMA((5,)),
            pltpu.SemaphoreType.DMA((n_sem,)),
            pltpu.SemaphoreType.DMA((n_sem,)),
        ],
        compiler_params=pltpu.CompilerParams(
            collective_id=0, has_side_effects=True, vmem_limit_bytes=60 * 1024 * 1024
        ),
    )(tokens, upstream, corpus, lengths, owners, w_in, w_out)


def local(tokens, upstream, corpus, lengths, owners, w_in, w_out):
    groups = lax.axis_size("group")
    replicas = lax.axis_size(DP)
    shard_rows = w_in.shape[0]
    local_ff = w_in.shape[1]
    width = shard_rows * groups * replicas
    scale_in = 1.0 / math.sqrt(width)
    scale_out = 1.0 / math.sqrt(local_ff * lax.axis_size("tensor"))
    return fused(tokens, upstream, corpus, lengths, owners, w_in, w_out, scale_in, scale_out)


def solution(mesh):
    torus = Mesh(
        mesh.devices.reshape(mesh.shape["group"], 2, NZ, mesh.shape["tensor"]),
        ("group", "dp_0", "dp_1", "tensor"),
    )
    return jax.shard_map(
        local,
        mesh=torus,
        in_specs=(
            P(DP, None),
            P(DP, None),
            P(DP, None),
            P(DP),
            P(DP),
            P(GROUP_DP, "tensor"),
            P(GROUP_DP, "tensor"),
        ),
        out_specs=(P(GROUP_DP, "tensor"), P(GROUP_DP, "tensor"), P(GROUP_DP, "tensor")),
        check_vma=False,
    )
```

```python
import functools
import math

import jax
import jax.numpy as jnp
from jax import lax
from jax.experimental import pallas as pl
from jax.experimental.pallas import tpu as pltpu
from jax.sharding import Mesh
from jax.sharding import PartitionSpec as P

DP = ("dp_0", "dp_1")
GROUP_DP = ("group", "dp_0", "dp_1")
MESH = pl.DeviceIdType.MESH

LEARN_RATE = 0.5
EPSILON = 1e-06
F32 = jnp.float32
BF16 = jnp.bfloat16
NZ = 8
NT = 8
TURNS = ((1, 1), (1, 0), (0, 1))


def kernel(
    plen,
    scale_in,
    scale_out,
    tokens_ref,
    upstream_ref,
    corpus_ref,
    len_ref,
    owner_ref,
    win_ref,
    wout_ref,
    new_in_ref,
    new_out_ref,
    index_ref,
    tok,
    up,
    cor,
    w_in,
    w_out,
    acc_p,
    acc_d,
    acc_c,
    hid,
    dpre,
    g_in,
    g_out,
    r_in,
    r_out,
    fin,
    land,
    lens_here,
    lens_there,
    pool,
    pool_in,
    square,
    square_in,
    letter,
    letter_in,
    lsem,
    ssem,
    rsem,
):
    g = lax.axis_index("group")
    yh = lax.axis_index("dp_0")
    z = lax.axis_index("dp_1")
    t = lax.axis_index("tensor")
    core = lax.rem(t, 2)
    par = lax.rem(t // 2, 2)
    cut = w_in.shape[-1]
    shard = w_in.shape[-2]

    def cell(dg, dy, dt):
        return (lax.rem(g + dg, 2), lax.rem(yh + dy, 2), z, lax.rem(t + dt, NT))

    def column(dg, dy):
        return cell(dg, dy, 0)

    twin = (g, yh, z, t + 1 - 2 * core)
    right, left = cell(0, 0, 2), cell(0, 0, NT - 2)
    mate, swap = column(1, 1), column(1, 0)
    ring = (
        (g, yh, lax.rem(z + 1, NZ), t),
        (g, yh, lax.rem(z + NZ - 1, NZ), t),
    )
    step_of = (1, -1)

    def at(k):
        return lax.rem(z + k + 2 * NZ, NZ)

    barrier = pltpu.get_barrier_semaphore()
    met = [column(dg, dy) for dg, dy in TURNS] + list(ring) + [twin, right, left]
    met += [cell(0, 0, 4)] + [cell(dg, dy, 4) for dg, dy in TURNS]
    for device in met:
        pl.semaphore_signal(barrier, inc=1, device_id=device, device_id_type=MESH)

    def cols_of(dg, dy):
        q = lax.rem(g + dg, 2) * 2 + lax.rem(yh + dy, 2)
        return pl.ds(pl.multiple_of(q * cut, cut), cut)

    own_cols = cols_of(0, 0)
    groups_of_half = tok.shape[0] // 2
    here = pl.ds(yh * groups_of_half, groups_of_half)
    loads = []
    for k, (src, dst) in enumerate(
        (
            (win_ref.at[:, own_cols], w_in.at[g, yh, z]),
            (wout_ref.at[:, own_cols], w_out.at[g, yh, z]),
            (tokens_ref, tok.at[here]),
            (corpus_ref, cor.at[here]),
            (upstream_ref, up.at[here]),
        )
    ):
        copy = pltpu.make_async_copy(src, dst, lsem.at[k])
        copy.start()
        loads.append(copy)

    passages = len_ref.shape[0]

    def per_passage(ref, shape):
        row = lax.broadcasted_iota(jnp.int32, shape, 0)
        out = jnp.zeros(shape, jnp.int32)
        for i in range(passages):
            out = jnp.where(row == i, ref[i], out)
        return out

    lens_here[...] = per_passage(len_ref, lens_here.shape)

    half_nz = NZ // 2
    pair = z // 2
    e = 1 - 2 * lax.rem(z, 2)
    pairs = (
        None,
        pair,
        lax.rem(pair - e + half_nz, half_nz),
        lax.rem(pair + e + half_nz, half_nz),
        lax.rem(pair + 2, half_nz),
    )

    count = [0]
    sent = []

    def push(src, dst, device):
        k = count[0]
        count[0] += 1
        copy = pltpu.make_async_remote_copy(
            src_ref=src,
            dst_ref=dst,
            send_sem=ssem.at[k],
            recv_sem=rsem.at[k],
            device_id=device,
            device_id_type=MESH,
        )
        copy.start()
        sent.append(copy)
        return copy

    def same(ref, device):
        return push(ref, ref, device)

    pl.semaphore_wait(barrier, len(met))

    weights = ((win_ref, w_in), (wout_ref, w_out))
    first = [[[] for _ in range(2)] for _ in range(2)]
    for a, (src, w) in enumerate(weights):
        for d in range(2):
            first[a][d].append(push(src.at[:, own_cols], w.at[g, yh, z], ring[d]))
    slices = [[], []]
    for a, (src, w) in enumerate(weights):
        for dg, dy in TURNS:
            slices[a].append(push(src.at[:, cols_of(dg, dy)], w.at[g, yh, z], column(dg, dy)))

    def part(half, h, who=core):
        return pl.ds(half * groups_of_half + who * 4 + h * 2, 2)

    there = 1 - yh
    arrays = ((tokens_ref, tok), (upstream_ref, up), (corpus_ref, cor))
    from_mate = []
    for src, buf in arrays:
        given = pl.ds(core * 4 + (1 - g) * 2, 2)
        from_mate.append(push(src.at[given, par], buf.at[part(yh, 1 - g), par], mate))
    lens_copy = push(lens_here, lens_there, mate)
    from_swap = [None] * 3
    from_side = [[] for _ in range(3)]
    from_twin = [[] for _ in range(3)]

    def sideways(k, h):
        buf = arrays[k][1]
        start = there * groups_of_half + core * 4 + h * 2
        from_side[k].append(same(buf.at[pl.ds(start + 1, 1), par], right))
        from_side[k].append(same(buf.at[pl.ds(start, 1), par], left))

    def after_mate(k):
        buf = arrays[k][1]
        from_mate[k].wait_recv()
        from_swap[k] = same(buf.at[part(there, g), par], swap)
        sideways(k, g)
        from_twin[k].append(same(buf.at[part(there, g), par], twin))

    def after_swap(k):
        buf = arrays[k][1]
        from_swap[k].wait_recv()
        sideways(k, 1 - g)
        from_twin[k].append(same(buf.at[part(there, 1 - g), par], twin))

    def after_side(k):
        buf = arrays[k][1]
        for i, h in enumerate((g, 1 - g)):
            from_side[k][2 * i].wait_recv()
            from_side[k][2 * i + 1].wait_recv()
            from_twin[k].append(same(buf.at[part(there, h), 1 - par], twin))

    def after_twin(k):
        for copy in from_twin[k]:
            copy.wait_recv()

    loads[0].wait()
    loads[1].wait()
    for a, (_, w) in enumerate(weights):
        for i, (dg, dy) in enumerate(TURNS):
            slices[a][i].wait_recv()
            block = w.at[lax.rem(g + dg, 2), lax.rem(yh + dy, 2), z]
            for d in range(2):
                first[a][d].append(same(block, ring[d]))

    def send_ring(a, s, d):
        w = weights[a][1]
        o = at(-step_of[d] * (s - 1))
        return same(w.at[:, :, o] if s < 4 else w.at[d, :, o], ring[d])

    def rows_of(x, base, tile, p):
        parts = []
        per = x.shape[1] * x.shape[2]
        for q in range(4):
            at_q = pl.multiple_of(q * NZ * shard + p * 2 * shard, 2 * shard)
            block = x[pl.ds(base, tile // per), :, :, pl.ds(at_q, 2 * shard)]
            parts.append(block.reshape(tile, 2 * shard))
        return jnp.concatenate(parts, axis=1)

    def weight(w, p):
        parts = []
        for q in range(4):
            block = w[q // 2, q % 2, pl.ds(2 * p, 2)]
            parts.append(block.reshape(2 * shard, cut))
        return jnp.concatenate(parts, axis=0)

    def multiply(x, w, acc, half, p, is_first):
        per = x.shape[1] * x.shape[2]
        tile = 256
        rows_half = per * groups_of_half

        def body(m, carry):
            base = half * groups_of_half + m * (tile // per)
            rows = pl.ds(pl.multiple_of(half * rows_half + m * tile, tile), tile)
            part_sum = jnp.dot(rows_of(x, base, tile, p), weight(w, p), preferred_element_type=F32)
            acc[rows, :] = part_sum if is_first else acc[rows, :] + part_sum
            return carry

        lax.fori_loop(0, rows_half // tile, body, 0)

    got = [[[None] * 2 for _ in range(5)] for _ in range(2)]
    after_mate(0)
    for s in range(1, 5):
        for a in range(2):
            for d in range(2):
                if s == 1:
                    for copy in first[a][d]:
                        copy.wait_recv()
                else:
                    got[a][s][d].wait_recv()
                if s < 4:
                    got[a][s + 1][d] = send_ring(a, s + 1, d)
        if s == 1:
            after_swap(0)
            after_mate(1)
            loads[2].wait()
            loads[4].wait()
        elif s == 2:
            after_side(0)
            after_swap(1)
            after_mate(2)
        elif s == 3:
            after_side(1)
            after_swap(2)
            after_twin(0)
        multiply(tok, w_in, acc_p, yh, pairs[s], s == 1)
        multiply(up, w_out, acc_d, yh, pairs[s], s == 1)
        if s == 3:
            for k in range(1, 4):
                multiply(tok, w_in, acc_p, there, pairs[k], k == 1)
    after_side(2)
    multiply(tok, w_in, acc_p, there, pairs[4], False)
    after_twin(1)
    for k in range(1, 5):
        multiply(up, w_out, acc_d, there, pairs[k], k == 1)

    root = math.sqrt(2.0 / math.pi)

    def gelu_parts(p):
        th = jnp.tanh(root * (p + 0.044715 * (p * p * p)))
        return 0.5 * (1.0 + th), th

    slab = 64

    def activate(m, carry):
        rows = pl.ds(pl.multiple_of(m * slab, slab), slab)
        p = acc_p[rows, :] * scale_in
        dh = acc_d[rows, :] * scale_out
        cdf, th = gelu_parts(p)
        hid[rows, :] = (p * cdf).astype(BF16)
        slope = cdf + (0.5 * root) * p * (1.0 - th * th) * (1.0 + (3 * 0.044715) * (p * p))
        dpre[rows, :] = (dh * slope).astype(BF16)
        return carry

    n_tok = acc_p.shape[0]
    lax.fori_loop(0, n_tok // slab, activate, 0)

    def gradient(x, y, out, scale, p):
        def body(gg, carry):
            parts = []
            for yy in range(2):
                at_q = pl.multiple_of((gg * 2 + yy) * NZ * shard + p * 2 * shard, 2 * shard)
                block = x[:, :, :, pl.ds(at_q, 2 * shard)]
                parts.append(block.reshape(n_tok, 2 * shard))
            both = lax.dot_general(
                jnp.concatenate(parts, axis=1),
                y[...],
                (((0,), (0,)), ((), ())),
                preferred_element_type=F32,
            )
            both = (both * scale).astype(BF16).reshape(2, 2, shard, cut)
            for yy in range(2):
                out[gg, yy, pl.ds(2 * p, 2)] = both[yy]
            return carry

        lax.fori_loop(0, 2, body, 0)

    def add(a, b):
        return (a.astype(F32) + b.astype(F32)).astype(BF16)

    back = [[[None] * 2 for _ in range(5)] for _ in range(2)]

    def give_back(a, s, d):
        grad, arrived = ((g_in, r_in), (g_out, r_out))[a]
        o = at(step_of[d] * (5 - s))
        if s == 1:
            back[a][1][d] = push(grad.at[d, :, o], arrived.at[d, 0, d], ring[d])
            return
        back[a][s - 1][d].wait_recv()
        if s == 2:
            for yy in range(2):
                grad[d, yy, o] = add(grad[d, yy, o], arrived[d, 0, d, yy])
        else:
            for gg in range(2):
                for yy in range(2):
                    grad[gg, yy, o] = add(grad[gg, yy, o], arrived[d, s - 2, gg, yy])
        back[a][s][d] = push(grad.at[:, :, o], arrived.at[d, s - 1], ring[d])

    feat = pool.shape[-1]
    rows_c = acc_c.shape[0] // 2
    mine = pl.ds(pl.multiple_of(t * feat, feat), feat)

    def pool_rows():
        after_twin(2)
        lens_copy.wait_recv()
        loads[3].wait()
        for half in (yh, there):
            for k in range(1, 5):
                multiply(cor, w_in, acc_c, half, pairs[k], k == 1)
        shape = (passages, rows_c)
        row = lax.broadcasted_iota(jnp.int32, shape, 0)
        col = lax.broadcasted_iota(jnp.int32, shape, 1)
        stack = []
        for half, lens in ((yh, lens_here), (there, lens_there)):
            span = pl.ds(pl.multiple_of(half * rows_c, rows_c), rows_c)
            pre = acc_c[span, :] * scale_in
            cdf, _ = gelu_parts(pre)
            ch = (pre * cdf).astype(BF16)
            stop = row * plen + jnp.broadcast_to(lens[:, :1], shape)
            inside = jnp.logical_and(col >= row * plen, col < stop)
            live = jnp.where(inside, 1.0, 0.0).astype(BF16)
            if not stack:
                x = cor[pl.ds(yh * groups_of_half, groups_of_half), :, :, mine]
                base = jnp.dot(live, x.reshape(rows_c, feat), preferred_element_type=F32)
            ph = jnp.dot(live, ch, preferred_element_type=F32)
            hi = ph.astype(BF16).astype(F32)
            stack += [hi, ph - hi]
        hl = jnp.concatenate(stack, axis=0).astype(BF16)

        def branch(q, carry):
            w = w_out[q // 2, lax.rem(q, 2)].reshape(NZ * shard, cut)
            both = lax.dot_general(hl, w, (((1,), (1,)), ((), ())), preferred_element_type=F32)
            both = both * scale_out
            n = NZ * shard // feat
            for i in range(2):
                rows = both[2 * i * passages : (2 * i + 1) * passages]
                rows = rows + both[(2 * i + 1) * passages : (2 * i + 2) * passages]
                for k in range(n):
                    pool[i, q * n + k] = rows[:, k * feat : (k + 1) * feat]
            return carry

        lax.fori_loop(0, 4, branch, 0)
        copies = []
        for dy in range(2):
            for dg in range(2):
                for dt in range(NT):
                    if dy or dg or dt:
                        src = pool.at[dy, lax.rem(t + dt, NT)]
                        slot = pool_in.at[(dy * 2 + dg) * NT + dt]
                        copies.append(push(src, slot, cell(dg, dy, dt)))
        return base, copies

    def square_rows(base, copies):
        total = base + pool[0, t]
        for copy in copies:
            copy.wait_recv()
        for k in range(1, 4 * NT):
            total = total + pool_in[k]
        lens = jnp.broadcast_to(lens_here[:, :1], total.shape)
        pooled = total * (1.0 / lens.astype(F32))
        own_square = jnp.sum(pooled * pooled, axis=1, keepdims=True)
        square[...] = jnp.broadcast_to(own_square, square.shape)
        copies = [push(square, square_in.at[dt], cell(0, 0, dt)) for dt in range(1, NT)]
        return pooled, own_square, copies

    def post_rows(pooled, own_square, copies):
        for copy in copies:
            copy.wait_recv()
        total = own_square
        for dt in range(1, NT):
            total = total + square_in[dt][:, :1]
        rows = pooled * lax.rsqrt(total / (NT * feat) + EPSILON)
        owners = per_passage(owner_ref, rows.shape)
        copies = []
        for a in range(2):
            for b in range(NZ):
                to_yh, to_z = lax.rem(yh + a, 2), at(b)
                owner = (g * 2 + to_yh) * NZ + to_z
                row = jnp.sum(jnp.where(owners == owner, rows, 0.0), axis=0, keepdims=True)
                if a or b:
                    letter[a * NZ + b] = row
                    copies.append(
                        push(
                            letter.at[a * NZ + b],
                            letter_in.at[yh * NZ + z],
                            (g, to_yh, to_z, t),
                        )
                    )
                else:
                    letter_in[yh * NZ + z] = row
        return copies

    def read_rows(copies):
        for copy in copies:
            copy.wait_recv()
        row = lax.broadcasted_iota(jnp.int32, index_ref.shape, 0)
        out = jnp.zeros(index_ref.shape, F32)
        for d in range(2 * NZ):
            out = jnp.where(row == d, jnp.broadcast_to(letter_in[d], out.shape), out)
        index_ref[...] = out.astype(BF16)

    stage = None
    for s in range(1, 5):
        p = pairs[5 - s]
        gradient(tok, dpre, g_in, scale_in, p)
        for d in range(2):
            give_back(0, s, d)
        gradient(up, hid, g_out, scale_out, p)
        for d in range(2):
            give_back(1, s, d)
        if s == 1:
            stage = pool_rows()
        elif s == 2:
            stage = square_rows(*stage)
        elif s == 3:
            stage = post_rows(*stage)

    home = [[], []]
    outs = (new_in_ref, new_out_ref)
    sums = ((g_in, r_in, w_in), (g_out, r_out, w_out))
    for a, (grad, arrived, w) in enumerate(sums):
        for d in range(2):
            back[a][4][d].wait_recv()
        for i, (dg, dy) in enumerate(TURNS + ((0, 0),)):
            gg, yy = lax.rem(g + dg, 2), lax.rem(yh + dy, 2)
            total = (
                grad[gg, yy, z].astype(F32)
                + arrived[0, 3, gg, yy].astype(F32)
                + arrived[1, 3, gg, yy].astype(F32)
            )
            new = (w[gg, yy, z].astype(F32) - LEARN_RATE * total).astype(BF16)
            if dg or dy:
                fin[a, i] = new
                home[a].append(push(fin.at[a, i], land.at[a, i], column(dg, dy)))
            else:
                outs[a][:, own_cols] = new
    read_rows(stage)
    for a in range(2):
        for i, (dg, dy) in enumerate(TURNS):
            home[a][i].wait_recv()
            outs[a][:, cols_of(dg, dy)] = land[a, i]
    for copy in sent:
        copy.wait_send()


def fused(tokens, upstream, corpus, lengths, owners, w_in, w_out, scale_in, scale_out):
    shard, local_ff = w_in.shape
    cut = local_ff // 4
    n_tok, width = tokens.shape
    n_corpus = corpus.shape[0]
    npass = lengths.shape[0]
    full = (2, 2, NZ, shard, cut)
    n_sem = 160
    feat = width // NT
    rows_t, rows_c = n_tok // 16, n_corpus // 16
    any_spec = pl.BlockSpec(memory_space=pl.ANY)
    vmem_spec = pl.BlockSpec(memory_space=pltpu.VMEM)
    smem_spec = pl.BlockSpec(memory_space=pltpu.SMEM)
    return pl.pallas_call(
        functools.partial(kernel, n_corpus // npass, scale_in, scale_out),
        out_shape=(
            jax.ShapeDtypeStruct((shard, local_ff), BF16),
            jax.ShapeDtypeStruct((shard, local_ff), BF16),
            jax.ShapeDtypeStruct((2 * NZ, feat), BF16),
        ),
        in_specs=[any_spec, any_spec, any_spec, smem_spec, smem_spec, any_spec, any_spec],
        out_specs=(vmem_spec, vmem_spec, vmem_spec),
        scratch_shapes=[
            pltpu.VMEM((16, 2, rows_t, width), BF16),
            pltpu.VMEM((16, 2, rows_t, width), BF16),
            pltpu.VMEM((16, 2, rows_c, width), BF16),
            pltpu.VMEM(full, BF16),
            pltpu.VMEM(full, BF16),
            pltpu.VMEM((2 * n_tok, cut), F32),
            pltpu.VMEM((2 * n_tok, cut), F32),
            pltpu.VMEM((2 * n_corpus, cut), F32),
            pltpu.VMEM((2 * n_tok, cut), BF16),
            pltpu.VMEM((2 * n_tok, cut), BF16),
            pltpu.VMEM(full, BF16),
            pltpu.VMEM(full, BF16),
            pltpu.VMEM((2, 4, 2, 2, shard, cut), BF16),
            pltpu.VMEM((2, 4, 2, 2, shard, cut), BF16),
            pltpu.VMEM((2, 3, shard, cut), BF16),
            pltpu.VMEM((2, 3, shard, cut), BF16),
            pltpu.VMEM((npass, 128), jnp.int32),
            pltpu.VMEM((npass, 128), jnp.int32),
            pltpu.VMEM((2, NT, npass, feat), F32),
            pltpu.VMEM((4 * NT, npass, feat), F32),
            pltpu.VMEM((npass, 128), F32),
            pltpu.VMEM((NT, npass, 128), F32),
            pltpu.VMEM((2 * NZ, 1, feat), F32),
            pltpu.VMEM((2 * NZ, 1, feat), F32),
            pltpu.SemaphoreType.DMA((5,)),
            pltpu.SemaphoreType.DMA((n_sem,)),
            pltpu.SemaphoreType.DMA((n_sem,)),
        ],
        compiler_params=pltpu.CompilerParams(
            collective_id=0, has_side_effects=True, vmem_limit_bytes=60 * 1024 * 1024
        ),
    )(
        tokens.reshape(8, 2, rows_t, width),
        upstream.reshape(8, 2, rows_t, width),
        corpus.reshape(8, 2, rows_c, width),
        lengths,
        owners,
        w_in,
        w_out,
    )


def local(tokens, upstream, corpus, lengths, owners, w_in, w_out):
    width = w_in.shape[0] * lax.axis_size(GROUP_DP)
    hidden_units = w_in.shape[1] * lax.axis_size("tensor")
    scale_in = 1.0 / math.sqrt(width)
    scale_out = 1.0 / math.sqrt(hidden_units)
    return fused(tokens, upstream, corpus, lengths, owners, w_in, w_out, scale_in, scale_out)


def solution(mesh):
    torus = Mesh(
        mesh.devices.reshape(mesh.shape["group"], 2, NZ, mesh.shape["tensor"]),
        ("group", "dp_0", "dp_1", "tensor"),
    )
    return jax.shard_map(
        local,
        mesh=torus,
        in_specs=(
            P(DP, None),
            P(DP, None),
            P(DP, None),
            P(DP),
            P(DP),
            P(GROUP_DP, "tensor"),
            P(GROUP_DP, "tensor"),
        ),
        out_specs=(P(GROUP_DP, "tensor"), P(GROUP_DP, "tensor"), P(GROUP_DP, "tensor")),
        check_vma=False,
    )
```

```python
import functools
import math

import jax
import jax.numpy as jnp
from jax import lax
from jax.experimental import pallas as pl
from jax.experimental.pallas import tpu as pltpu
from jax.sharding import Mesh
from jax.sharding import PartitionSpec as P

DP = ("dp_0", "dp_1")
GROUP_DP = ("group", "dp_0", "dp_1")
MESH = pl.DeviceIdType.MESH

LEARN_RATE = 0.5
EPSILON = 1e-06
F32 = jnp.float32
BF16 = jnp.bfloat16
NZ = 8
NT = 8
N_SEM = 91
TURNS = ((1, 1), (1, 0), (0, 1))


def kernel(
    plen,
    scale_in,
    scale_out,
    tokens_ref,
    upstream_ref,
    corpus_ref,
    len_hbm,
    owner_hbm,
    win_ref,
    wout_ref,
    new_in_ref,
    new_out_ref,
    index_ref,
    tok,
    up,
    cor,
    w_in,
    w_out,
    acc_p,
    acc_d,
    acc_c,
    hid,
    dpre,
    g_in,
    g_out,
    r_in,
    r_out,
    fin,
    lens_here,
    lens_there,
    pool,
    pool_in,
    square,
    square_in,
    letter,
    letter_in,
    len_ref,
    owner_ref,
    lsem,
    ssem,
    rsem,
):
    g = lax.axis_index("group")
    yh = lax.axis_index("dp_0")
    z = lax.axis_index("dp_1")
    t = lax.axis_index("tensor")
    core = lax.rem(t, 2)
    par = lax.rem(t // 2, 2)
    cut = w_in.shape[-1]
    shard = w_in.shape[-2]

    def cell(dg, dy, dt):
        return (lax.rem(g + dg, 2), lax.rem(yh + dy, 2), z, lax.rem(t + dt, NT))

    def column(dg, dy):
        return cell(dg, dy, 0)

    twin = (g, yh, z, t + 1 - 2 * core)
    right, left = cell(0, 0, 2), cell(0, 0, NT - 2)
    mate, swap = column(1, 1), column(1, 0)
    ring = (
        (g, yh, lax.rem(z + 1, NZ), t),
        (g, yh, lax.rem(z + NZ - 1, NZ), t),
    )
    step_of = (1, -1)

    def at(k):
        return lax.rem(z + k + 2 * NZ, NZ)

    barrier = pltpu.get_barrier_semaphore()
    met = [column(dg, dy) for dg, dy in TURNS] + list(ring) + [twin, right, left]
    met += [cell(0, 0, 4)] + [cell(dg, dy, 4) for dg, dy in TURNS]
    for device in met:
        pl.semaphore_signal(barrier, inc=1, device_id=device, device_id_type=MESH)

    def cols_of(dg, dy):
        q = lax.rem(g + dg, 2) * 2 + lax.rem(yh + dy, 2)
        return pl.ds(pl.multiple_of(q * cut, cut), cut)

    own_cols = cols_of(0, 0)
    groups_of_half = tok.shape[0] // 2
    here = pl.ds(yh * groups_of_half, groups_of_half)
    loads = []

    def load(src, dst):
        copy = pltpu.make_async_copy(src, dst, lsem.at[len(loads)])
        copy.start()
        loads.append(copy)
        return copy

    load_lens = load(len_hbm, len_ref)
    load_owners = load(owner_hbm, owner_ref)
    load_in = load(win_ref.at[:, own_cols], w_in.at[g, yh, z])
    load_out = load(wout_ref.at[:, own_cols], w_out.at[g, yh, z])
    load_tok = load(tokens_ref, tok.at[here])
    load_up = load(upstream_ref, up.at[here])
    load_cor = load(corpus_ref, cor.at[here])

    passages = len_ref.shape[0]

    def per_passage(ref, shape):
        row = lax.broadcasted_iota(jnp.int32, shape, 0)
        out = jnp.zeros(shape, jnp.int32)
        for i in range(passages):
            out = jnp.where(row == i, ref[i], out)
        return out

    half_nz = NZ // 2
    pair = z // 2
    e = 1 - 2 * lax.rem(z, 2)
    pairs = (
        None,
        pair,
        lax.rem(pair - e + half_nz, half_nz),
        lax.rem(pair + e + half_nz, half_nz),
        lax.rem(pair + 2, half_nz),
    )

    count = [0]

    shared = {}
    families = {}

    def push(src, dst, device, family, key=None):
        k = shared.get(key)
        if k is None:
            k = count[0]
            count[0] += 1
            if key is not None:
                shared[key] = k
        copy = pltpu.make_async_remote_copy(
            src_ref=src,
            dst_ref=dst,
            send_sem=ssem.at[families.setdefault(family, len(families))],
            recv_sem=rsem.at[k],
            device_id=device,
            device_id_type=MESH,
        )
        copy.start()
        return copy

    def same(ref, device, family, key=None):
        return push(ref, ref, device, family, key)

    def whole(ref, family, key):
        return pltpu.make_async_remote_copy(
            src_ref=ref,
            dst_ref=ref,
            send_sem=ssem.at[families[family]],
            recv_sem=rsem.at[shared[key] if key is not None else 0],
            device_id=twin,
            device_id_type=MESH,
        )

    pl.semaphore_wait(barrier, len(met))

    weights = ((win_ref, w_in), (wout_ref, w_out))
    slices = [[], []]

    def open_ring(a):
        src, w = weights[a]
        for d in range(2):
            push(src.at[:, own_cols], w.at[g, yh, z], ring[d], (0, a), (0, a, d))

    def open_column(a):
        src, w = weights[a]
        for dg, dy in TURNS:
            slices[a].append(
                push(src.at[:, cols_of(dg, dy)], w.at[g, yh, z], column(dg, dy), (0, a))
            )

    def slice_arrives(a, i):
        dg, dy = TURNS[i]
        slices[a][i].wait_recv()
        block = weights[a][1].at[lax.rem(g + dg, 2), lax.rem(yh + dy, 2), z]
        for d in range(2):
            same(block, ring[d], (0, a), (0, a, d))

    ahead = {}

    def ring_arrives(a, s):
        w = weights[a][1]
        for h in range(2):
            for d in range(2):
                if s == 1:
                    if h == 0:
                        whole(w.at[:, :, at(-step_of[d])], (0, a), (0, a, d)).wait_recv()
                elif s < 4 or h == d:
                    ahead[a, s, h, d].wait_recv()
                if s < 3 or (s == 3 and h == d):
                    o = at(-step_of[d] * s)
                    ahead[a, s + 1, h, d] = same(w.at[h, :, o], ring[d], (0, a))

    there = 1 - yh
    arrays = ((tokens_ref, tok), (upstream_ref, up), (corpus_ref, cor))
    from_mate, from_swap, from_side = {}, {}, {}

    def spot(half, h, i, lane):
        return pl.ds(half * groups_of_half + core * 4 + h * 2 + i, 1), lane

    def open_part(k, i):
        src, buf = arrays[k]
        given = src.at[pl.ds(core * 4 + (1 - g) * 2 + i, 1), par]
        from_mate[k, i] = push(given, buf.at[spot(yh, 1 - g, i, par)], mate, (1, k))

    def pass_on(k, i, other):
        block = arrays[k][1].at[spot(there, 1 - g if other else g, i, par)]
        from_side[k, i, other] = same(block, right if i else left, (1, k))
        same(block, twin, (1, k), (1, k))

    def mate_arrives(k, i):
        from_mate[k, i].wait_recv()
        from_swap[k, i] = same(arrays[k][1].at[spot(there, g, i, par)], swap, (1, k))
        pass_on(k, i, 0)

    def swap_arrives(k, i):
        from_swap[k, i].wait_recv()
        pass_on(k, i, 1)

    def side_arrives(k, i, other):
        from_side[k, i, other].wait_recv()
        block = arrays[k][1].at[spot(there, 1 - g if other else g, i, 1 - par)]
        same(block, twin, (1, k), (1, k))

    def after_twin(k):
        start = there * groups_of_half + (1 - core) * 4
        whole(arrays[k][1].at[pl.ds(start, 4)], (1, k), (1, k)).wait_recv()

    def rows_of(x, base, tile, p):
        parts = []
        per = x.shape[1] * x.shape[2]
        for q in range(4):
            at_q = pl.multiple_of(q * NZ * shard + p * 2 * shard, 2 * shard)
            block = x[pl.ds(base, tile // per), :, :, pl.ds(at_q, 2 * shard)]
            parts.append(block.reshape(tile, 2 * shard))
        return jnp.concatenate(parts, axis=1)

    def weight(w, p):
        parts = []
        for q in range(4):
            block = w[q // 2, q % 2, pl.ds(2 * p, 2)]
            parts.append(block.reshape(2 * shard, cut))
        return jnp.concatenate(parts, axis=0)

    def multiply(x, w, acc, half, p, is_first):
        per = x.shape[1] * x.shape[2]
        tile = min(512, per * groups_of_half)
        rows_half = per * groups_of_half

        def body(m, carry):
            base = half * groups_of_half + m * (tile // per)
            rows = pl.ds(pl.multiple_of(half * rows_half + m * tile, tile), tile)
            part_sum = jnp.dot(rows_of(x, base, tile, p), weight(w, p), preferred_element_type=F32)
            acc[rows, :] = part_sum if is_first else acc[rows, :] + part_sum
            return carry

        lax.fori_loop(0, rows_half // tile, body, 0)

    root = math.sqrt(2.0 / math.pi)

    def gelu_parts(p):
        th = jnp.tanh(root * (p + 0.044715 * (p * p * p)))
        return 0.5 * (1.0 + th), th

    slab = 64
    n_tok = acc_p.shape[0]

    def activate():
        def body(m, carry):
            rows = pl.ds(pl.multiple_of(m * slab, slab), slab)
            p = acc_p[rows, :] * scale_in
            cdf, th = gelu_parts(p)
            hid[rows, :] = (p * cdf).astype(BF16)
            acc_p[rows, :] = cdf + (0.5 * root) * p * (1.0 - th * th) * (
                1.0 + (3 * 0.044715) * (p * p)
            )
            return carry

        lax.fori_loop(0, n_tok // slab, body, 0)

    def slope_rows():
        def body(m, carry):
            rows = pl.ds(pl.multiple_of(m * slab, slab), slab)
            dpre[rows, :] = (acc_d[rows, :] * scale_out * acc_p[rows, :]).astype(BF16)
            return carry

        lax.fori_loop(0, n_tok // slab, body, 0)

    open_ring(0)
    open_column(0)
    open_ring(1)
    open_part(0, 0)
    open_column(1)
    open_part(0, 1)
    for k in (1, 2):
        for i in range(2):
            open_part(k, i)
    load_in.wait()
    load_out.wait()
    load_lens.wait()
    load_owners.wait()
    lens_here[...] = per_passage(len_ref, lens_here.shape)
    lens_copy = push(lens_here, lens_there, mate, (2,))
    load_tok.wait()
    load_up.wait()
    events = []

    def event(time, what, *args):
        events.append((time, len(events), what, args))

    for a, at_slice, at_ring in (
        (0, (3.4, 3.5, 3.6), (8.0, 12.5, 17.0, 20.5)),
        (1, (9.0, 9.1, 9.2), (13.5, 18.5)),
    ):
        for i, time in enumerate(at_slice):
            event(time, slice_arrives, a, i)
        for i, time in enumerate(at_ring):
            event(time, ring_arrives, a, i + 1)
            x, w, acc = ((tok, w_in, acc_p), (up, w_out, acc_d))[a]
            event(time + 0.1, multiply, x, w, acc, yh, pairs[i + 1], i == 0)
    hop = 4.5
    for k, times in enumerate(((7.0, 10.5), (13.2, 15.6), (18.7, 19.7))):
        for i, time in enumerate(times):
            event(time, mate_arrives, k, i)
            if k < 2:
                event(time + hop, swap_arrives, k, i)
                event(time + hop + 0.1, side_arrives, k, i, 0)
    for i, time in enumerate((16.0, 19.5)):
        event(time, side_arrives, 0, i, 1)
    event(21.9, side_arrives, 1, 0, 1)
    event(22.0, after_twin, 0)
    for i in range(1, 4):
        event(22.1, multiply, tok, w_in, acc_p, there, pairs[i], i == 1)
    event(22.15, ring_arrives, 1, 3)
    event(22.2, side_arrives, 1, 1, 1)
    event(22.3, multiply, tok, w_in, acc_p, there, pairs[4], False)
    event(22.4, activate)
    for _, _, what, args in sorted(events, key=lambda x: x[:2]):
        what(*args)

    def gradient(x, y, out, scale, p):
        def body(gg, carry):
            parts = []
            for yy in range(2):
                at_q = pl.multiple_of((gg * 2 + yy) * NZ * shard + p * 2 * shard, 2 * shard)
                block = x[:, :, :, pl.ds(at_q, 2 * shard)]
                parts.append(block.reshape(n_tok, 2 * shard))
            both = lax.dot_general(
                jnp.concatenate(parts, axis=1),
                y[...],
                (((0,), (0,)), ((), ())),
                preferred_element_type=F32,
            )
            both = (both * scale).astype(BF16).reshape(2, 2, shard, cut)
            for yy in range(2):
                out[gg, yy, pl.ds(2 * p, 2)] = both[yy]
            return carry

        lax.fori_loop(0, 2, body, 0)

    def add(a, b):
        return (a.astype(F32) + b.astype(F32)).astype(BF16)

    back = {}

    def give_back(a, s):
        grad, arrived = ((g_in, r_in), (g_out, r_out))[a]
        for h in range(2):
            for d in range(2):
                o = at(step_of[d] * (5 - s))
                if s == 1 and h != d:
                    continue
                if s > 2 or (s == 2 and h == d):
                    back[a, s - 1, h, d].wait_recv()
                    for yy in range(2):
                        grad[h, yy, o] = add(grad[h, yy, o], arrived[d, s - 2, h, yy])
                back[a, s, h, d] = push(grad.at[h, :, o], arrived.at[d, s - 1, h], ring[d], (3, a))

    feat = pool.shape[-1]
    rows_c = acc_c.shape[0] // 2
    mine = pl.ds(pl.multiple_of(t * feat, feat), feat)

    def pool_rows():
        after_twin(2)
        lens_copy.wait_recv()
        load_cor.wait()
        for half in (yh, there):
            for k in range(1, 5):
                multiply(cor, w_in, acc_c, half, pairs[k], k == 1)
        shape = (passages, rows_c)
        row = lax.broadcasted_iota(jnp.int32, shape, 0)
        col = lax.broadcasted_iota(jnp.int32, shape, 1)
        stack = []
        for half, lens in ((yh, lens_here), (there, lens_there)):
            span = pl.ds(pl.multiple_of(half * rows_c, rows_c), rows_c)
            pre = acc_c[span, :] * scale_in
            cdf, _ = gelu_parts(pre)
            ch = (pre * cdf).astype(BF16)
            stop = row * plen + jnp.broadcast_to(lens[:, :1], shape)
            inside = jnp.logical_and(col >= row * plen, col < stop)
            live = jnp.where(inside, 1.0, 0.0).astype(BF16)
            if not stack:
                x = cor[pl.ds(yh * groups_of_half, groups_of_half), :, :, mine]
                base = jnp.dot(live, x.reshape(rows_c, feat), preferred_element_type=F32)
            ph = jnp.dot(live, ch, preferred_element_type=F32)
            hi = ph.astype(BF16).astype(F32)
            stack += [hi, ph - hi]
        hl = jnp.concatenate(stack, axis=0).astype(BF16)

        def branch(q, carry):
            w = w_out[q // 2, lax.rem(q, 2)].reshape(NZ * shard, cut)
            both = lax.dot_general(hl, w, (((1,), (1,)), ((), ())), preferred_element_type=F32)
            both = both * scale_out
            n = NZ * shard // feat
            for i in range(2):
                rows = both[2 * i * passages : (2 * i + 1) * passages]
                rows = rows + both[(2 * i + 1) * passages : (2 * i + 2) * passages]
                for k in range(n):
                    pool[i, q * n + k] = rows[:, k * feat : (k + 1) * feat]
            return carry

        lax.fori_loop(0, 4, branch, 0)
        for dy in range(2):
            for dg in range(2):
                for dt in range(NT):
                    if dy or dg or dt:
                        src = pool.at[dy, lax.rem(t + dt, NT)]
                        slot = pool_in.at[(dy * 2 + dg) * NT + dt]
                        push(src, slot, cell(dg, dy, dt), (4,), (4,))
        return (base,)

    def square_rows(base):
        total = base + pool[0, t]
        whole(pool_in.at[pl.ds(1, 4 * NT - 1)], (4,), (4,)).wait_recv()
        for k in range(1, 4 * NT):
            total = total + pool_in[k]
        lens = jnp.broadcast_to(lens_here[:, :1], total.shape)
        pooled = total * (1.0 / lens.astype(F32))
        own_square = jnp.sum(pooled * pooled, axis=1, keepdims=True)
        square[...] = jnp.broadcast_to(own_square, square.shape)
        for dt in range(1, NT):
            push(square, square_in.at[dt], cell(0, 0, dt), (5,), (5,))
        return pooled, own_square

    def post_rows(pooled, own_square):
        whole(square_in.at[pl.ds(1, NT - 1)], (5,), (5,)).wait_recv()
        total = own_square
        for dt in range(1, NT):
            total = total + square_in[dt][:, :1]
        rows = pooled * lax.rsqrt(total / (NT * feat) + EPSILON)
        owners = per_passage(owner_ref, rows.shape)
        for a in range(2):
            for b in range(NZ):
                to_yh, to_z = lax.rem(yh + a, 2), at(b)
                owner = (g * 2 + to_yh) * NZ + to_z
                row = jnp.sum(jnp.where(owners == owner, rows, 0.0), axis=0, keepdims=True)
                if a or b:
                    letter[a * NZ + b] = row
                    push(
                        letter.at[a * NZ + b],
                        letter_in.at[yh * NZ + z],
                        (g, to_yh, to_z, t),
                        (6,),
                        (6,),
                    )
                else:
                    letter_in[yh * NZ + z] = row

    def read_rows():
        whole(letter_in.at[pl.ds(0, 2 * NZ - 1)], (6,), (6,)).wait_recv()
        row = lax.broadcasted_iota(jnp.int32, index_ref.shape, 0)
        out = jnp.zeros(index_ref.shape, F32)
        for d in range(2 * NZ):
            out = jnp.where(row == d, jnp.broadcast_to(letter_in[d], out.shape), out)
        index_ref[...] = out.astype(BF16)

    outs = (new_in_ref, new_out_ref)
    sums = ((g_in, r_in, w_in), (g_out, r_out, w_out))

    def settle(a):
        grad, arrived, w = sums[a]
        for h in range(2):
            for d in range(2):
                back[a, 4, h, d].wait_recv()
        for i, (dg, dy) in enumerate(TURNS + ((0, 0),)):
            gg, yy = lax.rem(g + dg, 2), lax.rem(yh + dy, 2)
            total = (
                grad[gg, yy, z].astype(F32)
                + arrived[0, 3, gg, yy].astype(F32)
                + arrived[1, 3, gg, yy].astype(F32)
            )
            fin[a, i] = (w[gg, yy, z].astype(F32) - LEARN_RATE * total).astype(BF16)
            target = outs[a].at[:, own_cols]
            if dg or dy:
                push(fin.at[a, i], target, column(dg, dy), (7, a), (7, a))
            else:
                load(fin.at[a, i], target)

    def grad_out(j):
        gradient(up, hid, g_out, scale_out, pairs[j])

    def grad_in(j):
        gradient(tok, dpre, g_in, scale_in, pairs[j])

    after_twin(1)
    grad_out(4)
    give_back(1, 1)
    for i in range(2):
        swap_arrives(2, i)
        side_arrives(2, i, 0)
    grad_out(3)
    multiply(up, w_out, acc_d, yh, pairs[3], False)
    for k in range(1, 4):
        multiply(up, w_out, acc_d, there, pairs[k], k == 1)
    give_back(1, 2)
    ring_arrives(1, 4)
    for half in (yh, there):
        multiply(up, w_out, acc_d, half, pairs[4], False)
    slope_rows()
    grad_in(4)
    give_back(0, 1)
    for i in range(2):
        side_arrives(2, i, 1)
    grad_out(2)
    stage = pool_rows()
    give_back(1, 3)
    grad_in(3)
    give_back(0, 2)
    grad_out(1)
    give_back(1, 4)
    grad_in(2)
    give_back(0, 3)
    stage = square_rows(*stage)
    grad_in(1)
    give_back(0, 4)
    stage = post_rows(*stage)
    settle(1)
    settle(0)
    read_rows()
    for a in range(2):
        whole(outs[a].at[:, pl.ds(0, 3 * cut)], (7, a), (7, a)).wait_recv()
    for copy in loads[7:]:
        copy.wait()
    covers = [((0, 0), acc_p.at[pl.ds(0, 31 * n_tok // 32)])]
    covers += [((0, 1), acc_d.at[pl.ds(0, 31 * n_tok // 32)])]
    covers += [((1, k), arrays[k][1].at[pl.ds(0, groups_of_half)]) for k in range(3)]
    covers += [((2,), lens_here), ((4,), pool_in.at[pl.ds(1, 4 * NT - 1)])]
    covers += [((3, a), sums[a][0].at[:, :, pl.ds(0, NZ - 1)]) for a in range(2)]
    covers += [((5,), square_in.at[pl.ds(1, NT - 1)]), ((6,), letter_in.at[pl.ds(0, 2 * NZ - 1)])]
    covers += [((7, a), fin.at[a, pl.ds(0, 3)]) for a in range(2)]
    for family, ref in covers:
        whole(ref, family, None).wait_send()


def pass_through(*refs):
    n = len(refs) // 3
    sources, results, held = refs[:n], refs[n : 2 * n], refs[2 * n : 3 * n]
    sems = refs[3 * n]
    taken = []
    for k in range(n):
        copy = pltpu.make_async_copy(sources[k], held[k], sems.at[k])
        copy.start()
        taken.append(copy)
    given = []
    for k in range(n):
        taken[k].wait()
        copy = pltpu.make_async_copy(held[k], results[k], sems.at[n + k])
        copy.start()
        given.append(copy)
    for copy in given:
        copy.wait()


def handed_over(*arrays):
    any_spec = pl.BlockSpec(memory_space=pl.ANY)
    return pl.pallas_call(
        pass_through,
        out_shape=tuple(jax.ShapeDtypeStruct(x.shape, x.dtype) for x in arrays),
        in_specs=[any_spec] * len(arrays),
        out_specs=(any_spec,) * len(arrays),
        scratch_shapes=[pltpu.VMEM(x.shape, x.dtype) for x in arrays]
        + [pltpu.SemaphoreType.DMA((2 * len(arrays),))],
    )(*arrays)


def fused(tokens, upstream, corpus, lengths, owners, w_in, w_out, scale_in, scale_out):
    shard, local_ff = w_in.shape
    cut = local_ff // 4
    n_tok, width = tokens.shape
    n_corpus = corpus.shape[0]
    npass = lengths.shape[0]
    full = (2, 2, NZ, shard, cut)
    n_sem = N_SEM
    feat = width // NT
    rows_t, rows_c = n_tok // 16, n_corpus // 16
    any_spec = pl.BlockSpec(memory_space=pl.ANY)
    vmem_spec = pl.BlockSpec(memory_space=pltpu.VMEM)
    return pl.pallas_call(
        functools.partial(kernel, n_corpus // npass, scale_in, scale_out),
        out_shape=(
            jax.ShapeDtypeStruct((shard, local_ff), BF16),
            jax.ShapeDtypeStruct((shard, local_ff), BF16),
            jax.ShapeDtypeStruct((2 * NZ, feat), BF16),
        ),
        in_specs=[any_spec] * 7,
        out_specs=(any_spec, any_spec, vmem_spec),
        scratch_shapes=[
            pltpu.VMEM((16, 2, rows_t, width), BF16),
            pltpu.VMEM((16, 2, rows_t, width), BF16),
            pltpu.VMEM((16, 2, rows_c, width), BF16),
            pltpu.VMEM(full, BF16),
            pltpu.VMEM(full, BF16),
            pltpu.VMEM((2 * n_tok, cut), F32),
            pltpu.VMEM((2 * n_tok, cut), F32),
            pltpu.VMEM((2 * n_corpus, cut), F32),
            pltpu.VMEM((2 * n_tok, cut), BF16),
            pltpu.VMEM((2 * n_tok, cut), BF16),
            pltpu.VMEM(full, BF16),
            pltpu.VMEM(full, BF16),
            pltpu.VMEM((2, 4, 2, 2, shard, cut), BF16),
            pltpu.VMEM((2, 4, 2, 2, shard, cut), BF16),
            pltpu.VMEM((2, 4, shard, cut), BF16),
            pltpu.VMEM((npass, 128), jnp.int32),
            pltpu.VMEM((npass, 128), jnp.int32),
            pltpu.VMEM((2, NT, npass, feat), F32),
            pltpu.VMEM((4 * NT, npass, feat), F32),
            pltpu.VMEM((npass, 128), F32),
            pltpu.VMEM((NT, npass, 128), F32),
            pltpu.VMEM((2 * NZ, 1, feat), F32),
            pltpu.VMEM((2 * NZ, 1, feat), F32),
            pltpu.SMEM((npass,), jnp.int32),
            pltpu.SMEM((npass,), jnp.int32),
            pltpu.SemaphoreType.DMA((9,)),
            pltpu.SemaphoreType.DMA((13,)),
            pltpu.SemaphoreType.DMA((n_sem,)),
        ],
        compiler_params=pltpu.CompilerParams(
            collective_id=0, has_side_effects=True, vmem_limit_bytes=60 * 1024 * 1024
        ),
    )(
        tokens.reshape(8, 2, rows_t, width),
        upstream.reshape(8, 2, rows_t, width),
        corpus.reshape(8, 2, rows_c, width),
        lengths,
        owners,
        w_in,
        w_out,
    )


def local(tokens, upstream, corpus, lengths, owners, w_in, w_out):
    width = w_in.shape[0] * lax.axis_size(GROUP_DP)
    hidden_units = w_in.shape[1] * lax.axis_size("tensor")
    scale_in = 1.0 / math.sqrt(width)
    scale_out = 1.0 / math.sqrt(hidden_units)
    return handed_over(
        *fused(tokens, upstream, corpus, lengths, owners, w_in, w_out, scale_in, scale_out)
    )


def solution(mesh):
    torus = Mesh(
        mesh.devices.reshape(mesh.shape["group"], 2, NZ, mesh.shape["tensor"]),
        ("group", "dp_0", "dp_1", "tensor"),
    )
    return jax.shard_map(
        local,
        mesh=torus,
        in_specs=(
            P(DP, None),
            P(DP, None),
            P(DP, None),
            P(DP),
            P(DP),
            P(GROUP_DP, "tensor"),
            P(GROUP_DP, "tensor"),
        ),
        out_specs=(P(GROUP_DP, "tensor"), P(GROUP_DP, "tensor"), P(GROUP_DP, "tensor")),
        check_vma=False,
    )
```

```python
import functools
import math

import jax
import jax.numpy as jnp
from jax import lax
from jax.experimental import pallas as pl
from jax.experimental.pallas import tpu as pltpu
from jax.sharding import Mesh
from jax.sharding import PartitionSpec as P

DP = ("dp_0", "dp_1")
GROUP_DP = ("group", "dp_0", "dp_1")
MESH = pl.DeviceIdType.MESH

LEARN_RATE = 0.5
EPSILON = 1e-06
F32 = jnp.float32
BF16 = jnp.bfloat16
NZ = 8
NT = 8
N_SEM = 107
TURNS = ((1, 1), (1, 0), (0, 1))


def kernel(
    plen,
    scale_in,
    scale_out,
    tokens_ref,
    upstream_ref,
    corpus_ref,
    len_hbm,
    owner_hbm,
    win_ref,
    wout_ref,
    new_in_ref,
    new_out_ref,
    index_ref,
    tok,
    up,
    cor,
    w_in,
    w_out,
    acc_p,
    acc_d,
    acc_c,
    hid,
    dpre,
    g_in,
    g_out,
    r_in,
    r_out,
    fin,
    lens_here,
    lens_there,
    pool,
    pool_in,
    square,
    square_in,
    letter,
    letter_in,
    len_ref,
    owner_ref,
    lsem,
    ssem,
    rsem,
):
    g = lax.axis_index("group")
    yh = lax.axis_index("dp_0")
    z = lax.axis_index("dp_1")
    t = lax.axis_index("tensor")
    core = lax.rem(t, 2)
    par = lax.rem(t // 2, 2)
    cut = w_in.shape[-1]
    shard = w_in.shape[-2]

    def cell(dg, dy, dt):
        return (lax.rem(g + dg, 2), lax.rem(yh + dy, 2), z, lax.rem(t + dt, NT))

    def column(dg, dy):
        return cell(dg, dy, 0)

    twin = (g, yh, z, t + 1 - 2 * core)
    right, left = cell(0, 0, 2), cell(0, 0, NT - 2)
    mate, swap = column(1, 1), column(1, 0)
    ring = (
        (g, yh, lax.rem(z + 1, NZ), t),
        (g, yh, lax.rem(z + NZ - 1, NZ), t),
    )
    step_of = (1, -1)

    def at(k):
        return lax.rem(z + k + 2 * NZ, NZ)

    barrier = pltpu.get_barrier_semaphore()
    met = [column(dg, dy) for dg, dy in TURNS] + list(ring) + [twin, right, left]
    met += [cell(0, 0, 4)] + [cell(dg, dy, 4) for dg, dy in TURNS]
    for device in met:
        pl.semaphore_signal(barrier, inc=1, device_id=device, device_id_type=MESH)

    def cols_of(dg, dy):
        q = lax.rem(g + dg, 2) * 2 + lax.rem(yh + dy, 2)
        return pl.ds(pl.multiple_of(q * cut, cut), cut)

    own_cols = cols_of(0, 0)
    groups_of_half = tok.shape[0] // 2
    here = pl.ds(yh * groups_of_half, groups_of_half)
    loads = []

    def load(src, dst):
        copy = pltpu.make_async_copy(src, dst, lsem.at[len(loads)])
        copy.start()
        loads.append(copy)
        return copy

    load_lens = load(len_hbm, len_ref)
    load_owners = load(owner_hbm, owner_ref)
    load_in = load(win_ref.at[:, own_cols], w_in.at[g, yh, z])
    load_out = load(wout_ref.at[:, own_cols], w_out.at[g, yh, z])
    load_tok = load(tokens_ref, tok.at[here])
    load_up = load(upstream_ref, up.at[here])
    load_cor = load(corpus_ref, cor.at[here])

    passages = len_ref.shape[0]

    def per_passage(ref, shape):
        row = lax.broadcasted_iota(jnp.int32, shape, 0)
        out = jnp.zeros(shape, jnp.int32)
        for i in range(passages):
            out = jnp.where(row == i, ref[i], out)
        return out

    half_nz = NZ // 2
    pair = z // 2
    e = 1 - 2 * lax.rem(z, 2)
    pairs = (
        None,
        pair,
        lax.rem(pair - e + half_nz, half_nz),
        lax.rem(pair + e + half_nz, half_nz),
        lax.rem(pair + 2, half_nz),
    )

    count = [0]

    shared = {}
    families = {}

    def push(src, dst, device, family, key=None):
        k = shared.get(key)
        if k is None:
            k = count[0]
            count[0] += 1
            if key is not None:
                shared[key] = k
        copy = pltpu.make_async_remote_copy(
            src_ref=src,
            dst_ref=dst,
            send_sem=ssem.at[families.setdefault(family, len(families))],
            recv_sem=rsem.at[k],
            device_id=device,
            device_id_type=MESH,
        )
        copy.start()
        return copy

    def same(ref, device, family, key=None):
        return push(ref, ref, device, family, key)

    def whole(ref, family, key):
        return pltpu.make_async_remote_copy(
            src_ref=ref,
            dst_ref=ref,
            send_sem=ssem.at[families[family]],
            recv_sem=rsem.at[shared[key] if key is not None else 0],
            device_id=twin,
            device_id_type=MESH,
        )

    pl.semaphore_wait(barrier, len(met))

    weights = ((win_ref, w_in), (wout_ref, w_out))
    slices = [[], []]

    def open_ring(a):
        src, w = weights[a]
        for d in range(2):
            push(src.at[:, own_cols], w.at[g, yh, z], ring[d], (0, a), (0, a, d))

    def open_column(a):
        src, w = weights[a]
        for dg, dy in TURNS:
            slices[a].append(
                push(src.at[:, cols_of(dg, dy)], w.at[g, yh, z], column(dg, dy), (0, a))
            )

    def slice_arrives(a, i):
        dg, dy = TURNS[i]
        slices[a][i].wait_recv()
        block = weights[a][1].at[lax.rem(g + dg, 2), lax.rem(yh + dy, 2), z]
        for d in range(2):
            same(block, ring[d], (0, a), (0, a, d))

    ahead = {}

    def ring_arrives(a, s):
        w = weights[a][1]
        for h in range(2):
            for d in range(2):
                if s == 1:
                    if h == 0:
                        whole(w.at[:, :, at(-step_of[d])], (0, a), (0, a, d)).wait_recv()
                elif s < 4 or h == d:
                    ahead[a, s, h, d].wait_recv()
                if s < 3 or (s == 3 and h == d):
                    o = at(-step_of[d] * s)
                    ahead[a, s + 1, h, d] = same(w.at[h, :, o], ring[d], (0, a))

    there = 1 - yh
    arrays = ((tokens_ref, tok), (upstream_ref, up), (corpus_ref, cor))
    from_mate, from_swap, from_side = {}, {}, {}

    fine = 16

    def spot(half, h, i, lane, r):
        start = half * groups_of_half + core * 4 + h * 2 + i
        return pl.ds(start, 1), lane, pl.ds(r * fine, fine)

    def open_part(k, i, r):
        src, buf = arrays[k]
        given = src.at[pl.ds(core * 4 + (1 - g) * 2 + i, 1), par, pl.ds(r * fine, fine)]
        from_mate[k, i, r] = push(given, buf.at[spot(yh, 1 - g, i, par, r)], mate, (1, k))

    def pass_on(k, i, r, other):
        block = arrays[k][1].at[spot(there, 1 - g if other else g, i, par, r)]
        from_side[k, i, r, other] = same(block, right if i else left, (1, k))
        same(block, twin, (1, k), (1, k))

    def mate_arrives(k, i, r):
        from_mate[k, i, r].wait_recv()
        from_swap[k, i, r] = same(arrays[k][1].at[spot(there, g, i, par, r)], swap, (1, k))
        pass_on(k, i, r, 0)

    def swap_arrives(k, i, r):
        from_swap[k, i, r].wait_recv()
        pass_on(k, i, r, 1)

    def side_arrives(k, i, r, other):
        from_side[k, i, r, other].wait_recv()
        block = arrays[k][1].at[spot(there, 1 - g if other else g, i, 1 - par, r)]
        same(block, twin, (1, k), (1, k))

    def after_twin(k):
        start = there * groups_of_half + (1 - core) * 4
        whole(arrays[k][1].at[pl.ds(start, 4)], (1, k), (1, k)).wait_recv()

    def rows_of(x, base, tile, p):
        parts = []
        per = x.shape[1] * x.shape[2]
        for q in range(4):
            at_q = pl.multiple_of(q * NZ * shard + p * 2 * shard, 2 * shard)
            block = x[pl.ds(base, tile // per), :, :, pl.ds(at_q, 2 * shard)]
            parts.append(block.reshape(tile, 2 * shard))
        return jnp.concatenate(parts, axis=1)

    def weight(w, p):
        parts = []
        for q in range(4):
            block = w[q // 2, q % 2, pl.ds(2 * p, 2)]
            parts.append(block.reshape(2 * shard, cut))
        return jnp.concatenate(parts, axis=0)

    def multiply(x, w, acc, half, p, is_first):
        per = x.shape[1] * x.shape[2]
        tile = min(512, per * groups_of_half)
        rows_half = per * groups_of_half

        def body(m, carry):
            base = half * groups_of_half + m * (tile // per)
            rows = pl.ds(pl.multiple_of(half * rows_half + m * tile, tile), tile)
            part_sum = jnp.dot(rows_of(x, base, tile, p), weight(w, p), preferred_element_type=F32)
            acc[rows, :] = part_sum if is_first else acc[rows, :] + part_sum
            return carry

        lax.fori_loop(0, rows_half // tile, body, 0)

    root = math.sqrt(2.0 / math.pi)

    def gelu_parts(p):
        th = jnp.tanh(root * (p + 0.044715 * (p * p * p)))
        return 0.5 * (1.0 + th), th

    slab = 64
    n_tok = acc_p.shape[0]

    def activate():
        def body(m, carry):
            rows = pl.ds(pl.multiple_of(m * slab, slab), slab)
            p = acc_p[rows, :] * scale_in
            cdf, th = gelu_parts(p)
            hid[rows, :] = (p * cdf).astype(BF16)
            acc_p[rows, :] = cdf + (0.5 * root) * p * (1.0 - th * th) * (
                1.0 + (3 * 0.044715) * (p * p)
            )
            return carry

        lax.fori_loop(0, n_tok // slab, body, 0)

    def slope_rows():
        def body(m, carry):
            rows = pl.ds(pl.multiple_of(m * slab, slab), slab)
            dpre[rows, :] = (acc_d[rows, :] * scale_out * acc_p[rows, :]).astype(BF16)
            return carry

        lax.fori_loop(0, n_tok // slab, body, 0)

    order = ((0, 0), (1, 0), (0, 1), (1, 1))
    open_ring(0)
    open_column(0)
    open_ring(1)
    for i, r in order[:2]:
        open_part(0, i, r)
    open_column(1)
    for i, r in order[2:]:
        open_part(0, i, r)
    for i, r in order:
        open_part(1, i, r)
    for i in range(2):
        open_part(2, i, 0)
    load_in.wait()
    load_out.wait()
    load_lens.wait()
    load_owners.wait()
    lens_here[...] = per_passage(len_ref, lens_here.shape)
    lens_copy = push(lens_here, lens_there, mate, (2,))
    load_tok.wait()
    load_up.wait()
    load_cor.wait()
    events = []

    def event(time, what, *args):
        events.append((time, len(events), what, args))

    for a, at_slice, at_ring in (
        (0, (3.4, 3.5, 3.6), (8.0, 12.5, 17.0, 20.5)),
        (1, (7.5, 7.6, 7.7), (13.5, 18.0, 21.8)),
    ):
        for i, time in enumerate(at_slice):
            event(time, slice_arrives, a, i)
        for i, time in enumerate(at_ring):
            event(time, ring_arrives, a, i + 1)
            x, w, acc = ((tok, w_in, acc_p), (up, w_out, acc_d))[a]
            event(time + 0.1, multiply, x, w, acc, yh, pairs[i + 1], i == 0)
            if a == 0 and i < 3:
                event(time + 0.2, multiply, cor, w_in, acc_c, yh, pairs[i + 1], i == 0)
    hop = 3.3
    for k, times in enumerate(((5.8, 7.2, 9.2, 10.6), (12.0, 13.4, 14.8, 16.2))):
        for (i, r), time in zip(order, times):
            event(time, mate_arrives, k, i, r)
            event(time + hop, swap_arrives, k, i, r)
            event(time + hop + 0.1, side_arrives, k, i, r, 0)
            event(time + 2 * hop + 0.2, side_arrives, k, i, r, 1)
    for i, time in enumerate((18.0, 19.4)):
        event(time, mate_arrives, 2, i, 0)
    event(19.6, after_twin, 0)
    for i in range(1, 4):
        event(19.7, multiply, tok, w_in, acc_p, there, pairs[i], i == 1)
    event(20.7, multiply, tok, w_in, acc_p, there, pairs[4], False)
    for i in range(2):
        event(20.8, swap_arrives, 2, i, 0)
        event(20.8, side_arrives, 2, i, 0, 0)
    event(20.9, activate)
    for _, _, what, args in sorted(events, key=lambda x: x[:2]):
        what(*args)

    def gradient(x, y, out, scale, p):
        def body(gg, carry):
            parts = []
            for yy in range(2):
                at_q = pl.multiple_of((gg * 2 + yy) * NZ * shard + p * 2 * shard, 2 * shard)
                block = x[:, :, :, pl.ds(at_q, 2 * shard)]
                parts.append(block.reshape(n_tok, 2 * shard))
            both = lax.dot_general(
                jnp.concatenate(parts, axis=1),
                y[...],
                (((0,), (0,)), ((), ())),
                preferred_element_type=F32,
            )
            both = (both * scale).astype(BF16).reshape(2, 2, shard, cut)
            for yy in range(2):
                out[gg, yy, pl.ds(2 * p, 2)] = both[yy]
            return carry

        lax.fori_loop(0, 2, body, 0)

    def add(a, b):
        return (a.astype(F32) + b.astype(F32)).astype(BF16)

    back = {}

    def give_back(a, s):
        grad, arrived = ((g_in, r_in), (g_out, r_out))[a]
        for h in range(2):
            for d in range(2):
                o = at(step_of[d] * (5 - s))
                if s == 1 and h != d:
                    continue
                if s > 2 or (s == 2 and h == d):
                    back[a, s - 1, h, d].wait_recv()
                    for yy in range(2):
                        grad[h, yy, o] = add(grad[h, yy, o], arrived[d, s - 2, h, yy])
                back[a, s, h, d] = push(grad.at[h, :, o], arrived.at[d, s - 1, h], ring[d], (3, a))

    feat = pool.shape[-1]
    rows_c = acc_c.shape[0] // 2
    mine = pl.ds(pl.multiple_of((2 * t + g) * feat, feat), feat)

    def pool_rows():
        after_twin(2)
        lens_copy.wait_recv()
        multiply(cor, w_in, acc_c, yh, pairs[4], False)
        for k in range(1, 5):
            multiply(cor, w_in, acc_c, there, pairs[k], k == 1)
        shape = (passages, rows_c)
        row = lax.broadcasted_iota(jnp.int32, shape, 0)
        col = lax.broadcasted_iota(jnp.int32, shape, 1)
        stack = []
        for half, lens in ((yh, lens_here), (there, lens_there)):
            span = pl.ds(pl.multiple_of(half * rows_c, rows_c), rows_c)
            pre = acc_c[span, :] * scale_in
            cdf, _ = gelu_parts(pre)
            ch = (pre * cdf).astype(BF16)
            stop = row * plen + jnp.broadcast_to(lens[:, :1], shape)
            inside = jnp.logical_and(col >= row * plen, col < stop)
            live = jnp.where(inside, 1.0, 0.0).astype(BF16)
            if not stack:
                x = cor[pl.ds(yh * groups_of_half, groups_of_half), :, :, mine]
                base = jnp.dot(live, x.reshape(rows_c, feat), preferred_element_type=F32)
            ph = jnp.dot(live, ch, preferred_element_type=F32)
            hi = ph.astype(BF16).astype(F32)
            stack += [hi, ph - hi]
        hl = jnp.concatenate(stack, axis=0).astype(BF16)

        def branch(q, carry):
            w = w_out[q // 2, lax.rem(q, 2)].reshape(NZ * shard, cut)
            both = lax.dot_general(hl, w, (((1,), (1,)), ((), ())), preferred_element_type=F32)
            both = both * scale_out
            n = NZ * shard // feat
            for i in range(2):
                rows = both[2 * i * passages : (2 * i + 1) * passages]
                rows = rows + both[(2 * i + 1) * passages : (2 * i + 2) * passages]
                for k in range(n):
                    pool[i, q * n + k] = rows[:, k * feat : (k + 1) * feat]
            return carry

        lax.fori_loop(0, 4, branch, 0)
        for dy in range(2):
            for dg in range(2):
                for dt in range(NT):
                    if dy or dg or dt:
                        to_g, _, _, to_t = cell(dg, dy, dt)
                        src = pool.at[dy, 2 * to_t + to_g]
                        slot = pool_in.at[(dy * 2 + dg) * NT + dt]
                        push(src, slot, cell(dg, dy, dt), (4,), (4,))
        return (base,)

    def square_rows(base):
        total = base + pool[0, 2 * t + g]
        whole(pool_in.at[pl.ds(1, 4 * NT - 1)], (4,), (4,)).wait_recv()
        for k in range(1, 4 * NT):
            total = total + pool_in[k]
        lens = jnp.broadcast_to(lens_here[:, :1], total.shape)
        pooled = total * (1.0 / lens.astype(F32))
        own_square = jnp.sum(pooled * pooled, axis=1, keepdims=True)
        square[...] = jnp.broadcast_to(own_square, square.shape)
        for k in range(1, 2 * NT):
            push(square, square_in.at[k], cell(k // NT, 0, k % NT), (5,), (5,))
        return pooled, own_square

    def post_rows(pooled, own_square):
        whole(square_in.at[pl.ds(1, 2 * NT - 1)], (5,), (5,)).wait_recv()
        total = own_square
        for k in range(1, 2 * NT):
            total = total + square_in[k][:, :1]
        rows = pooled * lax.rsqrt(total / (2 * NT * feat) + EPSILON)
        owners = per_passage(owner_ref, rows.shape)
        here_slot = (g * 2 + yh) * NZ + z
        for k in range(4 * NZ):
            to_g, to_yh = lax.rem(g + k // (2 * NZ), 2), lax.rem(yh + k // NZ, 2)
            to_z = at(k % NZ)
            owner = (to_g * 2 + to_yh) * NZ + to_z
            row = jnp.sum(jnp.where(owners == owner, rows, 0.0), axis=0, keepdims=True)
            if k:
                letter[k] = row
                push(
                    letter.at[k], letter_in.at[here_slot], (to_g, to_yh, to_z, t), (6,), (6,)
                )
            else:
                letter_in[here_slot] = row

    def read_rows():
        whole(letter_in.at[pl.ds(0, 4 * NZ - 1)], (6,), (6,)).wait_recv()
        shape = (2 * NZ, feat)
        row = lax.broadcasted_iota(jnp.int32, shape, 0)
        for gg in range(2):
            out = jnp.zeros(shape, F32)
            for d in range(2 * NZ):
                out = jnp.where(row == d, jnp.broadcast_to(letter_in[gg * 2 * NZ + d], shape), out)
            index_ref[:, gg * feat : (gg + 1) * feat] = out.astype(BF16)

    outs = (new_in_ref, new_out_ref)
    sums = ((g_in, r_in, w_in), (g_out, r_out, w_out))

    def settle(a):
        grad, arrived, w = sums[a]
        for h in range(2):
            for d in range(2):
                back[a, 4, h, d].wait_recv()
        for i, (dg, dy) in enumerate(TURNS + ((0, 0),)):
            gg, yy = lax.rem(g + dg, 2), lax.rem(yh + dy, 2)
            total = (
                grad[gg, yy, z].astype(F32)
                + arrived[0, 3, gg, yy].astype(F32)
                + arrived[1, 3, gg, yy].astype(F32)
            )
            fin[a, i] = (w[gg, yy, z].astype(F32) - LEARN_RATE * total).astype(BF16)
            target = outs[a].at[:, own_cols]
            if dg or dy:
                push(fin.at[a, i], target, column(dg, dy), (7, a), (7, a))
            else:
                load(fin.at[a, i], target)

    def grad_out(j):
        gradient(up, hid, g_out, scale_out, pairs[j])

    def grad_in(j):
        gradient(tok, dpre, g_in, scale_in, pairs[j])

    after_twin(1)
    grad_out(4)
    give_back(1, 1)
    ring_arrives(1, 4)
    multiply(up, w_out, acc_d, yh, pairs[4], False)
    for k in range(1, 5):
        multiply(up, w_out, acc_d, there, pairs[k], k == 1)
    slope_rows()
    for i in range(2):
        side_arrives(2, i, 0, 1)
    grad_in(4)
    give_back(0, 1)
    grad_out(3)
    give_back(1, 2)
    stage = pool_rows()
    grad_in(3)
    give_back(0, 2)
    grad_out(2)
    give_back(1, 3)
    grad_in(2)
    give_back(0, 3)
    stage = square_rows(*stage)
    grad_out(1)
    give_back(1, 4)
    grad_in(1)
    give_back(0, 4)
    post_rows(*stage)
    settle(1)
    settle(0)
    read_rows()
    for a in range(2):
        whole(outs[a].at[:, pl.ds(0, 3 * cut)], (7, a), (7, a)).wait_recv()
    for copy in loads[7:]:
        copy.wait()
    covers = [((0, 0), acc_p.at[pl.ds(0, 31 * n_tok // 32)])]
    covers += [((0, 1), acc_d.at[pl.ds(0, 31 * n_tok // 32)])]
    covers += [((1, k), arrays[k][1].at[pl.ds(0, groups_of_half)]) for k in range(3)]
    covers += [((2,), lens_here), ((4,), pool_in.at[pl.ds(1, 4 * NT - 1)])]
    covers += [((3, a), sums[a][0].at[:, :, pl.ds(0, NZ - 1)]) for a in range(2)]
    covers += [((5,), square_in.at[pl.ds(1, 2 * NT - 1)]), ((6,), letter_in.at[pl.ds(0, 4 * NZ - 1)])]
    covers += [((7, a), fin.at[a, pl.ds(0, 3)]) for a in range(2)]
    for family, ref in covers:
        whole(ref, family, None).wait_send()


def pass_through(*refs):
    n = len(refs) // 3
    sources, results, held = refs[:n], refs[n : 2 * n], refs[2 * n : 3 * n]
    sems = refs[3 * n]
    taken = []
    for k in range(n):
        copy = pltpu.make_async_copy(sources[k], held[k], sems.at[k])
        copy.start()
        taken.append(copy)
    given = []
    for k in range(n):
        taken[k].wait()
        copy = pltpu.make_async_copy(held[k], results[k], sems.at[n + k])
        copy.start()
        given.append(copy)
    for copy in given:
        copy.wait()


def handed_over(*arrays):
    any_spec = pl.BlockSpec(memory_space=pl.ANY)
    return pl.pallas_call(
        pass_through,
        out_shape=tuple(jax.ShapeDtypeStruct(x.shape, x.dtype) for x in arrays),
        in_specs=[any_spec] * len(arrays),
        out_specs=(any_spec,) * len(arrays),
        scratch_shapes=[pltpu.VMEM(x.shape, x.dtype) for x in arrays]
        + [pltpu.SemaphoreType.DMA((2 * len(arrays),))],
    )(*arrays)


def fused(tokens, upstream, corpus, lengths, owners, w_in, w_out, scale_in, scale_out):
    shard, local_ff = w_in.shape
    cut = local_ff // 4
    n_tok, width = tokens.shape
    n_corpus = corpus.shape[0]
    npass = lengths.shape[0]
    full = (2, 2, NZ, shard, cut)
    n_sem = N_SEM
    feat = width // (2 * NT)
    rows_t, rows_c = n_tok // 16, n_corpus // 16
    any_spec = pl.BlockSpec(memory_space=pl.ANY)
    vmem_spec = pl.BlockSpec(memory_space=pltpu.VMEM)
    return pl.pallas_call(
        functools.partial(kernel, n_corpus // npass, scale_in, scale_out),
        out_shape=(
            jax.ShapeDtypeStruct((shard, local_ff), BF16),
            jax.ShapeDtypeStruct((shard, local_ff), BF16),
            jax.ShapeDtypeStruct((2 * NZ, 2 * feat), BF16),
        ),
        in_specs=[any_spec] * 7,
        out_specs=(any_spec, any_spec, vmem_spec),
        scratch_shapes=[
            pltpu.VMEM((16, 2, rows_t, width), BF16),
            pltpu.VMEM((16, 2, rows_t, width), BF16),
            pltpu.VMEM((16, 2, rows_c, width), BF16),
            pltpu.VMEM(full, BF16),
            pltpu.VMEM(full, BF16),
            pltpu.VMEM((2 * n_tok, cut), F32),
            pltpu.VMEM((2 * n_tok, cut), F32),
            pltpu.VMEM((2 * n_corpus, cut), F32),
            pltpu.VMEM((2 * n_tok, cut), BF16),
            pltpu.VMEM((2 * n_tok, cut), BF16),
            pltpu.VMEM(full, BF16),
            pltpu.VMEM(full, BF16),
            pltpu.VMEM((2, 4, 2, 2, shard, cut), BF16),
            pltpu.VMEM((2, 4, 2, 2, shard, cut), BF16),
            pltpu.VMEM((2, 4, shard, cut), BF16),
            pltpu.VMEM((npass, 128), jnp.int32),
            pltpu.VMEM((npass, 128), jnp.int32),
            pltpu.VMEM((2, 2 * NT, npass, feat), F32),
            pltpu.VMEM((4 * NT, npass, feat), F32),
            pltpu.VMEM((npass, 128), F32),
            pltpu.VMEM((2 * NT, npass, 128), F32),
            pltpu.VMEM((4 * NZ, 1, feat), F32),
            pltpu.VMEM((4 * NZ, 1, feat), F32),
            pltpu.SMEM((npass,), jnp.int32),
            pltpu.SMEM((npass,), jnp.int32),
            pltpu.SemaphoreType.DMA((9,)),
            pltpu.SemaphoreType.DMA((13,)),
            pltpu.SemaphoreType.DMA((n_sem,)),
        ],
        compiler_params=pltpu.CompilerParams(
            collective_id=0, has_side_effects=True, vmem_limit_bytes=60 * 1024 * 1024
        ),
    )(
        tokens.reshape(8, 2, rows_t, width),
        upstream.reshape(8, 2, rows_t, width),
        corpus.reshape(8, 2, rows_c, width),
        lengths,
        owners,
        w_in,
        w_out,
    )


def local(tokens, upstream, corpus, lengths, owners, w_in, w_out):
    width = w_in.shape[0] * lax.axis_size(GROUP_DP)
    hidden_units = w_in.shape[1] * lax.axis_size("tensor")
    scale_in = 1.0 / math.sqrt(width)
    scale_out = 1.0 / math.sqrt(hidden_units)
    return handed_over(
        *fused(tokens, upstream, corpus, lengths, owners, w_in, w_out, scale_in, scale_out)
    )


def solution(mesh):
    torus = Mesh(
        mesh.devices.reshape(mesh.shape["group"], 2, NZ, mesh.shape["tensor"]),
        ("group", "dp_0", "dp_1", "tensor"),
    )
    return jax.shard_map(
        local,
        mesh=torus,
        in_specs=(
            P(DP, None),
            P(DP, None),
            P(DP, None),
            P(DP),
            P(DP),
            P(GROUP_DP, "tensor"),
            P(GROUP_DP, "tensor"),
        ),
        out_specs=(P(GROUP_DP, "tensor"), P(GROUP_DP, "tensor"), P(GROUP_DP, "tensor")),
        check_vma=False,
    )
```

```python
import functools
import math

import jax
import jax.numpy as jnp
from jax import lax
from jax.experimental import pallas as pl
from jax.experimental.pallas import tpu as pltpu
from jax.sharding import Mesh
from jax.sharding import PartitionSpec as P

DP = ("dp_0", "dp_1")
GROUP_DP = ("group", "dp_0", "dp_1")
MESH = pl.DeviceIdType.MESH

LEARN_RATE = 0.5
EPSILON = 1e-06
F32 = jnp.float32
BF16 = jnp.bfloat16
NZ = 8
NT = 8
N_SEM = 107
TURNS = ((1, 1), (1, 0), (0, 1))


def kernel(
    plen,
    scale_in,
    scale_out,
    tokens_ref,
    upstream_ref,
    corpus_ref,
    len_hbm,
    owner_hbm,
    win_ref,
    wout_ref,
    new_in_ref,
    new_out_ref,
    index_ref,
    tok,
    up,
    cor,
    w_in,
    w_out,
    acc_p,
    acc_d,
    acc_c,
    hid,
    dpre,
    g_in,
    g_out,
    r_in,
    r_out,
    fin,
    held,
    lens_here,
    lens_there,
    pool,
    pool_in,
    square,
    square_in,
    letter,
    letter_in,
    len_ref,
    owner_ref,
    lsem,
    ssem,
    rsem,
):
    g = lax.axis_index("group")
    yh = lax.axis_index("dp_0")
    z = lax.axis_index("dp_1")
    t = lax.axis_index("tensor")
    core = lax.rem(t, 2)
    par = lax.rem(t // 2, 2)
    cut = w_in.shape[-1]
    shard = w_in.shape[-2]

    def cell(dg, dy, dt):
        return (lax.rem(g + dg, 2), lax.rem(yh + dy, 2), z, lax.rem(t + dt, NT))

    def column(dg, dy):
        return cell(dg, dy, 0)

    twin = (g, yh, z, t + 1 - 2 * core)
    right, left = cell(0, 0, 2), cell(0, 0, NT - 2)
    mate, swap = column(1, 1), column(1, 0)
    ring = (
        (g, yh, lax.rem(z + 1, NZ), t),
        (g, yh, lax.rem(z + NZ - 1, NZ), t),
    )
    step_of = (1, -1)

    def at(k):
        return lax.rem(z + k + 2 * NZ, NZ)

    barrier = pltpu.get_barrier_semaphore()
    met = [column(dg, dy) for dg, dy in TURNS] + list(ring) + [twin, right, left]
    met += [cell(0, 0, 4)] + [cell(dg, dy, 4) for dg, dy in TURNS]
    for device in met:
        pl.semaphore_signal(barrier, inc=1, device_id=device, device_id_type=MESH)

    def cols_of(dg, dy):
        q = lax.rem(g + dg, 2) * 2 + lax.rem(yh + dy, 2)
        return pl.ds(pl.multiple_of(q * cut, cut), cut)

    own_cols = cols_of(0, 0)
    groups_of_half = tok.shape[0] // 2
    here = pl.ds(yh * groups_of_half, groups_of_half)
    loads = []

    def load(src, dst):
        copy = pltpu.make_async_copy(src, dst, lsem.at[len(loads)])
        copy.start()
        loads.append(copy)
        return copy

    load_lens = load(len_hbm, len_ref)
    load_owners = load(owner_hbm, owner_ref)
    load_rows = [load(win_ref, held.at[0]), load(wout_ref, held.at[1])]
    load_in = load(win_ref.at[:, own_cols], w_in.at[g, yh, z])
    load_out = load(wout_ref.at[:, own_cols], w_out.at[g, yh, z])
    load_tok = load(tokens_ref, tok.at[here])
    load_up = load(upstream_ref, up.at[here])
    load_cor = load(corpus_ref, cor.at[here])

    passages = len_ref.shape[0]

    def per_passage(ref, shape):
        row = lax.broadcasted_iota(jnp.int32, shape, 0)
        out = jnp.zeros(shape, jnp.int32)
        for i in range(passages):
            out = jnp.where(row == i, ref[i], out)
        return out

    half_nz = NZ // 2
    pair = z // 2
    e = 1 - 2 * lax.rem(z, 2)
    pairs = (
        None,
        pair,
        lax.rem(pair - e + half_nz, half_nz),
        lax.rem(pair + e + half_nz, half_nz),
        lax.rem(pair + 2, half_nz),
    )

    count = [0]

    shared = {}
    families = {}

    def push(src, dst, device, family, key=None):
        k = shared.get(key)
        if k is None:
            k = count[0]
            count[0] += 1
            if key is not None:
                shared[key] = k
        copy = pltpu.make_async_remote_copy(
            src_ref=src,
            dst_ref=dst,
            send_sem=ssem.at[families.setdefault(family, len(families))],
            recv_sem=rsem.at[k],
            device_id=device,
            device_id_type=MESH,
        )
        copy.start()
        return copy

    def same(ref, device, family, key=None):
        return push(ref, ref, device, family, key)

    def whole(ref, family, key):
        return pltpu.make_async_remote_copy(
            src_ref=ref,
            dst_ref=ref,
            send_sem=ssem.at[families[family]],
            recv_sem=rsem.at[shared[key] if key is not None else 0],
            device_id=twin,
            device_id_type=MESH,
        )

    pl.semaphore_wait(barrier, len(met))

    weights = ((held.at[0], w_in), (held.at[1], w_out))
    slices = [[], []]

    def open_ring(a):
        src, w = weights[a]
        for d in range(2):
            push(src.at[:, own_cols], w.at[g, yh, z], ring[d], (0, a), (0, a, d))

    def open_column(a):
        src, w = weights[a]
        for dg, dy in TURNS:
            slices[a].append(
                push(src.at[:, cols_of(dg, dy)], w.at[g, yh, z], column(dg, dy), (0, a))
            )

    def slice_arrives(a, i):
        dg, dy = TURNS[i]
        slices[a][i].wait_recv()
        block = weights[a][1].at[lax.rem(g + dg, 2), lax.rem(yh + dy, 2), z]
        for d in range(2):
            same(block, ring[d], (0, a), (0, a, d))

    ahead = {}

    def ring_arrives(a, s):
        w = weights[a][1]
        for h in range(2):
            for d in range(2):
                if s == 1:
                    if h == 0:
                        whole(w.at[:, :, at(-step_of[d])], (0, a), (0, a, d)).wait_recv()
                elif s < 4 or h == d:
                    ahead[a, s, h, d].wait_recv()
                if s < 3 or (s == 3 and h == d):
                    o = at(-step_of[d] * s)
                    ahead[a, s + 1, h, d] = same(w.at[h, :, o], ring[d], (0, a))

    there = 1 - yh
    arrays = ((tokens_ref, tok), (upstream_ref, up), (corpus_ref, cor))
    from_mate, from_swap, from_side = {}, {}, {}

    fine = 16

    def spot(half, h, i, lane, r):
        start = half * groups_of_half + core * 4 + h * 2 + i
        return pl.ds(start, 1), lane, pl.ds(r * fine, fine)

    def open_part(k, i, r):
        buf = arrays[k][1]
        from_mate[k, i, r] = same(buf.at[spot(yh, 1 - g, i, par, r)], mate, (1, k))

    def pass_on(k, i, r, other):
        block = arrays[k][1].at[spot(there, 1 - g if other else g, i, par, r)]
        from_side[k, i, r, other] = same(block, right if i else left, (1, k))
        same(block, twin, (1, k), (1, k))

    def mate_arrives(k, i, r):
        from_mate[k, i, r].wait_recv()
        from_swap[k, i, r] = same(arrays[k][1].at[spot(there, g, i, par, r)], swap, (1, k))
        pass_on(k, i, r, 0)

    def swap_arrives(k, i, r):
        from_swap[k, i, r].wait_recv()
        pass_on(k, i, r, 1)

    def side_arrives(k, i, r, other):
        from_side[k, i, r, other].wait_recv()
        block = arrays[k][1].at[spot(there, 1 - g if other else g, i, 1 - par, r)]
        same(block, twin, (1, k), (1, k))

    def after_twin(k):
        start = there * groups_of_half + (1 - core) * 4
        whole(arrays[k][1].at[pl.ds(start, 4)], (1, k), (1, k)).wait_recv()

    def rows_of(x, base, tile, p):
        parts = []
        per = x.shape[1] * x.shape[2]
        for q in range(4):
            at_q = pl.multiple_of(q * NZ * shard + p * 2 * shard, 2 * shard)
            block = x[pl.ds(base, tile // per), :, :, pl.ds(at_q, 2 * shard)]
            parts.append(block.reshape(tile, 2 * shard))
        return jnp.concatenate(parts, axis=1)

    def weight(w, p):
        parts = []
        for q in range(4):
            block = w[q // 2, q % 2, pl.ds(2 * p, 2)]
            parts.append(block.reshape(2 * shard, cut))
        return jnp.concatenate(parts, axis=0)

    def multiply(x, w, acc, half, p, is_first):
        per = x.shape[1] * x.shape[2]
        tile = min(512, per * groups_of_half)
        rows_half = per * groups_of_half

        def body(m, carry):
            base = half * groups_of_half + m * (tile // per)
            rows = pl.ds(pl.multiple_of(half * rows_half + m * tile, tile), tile)
            part_sum = jnp.dot(rows_of(x, base, tile, p), weight(w, p), preferred_element_type=F32)
            acc[rows, :] = part_sum if is_first else acc[rows, :] + part_sum
            return carry

        lax.fori_loop(0, rows_half // tile, body, 0)

    root = math.sqrt(2.0 / math.pi)

    def gelu_parts(p):
        th = jnp.tanh(root * (p + 0.044715 * (p * p * p)))
        return 0.5 * (1.0 + th), th

    slab = 64
    n_tok = acc_p.shape[0]

    def activate():
        def body(m, carry):
            rows = pl.ds(pl.multiple_of(m * slab, slab), slab)
            p = acc_p[rows, :] * scale_in
            cdf, th = gelu_parts(p)
            hid[rows, :] = (p * cdf).astype(BF16)
            acc_p[rows, :] = cdf + (0.5 * root) * p * (1.0 - th * th) * (
                1.0 + (3 * 0.044715) * (p * p)
            )
            return carry

        lax.fori_loop(0, n_tok // slab, body, 0)

    def slope_rows():
        def body(m, carry):
            rows = pl.ds(pl.multiple_of(m * slab, slab), slab)
            dpre[rows, :] = (acc_d[rows, :] * scale_out * acc_p[rows, :]).astype(BF16)
            return carry

        lax.fori_loop(0, n_tok // slab, body, 0)

    order = ((0, 0), (1, 0), (0, 1), (1, 1))
    for copy in load_rows:
        copy.wait()
    open_ring(0)
    open_column(0)
    open_ring(1)
    load_tok.wait()
    for i, r in order[:2]:
        open_part(0, i, r)
    open_column(1)
    for i, r in order[2:]:
        open_part(0, i, r)
    load_up.wait()
    for i, r in order:
        open_part(1, i, r)
    load_cor.wait()
    for i in range(2):
        open_part(2, i, 0)
    load_in.wait()
    load_out.wait()
    load_lens.wait()
    load_owners.wait()
    lens_here[...] = per_passage(len_ref, lens_here.shape)
    lens_copy = push(lens_here, lens_there, mate, (2,))
    events = []

    def event(time, what, *args):
        events.append((time, len(events), what, args))

    for a, at_slice, at_ring in (
        (0, (3.4, 3.5, 3.6), (8.0, 13.7, 18.0, 21.5)),
        (1, (7.5, 7.6, 7.7), (14.5, 19.5, 23.0)),
    ):
        for i, time in enumerate(at_slice):
            event(time, slice_arrives, a, i)
        for i, time in enumerate(at_ring):
            event(time, ring_arrives, a, i + 1)
            x, w, acc = ((tok, w_in, acc_p), (up, w_out, acc_d))[a]
            event(time + 0.1, multiply, x, w, acc, yh, pairs[i + 1], i == 0)
            if a == 0 and i < 3:
                event(time + 0.2, multiply, cor, w_in, acc_c, yh, pairs[i + 1], i == 0)
    hop = 3.4
    for k, times in enumerate(((5.8, 7.2, 9.7, 11.1), (12.2, 13.6, 15.0, 16.4))):
        for (i, r), time in zip(order, times):
            event(time, mate_arrives, k, i, r)
            event(time + hop, swap_arrives, k, i, r)
            event(time + hop + 0.1, side_arrives, k, i, r, 0)
            event(time + 2 * hop + 0.6, side_arrives, k, i, r, 1)
    for i, time in enumerate((18.1, 19.5)):
        event(time, mate_arrives, 2, i, 0)
    event(22.0, after_twin, 0)
    for i in range(1, 5):
        event(22.1, multiply, tok, w_in, acc_p, there, pairs[i], i == 1)
    event(23.9, activate)
    for i in range(2):
        event(24.0, swap_arrives, 2, i, 0)
        event(24.0, side_arrives, 2, i, 0, 0)
    for _, _, what, args in sorted(events, key=lambda x: x[:2]):
        what(*args)

    def gradient(x, y, out, scale, p):
        def body(gg, carry):
            parts = []
            for yy in range(2):
                at_q = pl.multiple_of((gg * 2 + yy) * NZ * shard + p * 2 * shard, 2 * shard)
                block = x[:, :, :, pl.ds(at_q, 2 * shard)]
                parts.append(block.reshape(n_tok, 2 * shard))
            both = lax.dot_general(
                jnp.concatenate(parts, axis=1),
                y[...],
                (((0,), (0,)), ((), ())),
                preferred_element_type=F32,
            )
            both = (both * scale).astype(BF16).reshape(2, 2, shard, cut)
            for yy in range(2):
                out[gg, yy, pl.ds(2 * p, 2)] = both[yy]
            return carry

        lax.fori_loop(0, 2, body, 0)

    def add(a, b):
        return (a.astype(F32) + b.astype(F32)).astype(BF16)

    back = {}

    def give_back(a, s):
        grad, arrived = ((g_in, r_in), (g_out, r_out))[a]
        for h in range(2):
            for d in range(2):
                o = at(step_of[d] * (5 - s))
                if s == 1 and h != d:
                    continue
                if s > 2 or (s == 2 and h == d):
                    back[a, s - 1, h, d].wait_recv()
                    for yy in range(2):
                        grad[h, yy, o] = add(grad[h, yy, o], arrived[d, s - 2, h, yy])
                back[a, s, h, d] = push(grad.at[h, :, o], arrived.at[d, s - 1, h], ring[d], (3, a))

    feat = pool.shape[-1]
    rows_c = acc_c.shape[0] // 2
    mine = pl.ds(pl.multiple_of((2 * t + g) * feat, feat), feat)

    def pool_rows():
        after_twin(2)
        lens_copy.wait_recv()
        multiply(cor, w_in, acc_c, yh, pairs[4], False)
        for k in range(1, 5):
            multiply(cor, w_in, acc_c, there, pairs[k], k == 1)
        shape = (passages, rows_c)
        row = lax.broadcasted_iota(jnp.int32, shape, 0)
        col = lax.broadcasted_iota(jnp.int32, shape, 1)
        stack = []
        for half, lens in ((yh, lens_here), (there, lens_there)):
            span = pl.ds(pl.multiple_of(half * rows_c, rows_c), rows_c)
            pre = acc_c[span, :] * scale_in
            cdf, _ = gelu_parts(pre)
            ch = (pre * cdf).astype(BF16)
            stop = row * plen + jnp.broadcast_to(lens[:, :1], shape)
            inside = jnp.logical_and(col >= row * plen, col < stop)
            live = jnp.where(inside, 1.0, 0.0).astype(BF16)
            if not stack:
                x = cor[pl.ds(yh * groups_of_half, groups_of_half), :, :, mine]
                base = jnp.dot(live, x.reshape(rows_c, feat), preferred_element_type=F32)
            ph = jnp.dot(live, ch, preferred_element_type=F32)
            hi = ph.astype(BF16).astype(F32)
            stack += [hi, ph - hi]
        hl = jnp.concatenate(stack, axis=0).astype(BF16)

        def branch(q, carry):
            w = w_out[q // 2, lax.rem(q, 2)].reshape(NZ * shard, cut)
            both = lax.dot_general(hl, w, (((1,), (1,)), ((), ())), preferred_element_type=F32)
            both = both * scale_out
            n = NZ * shard // feat
            for i in range(2):
                rows = both[2 * i * passages : (2 * i + 1) * passages]
                rows = rows + both[(2 * i + 1) * passages : (2 * i + 2) * passages]
                for k in range(n):
                    pool[i, q * n + k] = rows[:, k * feat : (k + 1) * feat]
            return carry

        lax.fori_loop(0, 4, branch, 0)
        for dy in range(2):
            for dg in range(2):
                for dt in range(NT):
                    if dy or dg or dt:
                        to_g, _, _, to_t = cell(dg, dy, dt)
                        src = pool.at[dy, 2 * to_t + to_g]
                        slot = pool_in.at[(dy * 2 + dg) * NT + dt]
                        push(src, slot, cell(dg, dy, dt), (4,), (4,))
        return (base,)

    def square_rows(base):
        total = base + pool[0, 2 * t + g]
        whole(pool_in.at[pl.ds(1, 4 * NT - 1)], (4,), (4,)).wait_recv()
        for k in range(1, 4 * NT):
            total = total + pool_in[k]
        lens = jnp.broadcast_to(lens_here[:, :1], total.shape)
        pooled = total * (1.0 / lens.astype(F32))
        own_square = jnp.sum(pooled * pooled, axis=1, keepdims=True)
        square[...] = jnp.broadcast_to(own_square, square.shape)
        for k in range(1, 2 * NT):
            push(square, square_in.at[k], cell(k // NT, 0, k % NT), (5,), (5,))
        return pooled, own_square

    def post_rows(pooled, own_square):
        whole(square_in.at[pl.ds(1, 2 * NT - 1)], (5,), (5,)).wait_recv()
        total = own_square
        for k in range(1, 2 * NT):
            total = total + square_in[k][:, :1]
        rows = pooled * lax.rsqrt(total / (2 * NT * feat) + EPSILON)
        owners = per_passage(owner_ref, rows.shape)
        here_slot = (g * 2 + yh) * NZ + z
        for k in range(4 * NZ):
            to_g, to_yh = lax.rem(g + k // (2 * NZ), 2), lax.rem(yh + k // NZ, 2)
            to_z = at(k % NZ)
            owner = (to_g * 2 + to_yh) * NZ + to_z
            row = jnp.sum(jnp.where(owners == owner, rows, 0.0), axis=0, keepdims=True)
            if k:
                letter[k] = row
                push(
                    letter.at[k], letter_in.at[here_slot], (to_g, to_yh, to_z, t), (6,), (6,)
                )
            else:
                letter_in[here_slot] = row

    def read_rows():
        whole(letter_in.at[pl.ds(0, 4 * NZ - 1)], (6,), (6,)).wait_recv()
        shape = (2 * NZ, feat)
        row = lax.broadcasted_iota(jnp.int32, shape, 0)
        for gg in range(2):
            out = jnp.zeros(shape, F32)
            for d in range(2 * NZ):
                out = jnp.where(row == d, jnp.broadcast_to(letter_in[gg * 2 * NZ + d], shape), out)
            index_ref[:, gg * feat : (gg + 1) * feat] = out.astype(BF16)

    outs = (new_in_ref, new_out_ref)
    sums = ((g_in, r_in, w_in), (g_out, r_out, w_out))

    def settle(a):
        grad, arrived, w = sums[a]
        for h in range(2):
            for d in range(2):
                back[a, 4, h, d].wait_recv()
        for i, (dg, dy) in enumerate(TURNS + ((0, 0),)):
            gg, yy = lax.rem(g + dg, 2), lax.rem(yh + dy, 2)
            total = (
                grad[gg, yy, z].astype(F32)
                + arrived[0, 3, gg, yy].astype(F32)
                + arrived[1, 3, gg, yy].astype(F32)
            )
            fin[a, i] = (w[gg, yy, z].astype(F32) - LEARN_RATE * total).astype(BF16)
            target = outs[a].at[:, own_cols]
            if dg or dy:
                push(fin.at[a, i], target, column(dg, dy), (7, a), (7, a))
            else:
                load(fin.at[a, i], target)

    def grad_out(j):
        gradient(up, hid, g_out, scale_out, pairs[j])

    def grad_in(j):
        gradient(tok, dpre, g_in, scale_in, pairs[j])

    after_twin(1)
    grad_out(4)
    give_back(1, 1)
    ring_arrives(1, 4)
    multiply(up, w_out, acc_d, yh, pairs[4], False)
    for k in range(1, 5):
        multiply(up, w_out, acc_d, there, pairs[k], k == 1)
    slope_rows()
    for i in range(2):
        side_arrives(2, i, 0, 1)
    grad_in(4)
    give_back(0, 1)
    grad_out(3)
    give_back(1, 2)
    stage = pool_rows()
    grad_in(3)
    give_back(0, 2)
    grad_out(2)
    give_back(1, 3)
    grad_in(2)
    give_back(0, 3)
    stage = square_rows(*stage)
    grad_out(1)
    give_back(1, 4)
    grad_in(1)
    give_back(0, 4)
    post_rows(*stage)
    settle(1)
    settle(0)
    read_rows()
    for a in range(2):
        whole(outs[a].at[:, pl.ds(0, 3 * cut)], (7, a), (7, a)).wait_recv()
    for copy in loads[9:]:
        copy.wait()
    covers = [((0, 0), acc_p.at[pl.ds(0, 31 * n_tok // 32)])]
    covers += [((0, 1), acc_d.at[pl.ds(0, 31 * n_tok // 32)])]
    covers += [((1, k), arrays[k][1].at[pl.ds(0, groups_of_half)]) for k in range(3)]
    covers += [((2,), lens_here), ((4,), pool_in.at[pl.ds(1, 4 * NT - 1)])]
    covers += [((3, a), sums[a][0].at[:, :, pl.ds(0, NZ - 1)]) for a in range(2)]
    covers += [((5,), square_in.at[pl.ds(1, 2 * NT - 1)]), ((6,), letter_in.at[pl.ds(0, 4 * NZ - 1)])]
    covers += [((7, a), fin.at[a, pl.ds(0, 3)]) for a in range(2)]
    for family, ref in covers:
        whole(ref, family, None).wait_send()


def pass_through(*refs):
    n = len(refs) // 3
    sources, results, held = refs[:n], refs[n : 2 * n], refs[2 * n : 3 * n]
    sems = refs[3 * n]
    taken = []
    for k in range(n):
        copy = pltpu.make_async_copy(sources[k], held[k], sems.at[k])
        copy.start()
        taken.append(copy)
    given = []
    for k in range(n):
        taken[k].wait()
        copy = pltpu.make_async_copy(held[k], results[k], sems.at[n + k])
        copy.start()
        given.append(copy)
    for copy in given:
        copy.wait()


def handed_over(*arrays):
    any_spec = pl.BlockSpec(memory_space=pl.ANY)
    return pl.pallas_call(
        pass_through,
        out_shape=tuple(jax.ShapeDtypeStruct(x.shape, x.dtype) for x in arrays),
        in_specs=[any_spec] * len(arrays),
        out_specs=(any_spec,) * len(arrays),
        scratch_shapes=[pltpu.VMEM(x.shape, x.dtype) for x in arrays]
        + [pltpu.SemaphoreType.DMA((2 * len(arrays),))],
    )(*arrays)


def fused(tokens, upstream, corpus, lengths, owners, w_in, w_out, scale_in, scale_out):
    shard, local_ff = w_in.shape
    cut = local_ff // 4
    n_tok, width = tokens.shape
    n_corpus = corpus.shape[0]
    npass = lengths.shape[0]
    full = (2, 2, NZ, shard, cut)
    n_sem = N_SEM
    feat = width // (2 * NT)
    rows_t, rows_c = n_tok // 16, n_corpus // 16
    any_spec = pl.BlockSpec(memory_space=pl.ANY)
    vmem_spec = pl.BlockSpec(memory_space=pltpu.VMEM)
    return pl.pallas_call(
        functools.partial(kernel, n_corpus // npass, scale_in, scale_out),
        out_shape=(
            jax.ShapeDtypeStruct((shard, local_ff), BF16),
            jax.ShapeDtypeStruct((shard, local_ff), BF16),
            jax.ShapeDtypeStruct((2 * NZ, 2 * feat), BF16),
        ),
        in_specs=[any_spec] * 7,
        out_specs=(any_spec, any_spec, vmem_spec),
        scratch_shapes=[
            pltpu.VMEM((16, 2, rows_t, width), BF16),
            pltpu.VMEM((16, 2, rows_t, width), BF16),
            pltpu.VMEM((16, 2, rows_c, width), BF16),
            pltpu.VMEM(full, BF16),
            pltpu.VMEM(full, BF16),
            pltpu.VMEM((2 * n_tok, cut), F32),
            pltpu.VMEM((2 * n_tok, cut), F32),
            pltpu.VMEM((2 * n_corpus, cut), F32),
            pltpu.VMEM((2 * n_tok, cut), BF16),
            pltpu.VMEM((2 * n_tok, cut), BF16),
            pltpu.VMEM(full, BF16),
            pltpu.VMEM(full, BF16),
            pltpu.VMEM((2, 4, 2, 2, shard, cut), BF16),
            pltpu.VMEM((2, 4, 2, 2, shard, cut), BF16),
            pltpu.VMEM((2, 4, shard, cut), BF16),
            pltpu.VMEM((2, shard, local_ff), BF16),
            pltpu.VMEM((npass, 128), jnp.int32),
            pltpu.VMEM((npass, 128), jnp.int32),
            pltpu.VMEM((2, 2 * NT, npass, feat), F32),
            pltpu.VMEM((4 * NT, npass, feat), F32),
            pltpu.VMEM((npass, 128), F32),
            pltpu.VMEM((2 * NT, npass, 128), F32),
            pltpu.VMEM((4 * NZ, 1, feat), F32),
            pltpu.VMEM((4 * NZ, 1, feat), F32),
            pltpu.SMEM((npass,), jnp.int32),
            pltpu.SMEM((npass,), jnp.int32),
            pltpu.SemaphoreType.DMA((11,)),
            pltpu.SemaphoreType.DMA((13,)),
            pltpu.SemaphoreType.DMA((n_sem,)),
        ],
        compiler_params=pltpu.CompilerParams(
            collective_id=0, has_side_effects=True, vmem_limit_bytes=60 * 1024 * 1024
        ),
    )(
        tokens.reshape(8, 2, rows_t, width),
        upstream.reshape(8, 2, rows_t, width),
        corpus.reshape(8, 2, rows_c, width),
        lengths,
        owners,
        w_in,
        w_out,
    )


def local(tokens, upstream, corpus, lengths, owners, w_in, w_out):
    width = w_in.shape[0] * lax.axis_size(GROUP_DP)
    hidden_units = w_in.shape[1] * lax.axis_size("tensor")
    scale_in = 1.0 / math.sqrt(width)
    scale_out = 1.0 / math.sqrt(hidden_units)
    return handed_over(
        *fused(tokens, upstream, corpus, lengths, owners, w_in, w_out, scale_in, scale_out)
    )


def solution(mesh):
    torus = Mesh(
        mesh.devices.reshape(mesh.shape["group"], 2, NZ, mesh.shape["tensor"]),
        ("group", "dp_0", "dp_1", "tensor"),
    )
    return jax.shard_map(
        local,
        mesh=torus,
        in_specs=(
            P(DP, None),
            P(DP, None),
            P(DP, None),
            P(DP),
            P(DP),
            P(GROUP_DP, "tensor"),
            P(GROUP_DP, "tensor"),
        ),
        out_specs=(P(GROUP_DP, "tensor"), P(GROUP_DP, "tensor"), P(GROUP_DP, "tensor")),
        check_vma=False,
    )
```

```python
import functools
import math

import jax
import jax.numpy as jnp
from jax import lax
from jax.experimental import pallas as pl
from jax.experimental.pallas import tpu as pltpu
from jax.sharding import Mesh
from jax.sharding import PartitionSpec as P

DP = ("dp_0", "dp_1")
GROUP_DP = ("group", "dp_0", "dp_1")
MESH = pl.DeviceIdType.MESH

LEARN_RATE = 0.5
EPSILON = 1e-06
F32 = jnp.float32
BF16 = jnp.bfloat16
NZ = 8
NT = 8
N_SEM = 107
TURNS = ((1, 1), (1, 0), (0, 1))


def kernel(
    plen,
    scale_in,
    scale_out,
    tokens_ref,
    upstream_ref,
    corpus_ref,
    len_hbm,
    owner_hbm,
    win_ref,
    wout_ref,
    new_in_ref,
    new_out_ref,
    index_ref,
    tok,
    up,
    cor,
    w_in,
    w_out,
    acc_p,
    acc_d,
    acc_c,
    hid,
    dpre,
    g_in,
    g_out,
    r_in,
    r_out,
    fin,
    held,
    index_rows,
    lens_here,
    lens_there,
    pool,
    pool_in,
    square,
    square_in,
    letter,
    letter_in,
    len_ref,
    owner_ref,
    lsem,
    ssem,
    rsem,
):
    g = lax.axis_index("group")
    yh = lax.axis_index("dp_0")
    z = lax.axis_index("dp_1")
    t = lax.axis_index("tensor")
    core = lax.rem(t, 2)
    par = lax.rem(t // 2, 2)
    cut = w_in.shape[-1]
    shard = w_in.shape[-2]

    def cell(dg, dy, dt):
        return (lax.rem(g + dg, 2), lax.rem(yh + dy, 2), z, lax.rem(t + dt, NT))

    def column(dg, dy):
        return cell(dg, dy, 0)

    twin = (g, yh, z, t + 1 - 2 * core)
    right, left = cell(0, 0, 2), cell(0, 0, NT - 2)
    mate, swap = column(1, 1), column(1, 0)
    ring = (
        (g, yh, lax.rem(z + 1, NZ), t),
        (g, yh, lax.rem(z + NZ - 1, NZ), t),
    )
    step_of = (1, -1)

    def at(k):
        return lax.rem(z + k + 2 * NZ, NZ)

    barrier = pltpu.get_barrier_semaphore()
    met = [column(dg, dy) for dg, dy in TURNS] + list(ring) + [twin, right, left]
    met += [cell(0, 0, 4)] + [cell(dg, dy, 4) for dg, dy in TURNS]
    for device in met:
        pl.semaphore_signal(barrier, inc=1, device_id=device, device_id_type=MESH)

    def cols_of(dg, dy):
        q = lax.rem(g + dg, 2) * 2 + lax.rem(yh + dy, 2)
        return pl.ds(pl.multiple_of(q * cut, cut), cut)

    own_cols = cols_of(0, 0)
    groups_of_half = tok.shape[0] // 2
    here = pl.ds(yh * groups_of_half, groups_of_half)
    loads = []

    def load(src, dst):
        copy = pltpu.make_async_copy(src, dst, lsem.at[len(loads)])
        copy.start()
        loads.append(copy)
        return copy

    load_lens = load(len_hbm, len_ref)
    load_owners = load(owner_hbm, owner_ref)
    load_rows = [load(win_ref, held.at[0]), load(wout_ref, held.at[1])]
    load_in = load(win_ref.at[:, own_cols], w_in.at[g, yh, z])
    load_out = load(wout_ref.at[:, own_cols], w_out.at[g, yh, z])
    load_tok = load(tokens_ref, tok.at[here])
    load_up = load(upstream_ref, up.at[here])
    load_cor = load(corpus_ref, cor.at[here])

    passages = len_ref.shape[0]

    def per_passage(ref, shape):
        row = lax.broadcasted_iota(jnp.int32, shape, 0)
        out = jnp.zeros(shape, jnp.int32)
        for i in range(passages):
            out = jnp.where(row == i, ref[i], out)
        return out

    half_nz = NZ // 2
    pair = z // 2
    e = 1 - 2 * lax.rem(z, 2)
    pairs = (
        None,
        pair,
        lax.rem(pair - e + half_nz, half_nz),
        lax.rem(pair + e + half_nz, half_nz),
        lax.rem(pair + 2, half_nz),
    )

    count = [0]

    shared = {}
    families = {}

    def push(src, dst, device, family, key=None):
        k = shared.get(key)
        if k is None:
            k = count[0]
            count[0] += 1
            if key is not None:
                shared[key] = k
        copy = pltpu.make_async_remote_copy(
            src_ref=src,
            dst_ref=dst,
            send_sem=ssem.at[families.setdefault(family, len(families))],
            recv_sem=rsem.at[k],
            device_id=device,
            device_id_type=MESH,
        )
        copy.start()
        return copy

    def same(ref, device, family, key=None):
        return push(ref, ref, device, family, key)

    def whole(ref, family, key):
        return pltpu.make_async_remote_copy(
            src_ref=ref,
            dst_ref=ref,
            send_sem=ssem.at[families[family]],
            recv_sem=rsem.at[shared[key] if key is not None else 0],
            device_id=twin,
            device_id_type=MESH,
        )

    pl.semaphore_wait(barrier, len(met))

    weights = ((held.at[0], w_in), (held.at[1], w_out))
    slices = [[], []]

    def open_ring(a):
        src, w = weights[a]
        for d in range(2):
            push(src.at[:, own_cols], w.at[g, yh, z], ring[d], (0, a), (0, a, d))

    def open_column(a):
        src, w = weights[a]
        for dg, dy in TURNS:
            slices[a].append(
                push(src.at[:, cols_of(dg, dy)], w.at[g, yh, z], column(dg, dy), (0, a))
            )

    def slice_arrives(a, i):
        dg, dy = TURNS[i]
        slices[a][i].wait_recv()
        block = weights[a][1].at[lax.rem(g + dg, 2), lax.rem(yh + dy, 2), z]
        for d in range(2):
            same(block, ring[d], (0, a), (0, a, d))

    ahead = {}

    def ring_arrives(a, s):
        w = weights[a][1]
        for h in range(2):
            for d in range(2):
                if s == 1:
                    if h == 0:
                        whole(w.at[:, :, at(-step_of[d])], (0, a), (0, a, d)).wait_recv()
                elif s < 4 or h == d:
                    ahead[a, s, h, d].wait_recv()
                if s < 3 or (s == 3 and h == d):
                    o = at(-step_of[d] * s)
                    ahead[a, s + 1, h, d] = same(w.at[h, :, o], ring[d], (0, a))

    there = 1 - yh
    arrays = ((tokens_ref, tok), (upstream_ref, up), (corpus_ref, cor))
    from_mate, from_swap, from_side = {}, {}, {}

    fine = 16

    def spot(half, h, i, lane, r):
        start = half * groups_of_half + core * 4 + h * 2 + i
        return pl.ds(start, 1), lane, pl.ds(r * fine, fine)

    def open_part(k, i, r):
        buf = arrays[k][1]
        from_mate[k, i, r] = same(buf.at[spot(yh, 1 - g, i, par, r)], mate, (1, k))

    def pass_on(k, i, r, other):
        block = arrays[k][1].at[spot(there, 1 - g if other else g, i, par, r)]
        from_side[k, i, r, other] = same(block, right if i else left, (1, k))
        same(block, twin, (1, k), (1, k))

    def mate_arrives(k, i, r):
        from_mate[k, i, r].wait_recv()
        from_swap[k, i, r] = same(arrays[k][1].at[spot(there, g, i, par, r)], swap, (1, k))
        pass_on(k, i, r, 0)

    def swap_arrives(k, i, r):
        from_swap[k, i, r].wait_recv()
        pass_on(k, i, r, 1)

    def side_arrives(k, i, r, other):
        from_side[k, i, r, other].wait_recv()
        block = arrays[k][1].at[spot(there, 1 - g if other else g, i, 1 - par, r)]
        same(block, twin, (1, k), (1, k))

    def after_twin(k):
        start = there * groups_of_half + (1 - core) * 4
        whole(arrays[k][1].at[pl.ds(start, 4)], (1, k), (1, k)).wait_recv()

    def rows_of(x, base, tile, p):
        parts = []
        per = x.shape[1] * x.shape[2]
        for q in range(4):
            at_q = pl.multiple_of(q * NZ * shard + p * 2 * shard, 2 * shard)
            block = x[pl.ds(base, tile // per), :, :, pl.ds(at_q, 2 * shard)]
            parts.append(block.reshape(tile, 2 * shard))
        return jnp.concatenate(parts, axis=1)

    def weight(w, p):
        parts = []
        for q in range(4):
            block = w[q // 2, q % 2, pl.ds(2 * p, 2)]
            parts.append(block.reshape(2 * shard, cut))
        return jnp.concatenate(parts, axis=0)

    def multiply(x, w, acc, half, p, is_first):
        per = x.shape[1] * x.shape[2]
        tile = min(512, per * groups_of_half)
        rows_half = per * groups_of_half

        def body(m, carry):
            base = half * groups_of_half + m * (tile // per)
            rows = pl.ds(pl.multiple_of(half * rows_half + m * tile, tile), tile)
            part_sum = jnp.dot(rows_of(x, base, tile, p), weight(w, p), preferred_element_type=F32)
            acc[rows, :] = part_sum if is_first else acc[rows, :] + part_sum
            return carry

        lax.fori_loop(0, rows_half // tile, body, 0)

    root = math.sqrt(2.0 / math.pi)

    def gelu_parts(p):
        th = jnp.tanh(root * (p + 0.044715 * (p * p * p)))
        return 0.5 * (1.0 + th), th

    slab = 64
    n_tok = acc_p.shape[0]

    def activate():
        def body(m, carry):
            rows = pl.ds(pl.multiple_of(m * slab, slab), slab)
            p = acc_p[rows, :] * scale_in
            cdf, th = gelu_parts(p)
            hid[rows, :] = (p * cdf).astype(BF16)
            acc_p[rows, :] = cdf + (0.5 * root) * p * (1.0 - th * th) * (
                1.0 + (3 * 0.044715) * (p * p)
            )
            return carry

        lax.fori_loop(0, n_tok // slab, body, 0)

    def slope_rows():
        def body(m, carry):
            rows = pl.ds(pl.multiple_of(m * slab, slab), slab)
            dpre[rows, :] = (acc_d[rows, :] * scale_out * acc_p[rows, :]).astype(BF16)
            return carry

        lax.fori_loop(0, n_tok // slab, body, 0)

    order = ((0, 0), (1, 0), (0, 1), (1, 1))
    for copy in load_rows:
        copy.wait()
    open_ring(0)
    open_column(0)
    open_ring(1)
    load_tok.wait()
    for i, r in order[:2]:
        open_part(0, i, r)
    open_column(1)
    for i, r in order[2:]:
        open_part(0, i, r)
    load_up.wait()
    for i, r in order:
        open_part(1, i, r)
    load_cor.wait()
    for i in range(2):
        open_part(2, i, 0)
    load_in.wait()
    load_out.wait()
    load_lens.wait()
    load_owners.wait()
    lens_here[...] = per_passage(len_ref, lens_here.shape)
    lens_copy = push(lens_here, lens_there, mate, (2,))
    events = []

    def event(time, what, *args):
        events.append((time, len(events), what, args))

    for a, at_slice, at_ring in (
        (0, (3.4, 3.5, 3.6), (8.0, 13.7, 18.0, 21.5)),
        (1, (7.5, 7.6, 7.7), (14.5, 19.5, 23.0)),
    ):
        for i, time in enumerate(at_slice):
            event(time, slice_arrives, a, i)
        for i, time in enumerate(at_ring):
            event(time, ring_arrives, a, i + 1)
            x, w, acc = ((tok, w_in, acc_p), (up, w_out, acc_d))[a]
            event(time + 0.1, multiply, x, w, acc, yh, pairs[i + 1], i == 0)
            if a == 0 and i < 3:
                event(time + 0.2, multiply, cor, w_in, acc_c, yh, pairs[i + 1], i == 0)
    hop = 3.4
    for k, times in enumerate(((5.8, 7.2, 9.7, 11.1), (12.2, 13.6, 15.0, 16.4))):
        for (i, r), time in zip(order, times):
            event(time, mate_arrives, k, i, r)
            event(time + hop, swap_arrives, k, i, r)
            event(time + hop + 0.1, side_arrives, k, i, r, 0)
            event(time + 2 * hop + 0.6, side_arrives, k, i, r, 1)
    for i, time in enumerate((18.1, 19.5)):
        event(time, mate_arrives, 2, i, 0)
    event(22.0, after_twin, 0)
    for i in range(1, 5):
        event(22.1, multiply, tok, w_in, acc_p, there, pairs[i], i == 1)
    event(23.9, activate)
    for i in range(2):
        event(24.0, swap_arrives, 2, i, 0)
        event(24.0, side_arrives, 2, i, 0, 0)
    for _, _, what, args in sorted(events, key=lambda x: x[:2]):
        what(*args)

    def gradient(x, y, out, scale, p):
        def body(gg, carry):
            parts = []
            for yy in range(2):
                at_q = pl.multiple_of((gg * 2 + yy) * NZ * shard + p * 2 * shard, 2 * shard)
                block = x[:, :, :, pl.ds(at_q, 2 * shard)]
                parts.append(block.reshape(n_tok, 2 * shard))
            both = lax.dot_general(
                jnp.concatenate(parts, axis=1),
                y[...],
                (((0,), (0,)), ((), ())),
                preferred_element_type=F32,
            )
            both = (both * scale).astype(BF16).reshape(2, 2, shard, cut)
            for yy in range(2):
                out[gg, yy, pl.ds(2 * p, 2)] = both[yy]
            return carry

        lax.fori_loop(0, 2, body, 0)

    def add(a, b):
        return (a.astype(F32) + b.astype(F32)).astype(BF16)

    back = {}

    def give_back(a, s):
        grad, arrived = ((g_in, r_in), (g_out, r_out))[a]
        for h in range(2):
            for d in range(2):
                o = at(step_of[d] * (5 - s))
                if s == 1 and h != d:
                    continue
                if s > 2 or (s == 2 and h == d):
                    back[a, s - 1, h, d].wait_recv()
                    for yy in range(2):
                        grad[h, yy, o] = add(grad[h, yy, o], arrived[d, s - 2, h, yy])
                back[a, s, h, d] = push(grad.at[h, :, o], arrived.at[d, s - 1, h], ring[d], (3, a))

    feat = pool.shape[-1]
    rows_c = acc_c.shape[0] // 2
    mine = pl.ds(pl.multiple_of((2 * t + g) * feat, feat), feat)

    def pool_rows():
        after_twin(2)
        lens_copy.wait_recv()
        multiply(cor, w_in, acc_c, yh, pairs[4], False)
        for k in range(1, 5):
            multiply(cor, w_in, acc_c, there, pairs[k], k == 1)
        shape = (passages, rows_c)
        row = lax.broadcasted_iota(jnp.int32, shape, 0)
        col = lax.broadcasted_iota(jnp.int32, shape, 1)
        stack = []
        for half, lens in ((yh, lens_here), (there, lens_there)):
            span = pl.ds(pl.multiple_of(half * rows_c, rows_c), rows_c)
            pre = acc_c[span, :] * scale_in
            cdf, _ = gelu_parts(pre)
            ch = (pre * cdf).astype(BF16)
            stop = row * plen + jnp.broadcast_to(lens[:, :1], shape)
            inside = jnp.logical_and(col >= row * plen, col < stop)
            live = jnp.where(inside, 1.0, 0.0).astype(BF16)
            if not stack:
                x = cor[pl.ds(yh * groups_of_half, groups_of_half), :, :, mine]
                base = jnp.dot(live, x.reshape(rows_c, feat), preferred_element_type=F32)
            ph = jnp.dot(live, ch, preferred_element_type=F32)
            hi = ph.astype(BF16).astype(F32)
            stack += [hi, ph - hi]
        hl = jnp.concatenate(stack, axis=0).astype(BF16)

        def branch(q, carry):
            w = w_out[q // 2, lax.rem(q, 2)].reshape(NZ * shard, cut)
            both = lax.dot_general(hl, w, (((1,), (1,)), ((), ())), preferred_element_type=F32)
            both = both * scale_out
            n = NZ * shard // feat
            for i in range(2):
                rows = both[2 * i * passages : (2 * i + 1) * passages]
                rows = rows + both[(2 * i + 1) * passages : (2 * i + 2) * passages]
                for k in range(n):
                    pool[i, q * n + k] = rows[:, k * feat : (k + 1) * feat]
            return carry

        lax.fori_loop(0, 4, branch, 0)
        for dy in range(2):
            for dg in range(2):
                for dt in range(NT):
                    if dy or dg or dt:
                        to_g, _, _, to_t = cell(dg, dy, dt)
                        src = pool.at[dy, 2 * to_t + to_g]
                        slot = pool_in.at[(dy * 2 + dg) * NT + dt]
                        push(src, slot, cell(dg, dy, dt), (4,), (4,))
        return (base,)

    def square_rows(base):
        total = base + pool[0, 2 * t + g]
        whole(pool_in.at[pl.ds(1, 4 * NT - 1)], (4,), (4,)).wait_recv()
        for k in range(1, 4 * NT):
            total = total + pool_in[k]
        lens = jnp.broadcast_to(lens_here[:, :1], total.shape)
        pooled = total * (1.0 / lens.astype(F32))
        own_square = jnp.sum(pooled * pooled, axis=1, keepdims=True)
        square[...] = jnp.broadcast_to(own_square, square.shape)
        for k in range(1, 2 * NT):
            push(square, square_in.at[k], cell(k // NT, 0, k % NT), (5,), (5,))
        return pooled, own_square

    def post_rows(pooled, own_square):
        whole(square_in.at[pl.ds(1, 2 * NT - 1)], (5,), (5,)).wait_recv()
        total = own_square
        for k in range(1, 2 * NT):
            total = total + square_in[k][:, :1]
        rows = pooled * lax.rsqrt(total / (2 * NT * feat) + EPSILON)
        owners = per_passage(owner_ref, rows.shape)
        here_slot = (g * 2 + yh) * NZ + z
        for k in range(4 * NZ):
            to_g, to_yh = lax.rem(g + k // (2 * NZ), 2), lax.rem(yh + k // NZ, 2)
            to_z = at(k % NZ)
            owner = (to_g * 2 + to_yh) * NZ + to_z
            row = jnp.sum(jnp.where(owners == owner, rows, 0.0), axis=0, keepdims=True)
            if k:
                letter[k] = row
                push(
                    letter.at[k], letter_in.at[here_slot], (to_g, to_yh, to_z, t), (6,), (6,)
                )
            else:
                letter_in[here_slot] = row

    def read_rows():
        whole(letter_in.at[pl.ds(0, 4 * NZ - 1)], (6,), (6,)).wait_recv()
        shape = (2 * NZ, feat)
        row = lax.broadcasted_iota(jnp.int32, shape, 0)
        for gg in range(2):
            out = jnp.zeros(shape, F32)
            for d in range(2 * NZ):
                out = jnp.where(row == d, jnp.broadcast_to(letter_in[gg * 2 * NZ + d], shape), out)
            index_rows[:, gg * feat : (gg + 1) * feat] = out.astype(BF16)
        load(index_rows, index_ref)

    outs = (new_in_ref, new_out_ref)
    sums = ((g_in, r_in, w_in), (g_out, r_out, w_out))

    def settle(a):
        grad, arrived, w = sums[a]
        for h in range(2):
            for d in range(2):
                back[a, 4, h, d].wait_recv()
        for i, (dg, dy) in enumerate(TURNS + ((0, 0),)):
            gg, yy = lax.rem(g + dg, 2), lax.rem(yh + dy, 2)
            total = (
                grad[gg, yy, z].astype(F32)
                + arrived[0, 3, gg, yy].astype(F32)
                + arrived[1, 3, gg, yy].astype(F32)
            )
            fin[a, i] = (w[gg, yy, z].astype(F32) - LEARN_RATE * total).astype(BF16)
            target = outs[a].at[:, own_cols]
            if dg or dy:
                push(fin.at[a, i], target, column(dg, dy), (7, a), (7, a))
            else:
                load(fin.at[a, i], target)

    def grad_out(j):
        gradient(up, hid, g_out, scale_out, pairs[j])

    def grad_in(j):
        gradient(tok, dpre, g_in, scale_in, pairs[j])

    after_twin(1)
    grad_out(4)
    give_back(1, 1)
    ring_arrives(1, 4)
    multiply(up, w_out, acc_d, yh, pairs[4], False)
    for k in range(1, 5):
        multiply(up, w_out, acc_d, there, pairs[k], k == 1)
    slope_rows()
    for i in range(2):
        side_arrives(2, i, 0, 1)
    grad_in(4)
    give_back(0, 1)
    grad_out(3)
    give_back(1, 2)
    stage = pool_rows()
    grad_in(3)
    give_back(0, 2)
    grad_out(2)
    give_back(1, 3)
    grad_in(2)
    give_back(0, 3)
    stage = square_rows(*stage)
    grad_out(1)
    give_back(1, 4)
    grad_in(1)
    give_back(0, 4)
    post_rows(*stage)
    settle(1)
    settle(0)
    read_rows()
    for a in range(2):
        whole(outs[a].at[:, pl.ds(0, 3 * cut)], (7, a), (7, a)).wait_recv()
    for copy in loads[9:]:
        copy.wait()
    covers = [((0, 0), acc_p.at[pl.ds(0, 31 * n_tok // 32)])]
    covers += [((0, 1), acc_d.at[pl.ds(0, 31 * n_tok // 32)])]
    covers += [((1, k), arrays[k][1].at[pl.ds(0, groups_of_half)]) for k in range(3)]
    covers += [((2,), lens_here), ((4,), pool_in.at[pl.ds(1, 4 * NT - 1)])]
    covers += [((3, a), sums[a][0].at[:, :, pl.ds(0, NZ - 1)]) for a in range(2)]
    covers += [((5,), square_in.at[pl.ds(1, 2 * NT - 1)]), ((6,), letter_in.at[pl.ds(0, 4 * NZ - 1)])]
    covers += [((7, a), fin.at[a, pl.ds(0, 3)]) for a in range(2)]
    for family, ref in covers:
        whole(ref, family, None).wait_send()


def pass_through(*refs):
    n = len(refs) // 3
    sources, results, held = refs[:n], refs[n : 2 * n], refs[2 * n : 3 * n]
    sems = refs[3 * n]
    taken = []
    for k in range(n):
        copy = pltpu.make_async_copy(sources[k], held[k], sems.at[k])
        copy.start()
        taken.append(copy)
    given = []
    for k in range(n):
        taken[k].wait()
        copy = pltpu.make_async_copy(held[k], results[k], sems.at[n + k])
        copy.start()
        given.append(copy)
    for copy in given:
        copy.wait()


def handed_over(*arrays):
    any_spec = pl.BlockSpec(memory_space=pl.ANY)
    return pl.pallas_call(
        pass_through,
        out_shape=tuple(jax.ShapeDtypeStruct(x.shape, x.dtype) for x in arrays),
        in_specs=[any_spec] * len(arrays),
        out_specs=(any_spec,) * len(arrays),
        scratch_shapes=[pltpu.VMEM(x.shape, x.dtype) for x in arrays]
        + [pltpu.SemaphoreType.DMA((2 * len(arrays),))],
    )(*arrays)


def fused(tokens, upstream, corpus, lengths, owners, w_in, w_out, scale_in, scale_out):
    shard, local_ff = w_in.shape
    cut = local_ff // 4
    n_tok, width = tokens.shape
    n_corpus = corpus.shape[0]
    npass = lengths.shape[0]
    full = (2, 2, NZ, shard, cut)
    n_sem = N_SEM
    feat = width // (2 * NT)
    rows_t, rows_c = n_tok // 16, n_corpus // 16
    any_spec = pl.BlockSpec(memory_space=pl.ANY)
    return pl.pallas_call(
        functools.partial(kernel, n_corpus // npass, scale_in, scale_out),
        out_shape=(
            jax.ShapeDtypeStruct((shard, local_ff), BF16),
            jax.ShapeDtypeStruct((shard, local_ff), BF16),
            jax.ShapeDtypeStruct((2 * NZ, 2 * feat), BF16),
        ),
        in_specs=[any_spec] * 7,
        out_specs=(any_spec, any_spec, any_spec),
        scratch_shapes=[
            pltpu.VMEM((16, 2, rows_t, width), BF16),
            pltpu.VMEM((16, 2, rows_t, width), BF16),
            pltpu.VMEM((16, 2, rows_c, width), BF16),
            pltpu.VMEM(full, BF16),
            pltpu.VMEM(full, BF16),
            pltpu.VMEM((2 * n_tok, cut), F32),
            pltpu.VMEM((2 * n_tok, cut), F32),
            pltpu.VMEM((2 * n_corpus, cut), F32),
            pltpu.VMEM((2 * n_tok, cut), BF16),
            pltpu.VMEM((2 * n_tok, cut), BF16),
            pltpu.VMEM(full, BF16),
            pltpu.VMEM(full, BF16),
            pltpu.VMEM((2, 4, 2, 2, shard, cut), BF16),
            pltpu.VMEM((2, 4, 2, 2, shard, cut), BF16),
            pltpu.VMEM((2, 4, shard, cut), BF16),
            pltpu.VMEM((2, shard, local_ff), BF16),
            pltpu.VMEM((2 * NZ, 2 * feat), BF16),
            pltpu.VMEM((npass, 128), jnp.int32),
            pltpu.VMEM((npass, 128), jnp.int32),
            pltpu.VMEM((2, 2 * NT, npass, feat), F32),
            pltpu.VMEM((4 * NT, npass, feat), F32),
            pltpu.VMEM((npass, 128), F32),
            pltpu.VMEM((2 * NT, npass, 128), F32),
            pltpu.VMEM((4 * NZ, 1, feat), F32),
            pltpu.VMEM((4 * NZ, 1, feat), F32),
            pltpu.SMEM((npass,), jnp.int32),
            pltpu.SMEM((npass,), jnp.int32),
            pltpu.SemaphoreType.DMA((12,)),
            pltpu.SemaphoreType.DMA((13,)),
            pltpu.SemaphoreType.DMA((n_sem,)),
        ],
        compiler_params=pltpu.CompilerParams(
            collective_id=0, has_side_effects=True, vmem_limit_bytes=60 * 1024 * 1024
        ),
    )(
        tokens.reshape(8, 2, rows_t, width),
        upstream.reshape(8, 2, rows_t, width),
        corpus.reshape(8, 2, rows_c, width),
        lengths,
        owners,
        w_in,
        w_out,
    )


def local(tokens, upstream, corpus, lengths, owners, w_in, w_out):
    width = w_in.shape[0] * lax.axis_size(GROUP_DP)
    hidden_units = w_in.shape[1] * lax.axis_size("tensor")
    scale_in = 1.0 / math.sqrt(width)
    scale_out = 1.0 / math.sqrt(hidden_units)
    return handed_over(
        *fused(tokens, upstream, corpus, lengths, owners, w_in, w_out, scale_in, scale_out)
    )


def solution(mesh):
    torus = Mesh(
        mesh.devices.reshape(mesh.shape["group"], 2, NZ, mesh.shape["tensor"]),
        ("group", "dp_0", "dp_1", "tensor"),
    )
    return jax.shard_map(
        local,
        mesh=torus,
        in_specs=(
            P(DP, None),
            P(DP, None),
            P(DP, None),
            P(DP),
            P(DP),
            P(GROUP_DP, "tensor"),
            P(GROUP_DP, "tensor"),
        ),
        out_specs=(P(GROUP_DP, "tensor"), P(GROUP_DP, "tensor"), P(GROUP_DP, "tensor")),
        check_vma=False,
    )
```

```python
import functools
import math

import jax
import jax.numpy as jnp
from jax import lax
from jax.experimental import pallas as pl
from jax.experimental.pallas import tpu as pltpu
from jax.sharding import Mesh
from jax.sharding import PartitionSpec as P

DP = ("dp_0", "dp_1")
GROUP_DP = ("group", "dp_0", "dp_1")
MESH = pl.DeviceIdType.MESH

LEARN_RATE = 0.5
EPSILON = 1e-06
F32 = jnp.float32
BF16 = jnp.bfloat16
NZ = 8
NT = 8
N_SEM = 107
TURNS = ((1, 1), (1, 0), (0, 1))


def kernel(
    plen,
    scale_in,
    scale_out,
    tokens_ref,
    upstream_ref,
    corpus_ref,
    len_hbm,
    owner_hbm,
    win_ref,
    wout_ref,
    new_in_ref,
    new_out_ref,
    index_ref,
    tok,
    up,
    cor,
    w_in,
    w_out,
    acc_p,
    acc_d,
    acc_c,
    hid,
    dpre,
    g_in,
    g_out,
    r_in,
    r_out,
    fin,
    held,
    index_rows,
    lens_here,
    lens_there,
    pool,
    pool_in,
    square,
    square_in,
    letter,
    letter_in,
    len_ref,
    owner_ref,
    lsem,
    ssem,
    rsem,
):
    g = lax.axis_index("group")
    yh = lax.axis_index("dp_0")
    z = lax.axis_index("dp_1")
    t = lax.axis_index("tensor")
    core = lax.rem(t, 2)
    par = lax.rem(t // 2, 2)
    cut = w_in.shape[-1]
    shard = w_in.shape[-2]

    def cell(dg, dy, dt):
        return (lax.rem(g + dg, 2), lax.rem(yh + dy, 2), z, lax.rem(t + dt, NT))

    def column(dg, dy):
        return cell(dg, dy, 0)

    twin = (g, yh, z, t + 1 - 2 * core)
    right, left = cell(0, 0, 2), cell(0, 0, NT - 2)
    mate, swap = column(1, 1), column(1, 0)
    ring = (
        (g, yh, lax.rem(z + 1, NZ), t),
        (g, yh, lax.rem(z + NZ - 1, NZ), t),
    )
    step_of = (1, -1)

    def at(k):
        return lax.rem(z + k + 2 * NZ, NZ)

    barrier = pltpu.get_barrier_semaphore()
    met = [column(dg, dy) for dg, dy in TURNS] + list(ring) + [twin, right, left]
    met += [cell(0, 0, 4)] + [cell(dg, dy, 4) for dg, dy in TURNS]
    for device in met:
        pl.semaphore_signal(barrier, inc=1, device_id=device, device_id_type=MESH)

    def cols_of(dg, dy):
        q = lax.rem(g + dg, 2) * 2 + lax.rem(yh + dy, 2)
        return pl.ds(pl.multiple_of(q * cut, cut), cut)

    own_cols = cols_of(0, 0)
    groups_of_half = tok.shape[0] // 2
    here = pl.ds(yh * groups_of_half, groups_of_half)
    loads = []

    def load(src, dst):
        copy = pltpu.make_async_copy(src, dst, lsem.at[len(loads)])
        copy.start()
        loads.append(copy)
        return copy

    load_lens = load(len_hbm, len_ref)
    load_owners = load(owner_hbm, owner_ref)
    load_rows = [load(win_ref, held.at[0]), load(wout_ref, held.at[1])]
    load_in = load(win_ref.at[:, own_cols], w_in.at[g, yh, z])
    load_out = load(wout_ref.at[:, own_cols], w_out.at[g, yh, z])
    load_tok = load(tokens_ref, tok.at[here])
    load_up = load(upstream_ref, up.at[here])
    load_cor = load(corpus_ref, cor.at[here])

    passages = len_ref.shape[0]

    def per_passage(ref, shape):
        row = lax.broadcasted_iota(jnp.int32, shape, 0)
        out = jnp.zeros(shape, jnp.int32)
        for i in range(passages):
            out = jnp.where(row == i, ref[i], out)
        return out

    half_nz = NZ // 2
    pair = z // 2
    e = 1 - 2 * lax.rem(z, 2)
    pairs = (
        None,
        pair,
        lax.rem(pair - e + half_nz, half_nz),
        lax.rem(pair + e + half_nz, half_nz),
        lax.rem(pair + 2, half_nz),
    )

    count = [0]

    shared = {}
    families = {}

    def push(src, dst, device, family, key=None):
        k = shared.get(key)
        if k is None:
            k = count[0]
            count[0] += 1
            if key is not None:
                shared[key] = k
        copy = pltpu.make_async_remote_copy(
            src_ref=src,
            dst_ref=dst,
            send_sem=ssem.at[families.setdefault(family, len(families))],
            recv_sem=rsem.at[k],
            device_id=device,
            device_id_type=MESH,
        )
        copy.start()
        return copy

    def same(ref, device, family, key=None):
        return push(ref, ref, device, family, key)

    def whole(ref, family, key):
        return pltpu.make_async_remote_copy(
            src_ref=ref,
            dst_ref=ref,
            send_sem=ssem.at[families[family]],
            recv_sem=rsem.at[shared[key] if key is not None else 0],
            device_id=twin,
            device_id_type=MESH,
        )

    pl.semaphore_wait(barrier, len(met))

    weights = ((held.at[0], w_in), (held.at[1], w_out))
    slices = [[], []]

    def open_ring(a):
        src, w = weights[a]
        for d in range(2):
            push(src.at[:, own_cols], w.at[g, yh, z], ring[d], (0, a), (0, a, d))

    def open_column(a):
        src, w = weights[a]
        for dg, dy in TURNS:
            slices[a].append(
                push(src.at[:, cols_of(dg, dy)], w.at[g, yh, z], column(dg, dy), (0, a))
            )

    def slice_arrives(a, i):
        dg, dy = TURNS[i]
        slices[a][i].wait_recv()
        block = weights[a][1].at[lax.rem(g + dg, 2), lax.rem(yh + dy, 2), z]
        for d in range(2):
            same(block, ring[d], (0, a), (0, a, d))

    ahead = {}

    def ring_arrives(a, s):
        w = weights[a][1]
        for h in range(2):
            for d in range(2):
                if s == 1:
                    if h == 0:
                        whole(w.at[:, :, at(-step_of[d])], (0, a), (0, a, d)).wait_recv()
                elif s < 4 or h == d:
                    ahead[a, s, h, d].wait_recv()
                if s < 3 or (s == 3 and h == d):
                    o = at(-step_of[d] * s)
                    ahead[a, s + 1, h, d] = same(w.at[h, :, o], ring[d], (0, a))

    there = 1 - yh
    arrays = ((tokens_ref, tok), (upstream_ref, up), (corpus_ref, cor))
    from_mate, from_swap, from_side = {}, {}, {}

    fine = 16

    def spot(half, h, i, lane, r):
        start = half * groups_of_half + core * 4 + h * 2 + i
        return pl.ds(start, 1), lane, pl.ds(r * fine, fine)

    def open_part(k, i, r):
        buf = arrays[k][1]
        from_mate[k, i, r] = same(buf.at[spot(yh, 1 - g, i, par, r)], mate, (1, k))

    def pass_on(k, i, r, other):
        block = arrays[k][1].at[spot(there, 1 - g if other else g, i, par, r)]
        from_side[k, i, r, other] = same(block, right if i else left, (1, k))
        same(block, twin, (1, k), (1, k))

    def mate_arrives(k, i, r):
        from_mate[k, i, r].wait_recv()
        from_swap[k, i, r] = same(arrays[k][1].at[spot(there, g, i, par, r)], swap, (1, k))
        pass_on(k, i, r, 0)

    def swap_arrives(k, i, r):
        from_swap[k, i, r].wait_recv()
        pass_on(k, i, r, 1)

    def side_arrives(k, i, r, other):
        from_side[k, i, r, other].wait_recv()
        block = arrays[k][1].at[spot(there, 1 - g if other else g, i, 1 - par, r)]
        same(block, twin, (1, k), (1, k))

    def after_twin(k):
        start = there * groups_of_half + (1 - core) * 4
        whole(arrays[k][1].at[pl.ds(start, 4)], (1, k), (1, k)).wait_recv()

    def rows_of(x, base, tile, p):
        parts = []
        per = x.shape[1] * x.shape[2]
        for q in range(4):
            at_q = pl.multiple_of(q * NZ * shard + p * 2 * shard, 2 * shard)
            block = x[pl.ds(base, tile // per), :, :, pl.ds(at_q, 2 * shard)]
            parts.append(block.reshape(tile, 2 * shard))
        return jnp.concatenate(parts, axis=1)

    def weight(w, p):
        parts = []
        for q in range(4):
            block = w[q // 2, q % 2, pl.ds(2 * p, 2)]
            parts.append(block.reshape(2 * shard, cut))
        return jnp.concatenate(parts, axis=0)

    def multiply(x, w, acc, half, p, is_first):
        per = x.shape[1] * x.shape[2]
        tile = min(512, per * groups_of_half)
        rows_half = per * groups_of_half

        def body(m, carry):
            base = half * groups_of_half + m * (tile // per)
            rows = pl.ds(pl.multiple_of(half * rows_half + m * tile, tile), tile)
            part_sum = jnp.dot(rows_of(x, base, tile, p), weight(w, p), preferred_element_type=F32)
            acc[rows, :] = part_sum if is_first else acc[rows, :] + part_sum
            return carry

        lax.fori_loop(0, rows_half // tile, body, 0)

    root = math.sqrt(2.0 / math.pi)

    def gelu_parts(p):
        th = jnp.tanh(root * (p + 0.044715 * (p * p * p)))
        return 0.5 * (1.0 + th), th

    slab = 64
    n_tok = acc_p.shape[0]

    def activate():
        def body(m, carry):
            rows = pl.ds(pl.multiple_of(m * slab, slab), slab)
            p = acc_p[rows, :] * scale_in
            cdf, th = gelu_parts(p)
            hid[rows, :] = (p * cdf).astype(BF16)
            acc_p[rows, :] = cdf + (0.5 * root) * p * (1.0 - th * th) * (
                1.0 + (3 * 0.044715) * (p * p)
            )
            return carry

        lax.fori_loop(0, n_tok // slab, body, 0)

    def slope_rows():
        def body(m, carry):
            rows = pl.ds(pl.multiple_of(m * slab, slab), slab)
            dpre[rows, :] = (acc_d[rows, :] * scale_out * acc_p[rows, :]).astype(BF16)
            return carry

        lax.fori_loop(0, n_tok // slab, body, 0)

    order = ((0, 0), (1, 0), (0, 1), (1, 1))
    for copy in load_rows:
        copy.wait()
    open_ring(0)
    open_column(0)
    open_ring(1)
    load_tok.wait()
    for i, r in order[:2]:
        open_part(0, i, r)
    open_column(1)
    for i, r in order[2:]:
        open_part(0, i, r)
    load_up.wait()
    for i, r in order:
        open_part(1, i, r)
    load_cor.wait()
    for i in range(2):
        open_part(2, i, 0)
    load_in.wait()
    load_out.wait()
    load_lens.wait()
    load_owners.wait()
    lens_here[...] = per_passage(len_ref, lens_here.shape)
    lens_copy = push(lens_here, lens_there, mate, (2,))
    events = []

    def event(time, what, *args):
        events.append((time, len(events), what, args))

    for a, at_slice, at_ring in (
        (0, (3.4, 3.5, 3.6), (8.0, 13.7, 18.0, 21.5)),
        (1, (7.5, 7.6, 7.7), (14.5, 19.5, 23.0)),
    ):
        for i, time in enumerate(at_slice):
            event(time, slice_arrives, a, i)
        for i, time in enumerate(at_ring):
            event(time, ring_arrives, a, i + 1)
            x, w, acc = ((tok, w_in, acc_p), (up, w_out, acc_d))[a]
            event(time + 0.1, multiply, x, w, acc, yh, pairs[i + 1], i == 0)
            if a == 0 and i < 3:
                event(time + 0.2, multiply, cor, w_in, acc_c, yh, pairs[i + 1], i == 0)
    hop = 3.4
    for k, times in enumerate(((5.8, 7.2, 9.7, 11.1), (12.2, 13.6, 15.0, 16.4))):
        for (i, r), time in zip(order, times):
            event(time, mate_arrives, k, i, r)
            event(time + hop, swap_arrives, k, i, r)
            event(time + hop + 0.1, side_arrives, k, i, r, 0)
            event(time + 2 * hop + 0.6, side_arrives, k, i, r, 1)
    for i, time in enumerate((18.1, 19.5)):
        event(time, mate_arrives, 2, i, 0)
    event(22.0, after_twin, 0)
    for i in range(1, 5):
        event(22.1, multiply, tok, w_in, acc_p, there, pairs[i], i == 1)
    event(23.9, activate)
    for i in range(2):
        event(22.2, swap_arrives, 2, i, 0)
        event(22.2, side_arrives, 2, i, 0, 0)
    for _, _, what, args in sorted(events, key=lambda x: x[:2]):
        what(*args)

    def gradient(x, y, out, scale, p):
        def body(gg, carry):
            parts = []
            for yy in range(2):
                at_q = pl.multiple_of((gg * 2 + yy) * NZ * shard + p * 2 * shard, 2 * shard)
                block = x[:, :, :, pl.ds(at_q, 2 * shard)]
                parts.append(block.reshape(n_tok, 2 * shard))
            both = lax.dot_general(
                jnp.concatenate(parts, axis=1),
                y[...],
                (((0,), (0,)), ((), ())),
                preferred_element_type=F32,
            )
            both = (both * scale).astype(BF16).reshape(2, 2, shard, cut)
            for yy in range(2):
                out[gg, yy, pl.ds(2 * p, 2)] = both[yy]
            return carry

        lax.fori_loop(0, 2, body, 0)

    def add(a, b):
        return (a.astype(F32) + b.astype(F32)).astype(BF16)

    back = {}

    def give_back(a, s):
        grad, arrived = ((g_in, r_in), (g_out, r_out))[a]
        for h in range(2):
            for d in range(2):
                o = at(step_of[d] * (5 - s))
                if s == 1 and h != d:
                    continue
                if s > 2 or (s == 2 and h == d):
                    back[a, s - 1, h, d].wait_recv()
                    for yy in range(2):
                        grad[h, yy, o] = add(grad[h, yy, o], arrived[d, s - 2, h, yy])
                back[a, s, h, d] = push(grad.at[h, :, o], arrived.at[d, s - 1, h], ring[d], (3, a))

    feat = pool.shape[-1]
    rows_c = acc_c.shape[0] // 2
    mine = pl.ds(pl.multiple_of((2 * t + g) * feat, feat), feat)

    def pool_rows():
        after_twin(2)
        lens_copy.wait_recv()
        multiply(cor, w_in, acc_c, yh, pairs[4], False)
        for k in range(1, 5):
            multiply(cor, w_in, acc_c, there, pairs[k], k == 1)
        shape = (passages, rows_c)
        row = lax.broadcasted_iota(jnp.int32, shape, 0)
        col = lax.broadcasted_iota(jnp.int32, shape, 1)
        stack = []
        for half, lens in ((yh, lens_here), (there, lens_there)):
            span = pl.ds(pl.multiple_of(half * rows_c, rows_c), rows_c)
            pre = acc_c[span, :] * scale_in
            cdf, _ = gelu_parts(pre)
            ch = (pre * cdf).astype(BF16)
            stop = row * plen + jnp.broadcast_to(lens[:, :1], shape)
            inside = jnp.logical_and(col >= row * plen, col < stop)
            live = jnp.where(inside, 1.0, 0.0).astype(BF16)
            if not stack:
                x = cor[pl.ds(yh * groups_of_half, groups_of_half), :, :, mine]
                base = jnp.dot(live, x.reshape(rows_c, feat), preferred_element_type=F32)
            ph = jnp.dot(live, ch, preferred_element_type=F32)
            hi = ph.astype(BF16).astype(F32)
            stack += [hi, ph - hi]
        hl = jnp.concatenate(stack, axis=0).astype(BF16)

        def branch(q, carry):
            w = w_out[q // 2, lax.rem(q, 2)].reshape(NZ * shard, cut)
            both = lax.dot_general(hl, w, (((1,), (1,)), ((), ())), preferred_element_type=F32)
            both = both * scale_out
            n = NZ * shard // feat
            for i in range(2):
                rows = both[2 * i * passages : (2 * i + 1) * passages]
                rows = rows + both[(2 * i + 1) * passages : (2 * i + 2) * passages]
                for k in range(n):
                    pool[i, q * n + k] = rows[:, k * feat : (k + 1) * feat]
            return carry

        lax.fori_loop(0, 4, branch, 0)
        for dy in range(2):
            for dg in range(2):
                for dt in range(NT):
                    if dy or dg or dt:
                        to_g, _, _, to_t = cell(dg, dy, dt)
                        src = pool.at[dy, 2 * to_t + to_g]
                        slot = pool_in.at[(dy * 2 + dg) * NT + dt]
                        push(src, slot, cell(dg, dy, dt), (4,), (4,))
        return (base,)

    def square_rows(base):
        total = base + pool[0, 2 * t + g]
        whole(pool_in.at[pl.ds(1, 4 * NT - 1)], (4,), (4,)).wait_recv()
        for k in range(1, 4 * NT):
            total = total + pool_in[k]
        lens = jnp.broadcast_to(lens_here[:, :1], total.shape)
        pooled = total * (1.0 / lens.astype(F32))
        own_square = jnp.sum(pooled * pooled, axis=1, keepdims=True)
        square[...] = jnp.broadcast_to(own_square, square.shape)
        for k in range(1, 2 * NT):
            push(square, square_in.at[k], cell(k // NT, 0, k % NT), (5,), (5,))
        return pooled, own_square

    def post_rows(pooled, own_square):
        whole(square_in.at[pl.ds(1, 2 * NT - 1)], (5,), (5,)).wait_recv()
        total = own_square
        for k in range(1, 2 * NT):
            total = total + square_in[k][:, :1]
        rows = pooled * lax.rsqrt(total / (2 * NT * feat) + EPSILON)
        owners = per_passage(owner_ref, rows.shape)
        here_slot = (g * 2 + yh) * NZ + z
        for k in range(4 * NZ):
            to_g, to_yh = lax.rem(g + k // (2 * NZ), 2), lax.rem(yh + k // NZ, 2)
            to_z = at(k % NZ)
            owner = (to_g * 2 + to_yh) * NZ + to_z
            row = jnp.sum(jnp.where(owners == owner, rows, 0.0), axis=0, keepdims=True)
            if k:
                letter[k] = row
                push(
                    letter.at[k], letter_in.at[here_slot], (to_g, to_yh, to_z, t), (6,), (6,)
                )
            else:
                letter_in[here_slot] = row

    def read_rows():
        whole(letter_in.at[pl.ds(0, 4 * NZ - 1)], (6,), (6,)).wait_recv()
        shape = (2 * NZ, feat)
        row = lax.broadcasted_iota(jnp.int32, shape, 0)
        for gg in range(2):
            out = jnp.zeros(shape, F32)
            for d in range(2 * NZ):
                out = jnp.where(row == d, jnp.broadcast_to(letter_in[gg * 2 * NZ + d], shape), out)
            index_rows[:, gg * feat : (gg + 1) * feat] = out.astype(BF16)
        load(index_rows, index_ref)

    outs = (new_in_ref, new_out_ref)
    sums = ((g_in, r_in, w_in), (g_out, r_out, w_out))

    def settle(a):
        grad, arrived, w = sums[a]
        for h in range(2):
            for d in range(2):
                back[a, 4, h, d].wait_recv()
        for i, (dg, dy) in enumerate(TURNS + ((0, 0),)):
            gg, yy = lax.rem(g + dg, 2), lax.rem(yh + dy, 2)
            total = (
                grad[gg, yy, z].astype(F32)
                + arrived[0, 3, gg, yy].astype(F32)
                + arrived[1, 3, gg, yy].astype(F32)
            )
            fin[a, i] = (w[gg, yy, z].astype(F32) - LEARN_RATE * total).astype(BF16)
            target = outs[a].at[:, own_cols]
            if dg or dy:
                push(fin.at[a, i], target, column(dg, dy), (7, a), (7, a))
            else:
                load(fin.at[a, i], target)

    def grad_out(j):
        gradient(up, hid, g_out, scale_out, pairs[j])

    def grad_in(j):
        gradient(tok, dpre, g_in, scale_in, pairs[j])

    after_twin(1)
    grad_out(4)
    give_back(1, 1)
    ring_arrives(1, 4)
    multiply(up, w_out, acc_d, yh, pairs[4], False)
    for k in range(1, 5):
        multiply(up, w_out, acc_d, there, pairs[k], k == 1)
    slope_rows()
    for i in range(2):
        side_arrives(2, i, 0, 1)
    grad_in(4)
    give_back(0, 1)
    grad_out(3)
    give_back(1, 2)
    stage = pool_rows()
    grad_in(3)
    give_back(0, 2)
    grad_out(2)
    give_back(1, 3)
    grad_in(2)
    give_back(0, 3)
    stage = square_rows(*stage)
    grad_out(1)
    give_back(1, 4)
    grad_in(1)
    give_back(0, 4)
    post_rows(*stage)
    settle(1)
    settle(0)
    read_rows()
    for a in range(2):
        whole(outs[a].at[:, pl.ds(0, 3 * cut)], (7, a), (7, a)).wait_recv()
    for copy in loads[9:]:
        copy.wait()
    covers = [((0, 0), acc_p.at[pl.ds(0, 31 * n_tok // 32)])]
    covers += [((0, 1), acc_d.at[pl.ds(0, 31 * n_tok // 32)])]
    covers += [((1, k), arrays[k][1].at[pl.ds(0, groups_of_half)]) for k in range(3)]
    covers += [((2,), lens_here), ((4,), pool_in.at[pl.ds(1, 4 * NT - 1)])]
    covers += [((3, a), sums[a][0].at[:, :, pl.ds(0, NZ - 1)]) for a in range(2)]
    covers += [((5,), square_in.at[pl.ds(1, 2 * NT - 1)]), ((6,), letter_in.at[pl.ds(0, 4 * NZ - 1)])]
    covers += [((7, a), fin.at[a, pl.ds(0, 3)]) for a in range(2)]
    for family, ref in covers:
        whole(ref, family, None).wait_send()


def pass_through(*refs):
    n = len(refs) // 3
    sources, results, held = refs[:n], refs[n : 2 * n], refs[2 * n : 3 * n]
    sems = refs[3 * n]
    taken = []
    for k in range(n):
        copy = pltpu.make_async_copy(sources[k], held[k], sems.at[k])
        copy.start()
        taken.append(copy)
    given = []
    for k in range(n):
        taken[k].wait()
        copy = pltpu.make_async_copy(held[k], results[k], sems.at[n + k])
        copy.start()
        given.append(copy)
    for copy in given:
        copy.wait()


def handed_over(*arrays):
    any_spec = pl.BlockSpec(memory_space=pl.ANY)
    return pl.pallas_call(
        pass_through,
        out_shape=tuple(jax.ShapeDtypeStruct(x.shape, x.dtype) for x in arrays),
        in_specs=[any_spec] * len(arrays),
        out_specs=(any_spec,) * len(arrays),
        scratch_shapes=[pltpu.VMEM(x.shape, x.dtype) for x in arrays]
        + [pltpu.SemaphoreType.DMA((2 * len(arrays),))],
    )(*arrays)


def fused(tokens, upstream, corpus, lengths, owners, w_in, w_out, scale_in, scale_out):
    shard, local_ff = w_in.shape
    cut = local_ff // 4
    n_tok, width = tokens.shape
    n_corpus = corpus.shape[0]
    npass = lengths.shape[0]
    full = (2, 2, NZ, shard, cut)
    n_sem = N_SEM
    feat = width // (2 * NT)
    rows_t, rows_c = n_tok // 16, n_corpus // 16
    any_spec = pl.BlockSpec(memory_space=pl.ANY)
    return pl.pallas_call(
        functools.partial(kernel, n_corpus // npass, scale_in, scale_out),
        out_shape=(
            jax.ShapeDtypeStruct((shard, local_ff), BF16),
            jax.ShapeDtypeStruct((shard, local_ff), BF16),
            jax.ShapeDtypeStruct((2 * NZ, 2 * feat), BF16),
        ),
        in_specs=[any_spec] * 7,
        out_specs=(any_spec, any_spec, any_spec),
        scratch_shapes=[
            pltpu.VMEM((16, 2, rows_t, width), BF16),
            pltpu.VMEM((16, 2, rows_t, width), BF16),
            pltpu.VMEM((16, 2, rows_c, width), BF16),
            pltpu.VMEM(full, BF16),
            pltpu.VMEM(full, BF16),
            pltpu.VMEM((2 * n_tok, cut), F32),
            pltpu.VMEM((2 * n_tok, cut), F32),
            pltpu.VMEM((2 * n_corpus, cut), F32),
            pltpu.VMEM((2 * n_tok, cut), BF16),
            pltpu.VMEM((2 * n_tok, cut), BF16),
            pltpu.VMEM(full, BF16),
            pltpu.VMEM(full, BF16),
            pltpu.VMEM((2, 4, 2, 2, shard, cut), BF16),
            pltpu.VMEM((2, 4, 2, 2, shard, cut), BF16),
            pltpu.VMEM((2, 4, shard, cut), BF16),
            pltpu.VMEM((2, shard, local_ff), BF16),
            pltpu.VMEM((2 * NZ, 2 * feat), BF16),
            pltpu.VMEM((npass, 128), jnp.int32),
            pltpu.VMEM((npass, 128), jnp.int32),
            pltpu.VMEM((2, 2 * NT, npass, feat), F32),
            pltpu.VMEM((4 * NT, npass, feat), F32),
            pltpu.VMEM((npass, 128), F32),
            pltpu.VMEM((2 * NT, npass, 128), F32),
            pltpu.VMEM((4 * NZ, 1, feat), F32),
            pltpu.VMEM((4 * NZ, 1, feat), F32),
            pltpu.SMEM((npass,), jnp.int32),
            pltpu.SMEM((npass,), jnp.int32),
            pltpu.SemaphoreType.DMA((12,)),
            pltpu.SemaphoreType.DMA((13,)),
            pltpu.SemaphoreType.DMA((n_sem,)),
        ],
        compiler_params=pltpu.CompilerParams(
            collective_id=0, has_side_effects=True, vmem_limit_bytes=60 * 1024 * 1024
        ),
    )(
        tokens.reshape(8, 2, rows_t, width),
        upstream.reshape(8, 2, rows_t, width),
        corpus.reshape(8, 2, rows_c, width),
        lengths,
        owners,
        w_in,
        w_out,
    )


def local(tokens, upstream, corpus, lengths, owners, w_in, w_out):
    width = w_in.shape[0] * lax.axis_size(GROUP_DP)
    hidden_units = w_in.shape[1] * lax.axis_size("tensor")
    scale_in = 1.0 / math.sqrt(width)
    scale_out = 1.0 / math.sqrt(hidden_units)
    return handed_over(
        *fused(tokens, upstream, corpus, lengths, owners, w_in, w_out, scale_in, scale_out)
    )


def solution(mesh):
    torus = Mesh(
        mesh.devices.reshape(mesh.shape["group"], 2, NZ, mesh.shape["tensor"]),
        ("group", "dp_0", "dp_1", "tensor"),
    )
    return jax.shard_map(
        local,
        mesh=torus,
        in_specs=(
            P(DP, None),
            P(DP, None),
            P(DP, None),
            P(DP),
            P(DP),
            P(GROUP_DP, "tensor"),
            P(GROUP_DP, "tensor"),
        ),
        out_specs=(P(GROUP_DP, "tensor"), P(GROUP_DP, "tensor"), P(GROUP_DP, "tensor")),
        check_vma=False,
    )
```
